32 devices in a mesh: section: 4 (over y, x), dp: 8 (over z, core).
Axes of the slice: x: 2, y: 2, z: 4, core: 2. Of those that a mesh axis runs over, the one named last changes fastest.
Arguments:
- fields: bfloat16 [24, 1024, 276], P('dp'), may hold values from -6 to 6
- targets: bfloat16 [24, 1024, 276], P('dp'), may hold values from -6 to 6
- level_count: int32 [24], P('dp'), may hold values from 5 to 13, as said below
- step_count: int32 [1], replicated, may hold values from 2 to 20
- dense: float32 [2029, 384], P(None, 'dp')
- dense_m: float32 [2029, 384], P(None, 'dp'), may hold values from -2.9802322e-07 to 2.9802322e-07
- dense_v: float32 [2029, 384], P(None, 'dp'), may hold values from 1.1573045e-14 to 9.258436e-14
- dense_ema: float32 [2029, 384], P(None, 'dp')
- vectors: float32 [6, 384], P(None, 'dp')
- vectors_m: float32 [6, 384], P(None, 'dp'), may hold values from -3.33786e-06 to 3.33786e-06
- vectors_v: float32 [6, 384], P(None, 'dp'), may hold values from 1.1573045e-12 to 9.258436e-12
- vectors_ema: float32 [6, 384], P(None, 'dp')
- w_qkv: float32 [2, 384, 1152], P(None, 'dp'), may hold values from -0.3125 to 0.3125
- w_out: float32 [2, 384, 384], P(None, 'dp'), may hold values from -5 to 5
- w_fc1: float32 [2, 384, 1536], P(None, 'dp'), may hold values from -0.3125 to 0.3125
- w_fc2: float32 [2, 1536, 384], P(None, 'dp'), may hold values from -0.15625 to 0.15625
- ema_qkv: float32 [2, 384, 1152], P(None, 'dp'), may hold values from -0.3125 to 0.3125
- ema_out: float32 [2, 384, 384], P(None, 'dp'), may hold values from -5 to 5
- ema_fc1: float32 [2, 384, 1536], P(None, 'dp'), may hold values from -0.3125 to 0.3125
- ema_fc2: float32 [2, 1536, 384], P(None, 'dp'), may hold values from -0.15625 to 0.15625
- stat_small: float32 [2, 5, 384, 384], P(None, None, 'dp')
- stat_qkv: float32 [2, 1152, 1152], P(None, 'dp')
- stat_wide: float32 [2, 2, 1536, 1536], P(None, None, 'dp')
- root_small: float32 [2, 5, 384, 384], P(None, None, 'dp'), as said below
- root_qkv: float32 [2, 1152, 1152], P(None, 'dp'), as said below
- root_wide: float32 [2, 2, 1536, 1536], P(None, None, 'dp'), as said below
Outputs:
- loss: float32 [], replicated
- grad_norm: float32 [], replicated
- dense_new: float32 [2029, 384], P(None, 'dp')
- dense_m_new: float32 [2029, 384], P(None, 'dp')
- dense_v_new: float32 [2029, 384], P(None, 'dp')
- dense_ema_new: float32 [2029, 384], P(None, 'dp')
- vectors_new: float32 [6, 384], P(None, 'dp')
- vectors_m_new: float32 [6, 384], P(None, 'dp')
- vectors_v_new: float32 [6, 384], P(None, 'dp')
- vectors_ema_new: float32 [6, 384], P(None, 'dp')
- qkv_new: float32 [2, 384, 1152], P(None, 'dp')
- out_new: float32 [2, 384, 384], P(None, 'dp')
- fc1_new: float32 [2, 384, 1536], P(None, 'dp')
- fc2_new: float32 [2, 1536, 384], P(None, 'dp')
- ema_qkv_new: float32 [2, 384, 1152], P(None, 'dp')
- ema_out_new: float32 [2, 384, 384], P(None, 'dp')
- ema_fc1_new: float32 [2, 384, 1536], P(None, 'dp')
- ema_fc2_new: float32 [2, 1536, 384], P(None, 'dp')
- stat_small_new: float32 [2, 5, 384, 384], P(None, None, 'dp')
- stat_qkv_new: float32 [2, 1152, 1152], P(None, 'dp')
- stat_wide_new: float32 [2, 2, 1536, 1536], P(None, None, 'dp')
The draws below stay inside these ranges and needn't reach their ends.
Inputs may be any that keep to these rules, and one draw needn't show every extreme that they name: An item's pressure levels that count are the first level_count of the 13 levels of every atmospheric variable. `root_small`: each matrix of inverse roots is symmetric. `root_qkv`: each matrix of inverse roots is symmetric. `root_wide`: each matrix of inverse roots is symmetric.
All inputs are finite; a program needn't handle non-finite values.
Results may differ from the reference program's by a relative error of at most 0.00055.
The reference program's roundings to bfloat16 on the way count: a program that leaves them out, or rounds other values in their place, can miss the bound.
Values may be sent and summed in bfloat16 or wider, within the bound.
A program may use at most 384 MiB of HBM per device.

```python
import math
import jax
import jax.numpy as jnp
from jax import lax

D = 384
HEADS = 6
HDIM = 64
FF = 1536
SURF = 4
LEVELS = 13
VARS = 69
PIX = 4
VP = 276
MIN_LEVELS = 5
LAT_ROWS = 64
LON_COLS = 16
SEQ = 1024
LAYERS = 2
ITEMS = 24
NPARAM = 4320384


def draw_level_count(key, part):
    own_key = jax.random.fold_in(key, 11)
    positions = jnp.arange(ITEMS)
    base_count = MIN_LEVELS + (LEVELS - MIN_LEVELS + 1) * positions // ITEMS
    jitter = jax.random.randint(own_key, (ITEMS,), -1, 2)
    level_counts = jnp.clip(base_count + jitter, MIN_LEVELS, LEVELS)
    level_counts = jnp.where(positions == 0, MIN_LEVELS, level_counts)
    level_counts = jnp.where(positions == ITEMS - 1, LEVELS, level_counts)
    return level_counts.astype(jnp.int32)


def dense_law(key):
    table_rows = VARS * (PIX + 1)
    row_count = table_rows + SEQ + D + VP
    noise = jnp.clip(jax.random.normal(key, (row_count, D), jnp.float32), -4.0, 4.0)
    row_index = jnp.arange(row_count)[:, None]
    row_scale = jnp.where(row_index < table_rows, 0.45, jnp.where(row_index < table_rows + SEQ, 0.5, jnp.where(row_index < table_rows + SEQ + D, 2.0 / D ** 0.5, 1.0 / D ** 0.5)))
    return noise * row_scale


def draw_dense(key, part):
    return dense_law(jax.random.fold_in(key, 21))


def draw_dense_ema(key, part):
    return dense_law(jax.random.fold_in(key, 22))


def vector_law(key):
    first, second = jax.random.split(key)
    query_row = jnp.clip(jax.random.normal(first, (1, D), jnp.float32), -4.0, 4.0)
    gain_rows = jax.random.uniform(second, (2 * LAYERS + 1, D), jnp.float32, 0.5, 1.5)
    return jnp.concatenate([query_row, gain_rows], axis=0)


def draw_vectors(key, part):
    return vector_law(jax.random.fold_in(key, 31))


def draw_vectors_ema(key, part):
    return vector_law(jax.random.fold_in(key, 32))


def grad_entry():
    return 0.001 / NPARAM ** 0.5


def symmetric_law(key, leading, size, diagonal):
    first, second = jax.random.split(key)
    noise = jax.random.normal(first, leading + (size, size), jnp.float32)
    symmetric = (noise + jnp.swapaxes(noise, -1, -2)) * (0.3 / size ** 0.5)
    scales = jax.random.uniform(second, leading + (size,), jnp.float32, 1.0, 2.0)
    identity = jnp.eye(size, dtype=jnp.float32)
    return diagonal * (symmetric + identity * scales[..., None])


def stat_scale():
    return 0.05 / 0.95 * D * grad_entry() ** 2


def root_scale():
    return (D * grad_entry() ** 2) ** (-0.25)


def draw_stat_small(key, part):
    return symmetric_law(jax.random.fold_in(key, 41), (LAYERS, 5), D, stat_scale())


def draw_stat_qkv(key, part):
    return symmetric_law(jax.random.fold_in(key, 42), (LAYERS,), 3 * D, stat_scale())


def draw_stat_wide(key, part):
    return symmetric_law(jax.random.fold_in(key, 43), (LAYERS, 2), FF, stat_scale())


def draw_root_small(key, part):
    return symmetric_law(jax.random.fold_in(key, 51), (LAYERS, 5), D, root_scale())


def draw_root_qkv(key, part):
    return symmetric_law(jax.random.fold_in(key, 52), (LAYERS,), 3 * D, root_scale())


def draw_root_wide(key, part):
    return symmetric_law(jax.random.fold_in(key, 53), (LAYERS, 2), FF, root_scale())


def block_levels(rng, extent, shards, smallest, top_value):
    gain = 1.0
    for axis_at, blocks in shards:
        draws = jax.random.uniform(jax.random.fold_in(jax.random.fold_in(rng, 6), axis_at), (blocks,), jnp.float32, smallest / len(shards), top_value / len(shards))
        gain = gain * jnp.repeat(jnp.exp(draws), extent[axis_at] // blocks).reshape((-1,) + (1,) * (len(extent) - 1 - axis_at))
    return gain


def centred(key, shape, scale, bound, cuts=(), kind=jnp.bfloat16):
    gain = block_levels(key, shape, cuts, -0.22, 0.18) if cuts else 1.0
    drawn = jax.random.normal(key, shape, jnp.float32) * scale * gain
    return jnp.minimum(jnp.maximum(drawn, -bound), bound).astype(kind)


def setup_inputs(seed: int = 0) -> dict:
    key_list = jax.random.split(jax.random.key(seed), 27)
    return {
        "fields": centred(key_list[0], (ITEMS, SEQ, VP), 1.0, 6.0, ((0, 8),)),
        "targets": centred(key_list[1], (ITEMS, SEQ, VP), 1.0, 6.0, ((0, 8),)),
        "level_count": draw_level_count(jax.random.fold_in(key_list[26], 71), 0),
        "step_count": jax.random.randint(key_list[3], (1,), 2, 21).astype(jnp.int32),
        "dense": draw_dense(jax.random.fold_in(key_list[26], 71), 0),
        "dense_m": centred(key_list[5], (VARS * (PIX + 1) + SEQ + D + VP, D), (0.11 * 0.001 / NPARAM ** 0.5), 2.980232238769531e-07, ((1, 8),), jnp.float32),
        "dense_v": jnp.clip(jnp.exp(math.log(9.258436031722717e-14) - 2.0794415 * jax.random.uniform(key_list[6], (VARS * (PIX + 1) + SEQ + D + VP, D), jnp.float32) ** block_levels(key_list[6], (VARS * (PIX + 1) + SEQ + D + VP, D), ((1, 8),), -0.2, 0.2)), 1.1573045039653396e-14, 9.258436031722717e-14),
        "dense_ema": draw_dense_ema(jax.random.fold_in(key_list[26], 71), 0),
        "vectors": draw_vectors(jax.random.fold_in(key_list[26], 71), 0),
        "vectors_m": centred(key_list[9], (2 * LAYERS + 2, D), (1.1 * 0.001 / NPARAM ** 0.5), 3.337860107421875e-06, ((1, 8),), jnp.float32),
        "vectors_v": jnp.clip(jnp.exp(math.log(9.258436031722717e-12) - 2.0794415 * jax.random.uniform(key_list[10], (2 * LAYERS + 2, D), jnp.float32) ** block_levels(key_list[10], (2 * LAYERS + 2, D), ((1, 8),), -0.2, 0.2)), 1.1573045039653396e-12, 9.258436031722717e-12),
        "vectors_ema": draw_vectors_ema(jax.random.fold_in(key_list[26], 71), 0),
        "w_qkv": centred(key_list[12], (LAYERS, D, 3 * D), D ** -0.5, 0.3125, ((1, 8),), jnp.float32),
        "w_out": centred(key_list[13], (LAYERS, D, D), (D * 4 / SEQ) ** -0.5, 5.0, ((1, 8),), jnp.float32),
        "w_fc1": centred(key_list[14], (LAYERS, D, FF), D ** -0.5, 0.3125, ((1, 8),), jnp.float32),
        "w_fc2": centred(key_list[15], (LAYERS, FF, D), FF ** -0.5, 0.15625, ((1, 8),), jnp.float32),
        "ema_qkv": centred(key_list[16], (LAYERS, D, 3 * D), D ** -0.5, 0.3125, ((1, 8),), jnp.float32),
        "ema_out": centred(key_list[17], (LAYERS, D, D), (D * 4 / SEQ) ** -0.5, 5.0, ((1, 8),), jnp.float32),
        "ema_fc1": centred(key_list[18], (LAYERS, D, FF), D ** -0.5, 0.3125, ((1, 8),), jnp.float32),
        "ema_fc2": centred(key_list[19], (LAYERS, FF, D), FF ** -0.5, 0.15625, ((1, 8),), jnp.float32),
        "stat_small": draw_stat_small(jax.random.fold_in(key_list[26], 71), 0),
        "stat_qkv": draw_stat_qkv(jax.random.fold_in(key_list[26], 71), 0),
        "stat_wide": draw_stat_wide(jax.random.fold_in(key_list[26], 71), 0),
        "root_small": draw_root_small(jax.random.fold_in(key_list[26], 71), 0),
        "root_qkv": draw_root_qkv(jax.random.fold_in(key_list[26], 71), 0),
        "root_wide": draw_root_wide(jax.random.fold_in(key_list[26], 71), 0),
    }


highest = lax.Precision.HIGHEST
norm_eps = 1e-05
clip_level = 0.001
rate_dense = 0.05
rate_vector = 0.2
rate_matrix = 0.5
beta_first = 0.9
beta_second = 0.95
adam_eps = 1e-08
weight_decay = 0.1
stat_beta = 0.95
ema_beta = 0.9

@jax.custom_vjp
def low(v):
    return lax.optimization_barrier(v.astype(jnp.bfloat16)).astype(jnp.float32)

@jax.custom_vjp
def low_back(v):
    return v

def low_keep(v):
    return (low(v), None)

def low_pass(kept, grad):
    return (grad,)

def back_keep(v):
    return (v, None)

def back_low(kept, grad):
    return (low(grad),)
low.defvjp(low_keep, low_pass)
low_back.defvjp(back_keep, back_low)

def send_value(values):
    return low(low_back(values))

def matmul(left_side, right_side):
    return jnp.dot(left_side, right_side, precision=highest)

def layer_norm(values, gain_row):
    center = values - lax.optimization_barrier(jnp.mean(values, -1, keepdims=True))
    spread = lax.optimization_barrier(jnp.mean(center * center, -1, keepdims=True))
    return center * lax.rsqrt(spread + norm_eps) * gain_row

def valid_flags(counts):
    var_index = jnp.arange(VARS)
    level_index = (var_index - SURF) % LEVELS
    inside = (var_index[None, :] < SURF) | (level_index[None, :] < counts[:, None])
    return jnp.where(inside, 1.0, 0.0).astype(jnp.float32)

def loss_weights(flags):
    pixel_rows = 2 * LAT_ROWS
    latitude = (jnp.arange(pixel_rows).astype(jnp.float32) + 0.5) * (jnp.pi / pixel_rows) - 0.5 * jnp.pi
    cosine = jnp.cos(latitude)
    cosine = cosine / jnp.mean(cosine)
    row_index = 2 * (jnp.arange(SEQ) // LON_COLS)[:, None] + (jnp.arange(PIX) // 2)[None, :]
    by_pixel = lax.optimization_barrier(jnp.sum(jnp.where(row_index[:, :, None] == jnp.arange(pixel_rows)[None, None, :], cosine, 0.0), axis=-1))
    return (flags[:, None, :, None] * by_pixel[None, :, None, :]).reshape(flags.shape[0], SEQ, VP)

def aggregate(field_rows, flag_row, var_table, query_row):
    length = field_rows.shape[0]
    extended = jnp.concatenate([field_rows.reshape(length, VARS, PIX), jnp.ones((length, VARS, 1), jnp.float32)], axis=2)
    head_scale = HDIM ** (-0.5)
    query_table = (var_table * query_row).reshape(VARS, PIX + 1, HEADS, HDIM).sum(-1) * head_scale
    scores = jnp.einsum('svp,vph->shv', extended, query_table, precision=highest)
    scores = jnp.where(flag_row > 0, scores, -1000000000.0)
    weights = jax.nn.softmax(scores, axis=-1)
    mixing = (weights[..., None] * extended[:, None]).reshape(length, HEADS, VARS * (PIX + 1))
    merged = jnp.einsum('shk,khd->shd', mixing, var_table.reshape(VARS * (PIX + 1), HEADS, HDIM), precision=highest)
    return merged.reshape(length, D)

def block_output(values, gain_pair, w_qkv, w_out, w_fc1, w_fc2):
    length = values.shape[0]
    hidden = low(layer_norm(values, gain_pair[0]))
    qkv = low(low_back(matmul(hidden, w_qkv)))
    heads_view = qkv.reshape(length, 3, HEADS, HDIM)
    scores = low_back(jnp.einsum('qhd,khd->hqk', heads_view[:, 0], heads_view[:, 1], precision=highest) * HDIM ** (-0.5))
    probability = low(jax.nn.softmax(scores, axis=-1))
    mixed_out = jnp.einsum('hqk,khd->qhd', probability, heads_view[:, 2], precision=highest).reshape(length, D)
    mixed_out = low(low_back(mixed_out))
    middle = values + low_back(matmul(mixed_out, w_out))
    hidden_two = low(layer_norm(middle, gain_pair[1]))
    before = low_back(matmul(hidden_two, w_fc1))
    active = low(jax.nn.gelu(before, approximate=False))
    return middle + low_back(matmul(active, w_fc2))

def head_error(values, gain_row, head_rows, target, weight):
    hidden = low(layer_norm(values, gain_row))
    predicted = low_back(jnp.dot(hidden, head_rows.T, precision=highest))
    residual_error = predicted - target
    return jnp.sum(weight * residual_error * residual_error)

def total_error(params, field_all, target_all, flags, weights):
    dense, vectors, w_qkv, w_out, w_fc1, w_fc2 = [low(param) for param in params]
    table_rows = VARS * (PIX + 1)
    var_table = dense[:table_rows].reshape(VARS, PIX + 1, D)
    position = dense[table_rows:table_rows + SEQ]
    agg_weight = dense[table_rows + SEQ:table_rows + SEQ + D]
    head_rows = dense[table_rows + SEQ + D:]

    def item_fn(carried, item_data):
        field_rows, target, flag_row, weight = item_data
        merged = low(aggregate(field_rows, flag_row, var_table, vectors[0]))
        values = send_value(matmul(merged, agg_weight) + position)
        for layer_index in range(LAYERS):
            values = send_value(block_output(values, vectors[1 + 2 * layer_index:3 + 2 * layer_index], w_qkv[layer_index], w_out[layer_index], w_fc1[layer_index], w_fc2[layer_index]))
        return (carried + head_error(values, vectors[2 * LAYERS + 1], head_rows, target, weight), None)
    result, unused = lax.scan(jax.checkpoint(item_fn), jnp.zeros((), jnp.float32), (field_all, target_all, flags, weights))
    return result

def adam_update(weight, moment_one, moment_two, gradient, learn_rate, decay_rate, steps_done):
    first = beta_first * moment_one + (1.0 - beta_first) * gradient
    second = beta_second * moment_two + (1.0 - beta_second) * gradient * gradient
    first_hat = first / (1.0 - jnp.power(beta_first, steps_done))
    second_hat = second / (1.0 - jnp.power(beta_second, steps_done))
    updated = weight - learn_rate * (first_hat / (jnp.sqrt(second_hat) + adam_eps) + decay_rate * weight)
    return (updated, first, second)

def shampoo(gradient, left_state, right_state, left_root, right_root, weight):
    left_new = stat_beta * left_state + (1.0 - stat_beta) * jnp.einsum('kin,kjn->kij', gradient, gradient, precision=highest)
    right_new = stat_beta * right_state + (1.0 - stat_beta) * jnp.einsum('kmi,kmj->kij', gradient, gradient, precision=highest)
    right_side = jnp.einsum('kmn,knj->kmj', gradient, right_root, precision=highest)
    step_size = jnp.einsum('kim,kmn->kin', left_root, right_side, precision=highest)
    return (weight - rate_matrix * step_size, left_new, right_new)

def average(old_state, new_state):
    return ema_beta * old_state + (1.0 - ema_beta) * new_state

def reference(fields, targets, level_count, step_count, dense, dense_m, dense_v, dense_ema, vectors, vectors_m, vectors_v, vectors_ema, w_qkv, w_out, w_fc1, w_fc2, ema_qkv, ema_out, ema_fc1, ema_fc2, stat_small, stat_qkv, stat_wide, root_small, root_qkv, root_wide):
    flags = valid_flags(level_count)
    weights = loss_weights(flags)
    field_all = fields.astype(jnp.float32)
    target_all = targets.astype(jnp.float32)

    def objective(*params):
        return total_error(params, field_all, target_all, flags, weights)
    error_total, pull_back = jax.vjp(objective, dense, vectors, w_qkv, w_out, w_fc1, w_fc2)
    raw = pull_back(jnp.ones((), jnp.float32))
    weight_total = jnp.sum(weights)
    squares = sum((jnp.sum(gradient * gradient) for gradient in raw))
    grad_norm = jnp.sqrt(squares) / weight_total
    factor = jnp.minimum(1.0, clip_level / grad_norm) / weight_total
    clipped = [gradient * factor for gradient in raw]
    steps_done = step_count[0].astype(jnp.float32)
    dense_new, dense_m_new, dense_v_new = adam_update(dense, dense_m, dense_v, clipped[0], rate_dense, weight_decay, steps_done)
    vectors_new, vectors_m_new, vectors_v_new = adam_update(vectors, vectors_m, vectors_v, clipped[1], rate_vector, 0.0, steps_done)
    lefts = [stat_small[:, 0], stat_small[:, 1], stat_small[:, 3], stat_wide[:, 1]]
    rights = [stat_qkv, stat_small[:, 2], stat_wide[:, 0], stat_small[:, 4]]
    left_roots = [root_small[:, 0], root_small[:, 1], root_small[:, 3], root_wide[:, 1]]
    right_roots = [root_qkv, root_small[:, 2], root_wide[:, 0], root_small[:, 4]]
    matrices = [w_qkv, w_out, w_fc1, w_fc2]
    new_weights, new_lefts, new_rights = ([], [], [])
    for matrix_index in range(4):
        updated, left_new, right_new = shampoo(clipped[2 + matrix_index], lefts[matrix_index], rights[matrix_index], left_roots[matrix_index], right_roots[matrix_index], matrices[matrix_index])
        new_weights.append(updated)
        new_lefts.append(left_new)
        new_rights.append(right_new)
    stat_small_new = jnp.stack([new_lefts[0], new_lefts[1], new_rights[1], new_lefts[2], new_rights[3]], axis=1)
    stat_wide_new = jnp.stack([new_rights[2], new_lefts[3]], axis=1)
    return (error_total / weight_total, grad_norm, dense_new, dense_m_new, dense_v_new, average(dense_ema, dense_new), vectors_new, vectors_m_new, vectors_v_new, average(vectors_ema, vectors_new), new_weights[0], new_weights[1], new_weights[2], new_weights[3], average(ema_qkv, new_weights[0]), average(ema_out, new_weights[1]), average(ema_fc1, new_weights[2]), average(ema_fc2, new_weights[3]), stat_small_new, new_rights[0], stat_wide_new)
```

```python
import functools
import math

import jax
import jax.numpy as jnp
import numpy as np
from jax import lax
from jax.experimental import pallas as pl
from jax.experimental.pallas import tpu as pltpu
from jax.sharding import PartitionSpec as P

D = 384
HEADS = 6
HDIM = 64
SURF = 4
LEVELS = 13
VARS = 69
PIX = 4
VP = 276
LAT_ROWS = 64
LON_COLS = 16
SEQ = 1024
LAYERS = 2
FF = 1536

LANES = 128
PAIRS = HEADS // 2
EXT = (PIX + 1) * LANES
TABLE = VARS * (PIX + 1)

highest = lax.Precision.HIGHEST
f32 = jnp.float32
bf16 = jnp.bfloat16
norm_eps = 1e-05
clip_level = 0.001
rate_dense = 0.05
rate_vector = 0.2
rate_matrix = 0.5
beta_first = 0.9
beta_second = 0.95
adam_eps = 1e-08
weight_decay = 0.1
stat_beta = 0.95
ema_beta = 0.9
LOG2E = math.log2(math.e)
SCALE2 = LOG2E * HDIM ** (-0.5)

NN = (((1,), (0,)), ((), ()))
NT = (((1,), (1,)), ((), ()))
TN = (((0,), (0,)), ((), ()))


def dot(left, right, dims=NN):
    return lax.dot_general(left, right, dims, preferred_element_type=f32)


def halves(value):
    high = value.astype(bf16)
    return high, (value - high.astype(f32)).astype(bf16)


def call(body, out_shape, scratch=(), vmem=60 << 20, flops=0, traffic=0):
    return pl.pallas_call(
        body,
        out_shape=out_shape,
        scratch_shapes=list(scratch),
        compiler_params=pltpu.CompilerParams(vmem_limit_bytes=vmem),
        cost_estimate=pl.CostEstimate(flops=flops, bytes_accessed=traffic, transcendentals=0),
    )


def shape(dims, kind=f32):
    return jax.ShapeDtypeStruct(dims, kind)


def norm_parts(values):
    center = values - jnp.mean(values, -1, keepdims=True)
    spread = jnp.mean(center * center, -1, keepdims=True)
    inverse = lax.rsqrt(spread + norm_eps)
    return center * inverse, inverse


def norm_back(values, gain, upstream):
    unit, inverse = norm_parts(values)
    scaled = upstream * gain
    back = inverse * (
        scaled
        - jnp.mean(scaled, -1, keepdims=True)
        - unit * jnp.mean(scaled * unit, -1, keepdims=True)
    )
    return back, jnp.sum(upstream * unit, 0, keepdims=True)


def tiles(count, body):
    def step(index, carry):
        body(index)
        return carry

    lax.fori_loop(0, count, step, 0)


def rows_of(index, size):
    return pl.ds(pl.multiple_of(index * size, size), size)


def head_mask(rows, which):
    lane = lax.broadcasted_iota(jnp.int32, (rows, LANES), 1)
    return (lane >= which * HDIM) & (lane < (which + 1) * HDIM)


def spread_fields(field_rows):
    row = lax.broadcasted_iota(jnp.int32, (VP, PIX * LANES), 0)
    col = lax.broadcasted_iota(jnp.int32, (VP, PIX * LANES), 1)
    var, pixel = col % LANES, col // LANES
    chosen = (row == PIX * var + pixel) & (var < VARS)
    return dot(field_rows, jnp.where(chosen, 1.0, 0.0).astype(bf16))


def query_mask(query_row):
    head = lax.broadcasted_iota(jnp.int32, (8, D), 0)
    lane = lax.broadcasted_iota(jnp.int32, (8, D), 1)
    return jnp.where(lane // HDIM == head, query_row * HDIM ** (-0.5), 0.0)


def query_scores(table_ref, mask, query_scr):
    for j in range(PIX + 1):
        part = table_ref[j * LANES : (j + 1) * LANES, :]
        query_scr[j * 8 : (j + 1) * 8, :] = dot(mask.astype(bf16), part, NT)


def mix_weights(extended, query_scr, head, valid):
    score = query_scr[pl.ds(PIX * 8 + head, 1), :]
    for j in range(PIX):
        score = score + extended[j] * query_scr[pl.ds(j * 8 + head, 1), :]
    score = jnp.where(valid > 0, score, jnp.where(valid < 0, -jnp.inf, -1e9))
    peak = jnp.max(score, -1, keepdims=True)
    weight = jnp.exp(score - peak)
    return weight / jnp.sum(weight, -1, keepdims=True)


def embed_body(field_ref, table_ref, query_ref, valid_ref, proj_ref, pos_ref, out_ref, agg_ref, query_scr):
    size = 256
    query_scores(table_ref, query_mask(query_ref[...]), query_scr)

    def tile(index):
        rows = rows_of(index, size)
        wide = spread_fields(field_ref[rows, :])
        extended = [wide[:, j * LANES : (j + 1) * LANES] for j in range(PIX)]
        valid = valid_ref[...]

        def pair(hp, carry):
            lanes = rows_of(hp, LANES)
            table = table_ref[:, lanes]
            total = jnp.zeros((size, LANES), f32)
            for which in range(2):
                weight = mix_weights(extended, query_scr, 2 * hp + which, valid)
                mixing = jnp.concatenate([weight * extended[j] for j in range(PIX)] + [weight], 1)
                own = jnp.where(head_mask(EXT, which), table, jnp.zeros_like(table))
                high, low = halves(mixing)
                total = total + dot(high, own) + dot(low, own)
            agg_ref[rows, lanes] = total.astype(bf16)
            return carry

        lax.fori_loop(0, PAIRS, pair, 0)
        out_ref[rows, :] = (dot(agg_ref[rows, :], proj_ref[...]) + pos_ref[rows, :].astype(f32)).astype(bf16)

    tiles(SEQ // size, tile)


def embed_forward(field_rows, table, query_row, valid, proj, position):
    return call(
        embed_body,
        (shape((SEQ, D), bf16), shape((SEQ, D), bf16)),
        [pltpu.VMEM((40, LANES), f32)],
        flops=4_000_000_000,
        traffic=4_000_000,
    )(field_rows, table, query_row, valid, proj, position)


def embed_back_body(
    field_ref, table_ref, query_ref, valid_ref, proj_ref, agg_ref, grad_ref,
    dtable_ref, dquery_ref, dproj_ref, query_scr, wide_scr, merged_scr, high_scr, low_scr, dscore_scr,
):
    size = 256
    mask = query_mask(query_ref[...])
    query_scores(table_ref, mask, query_scr)
    dproj_ref[...] = dot(agg_ref[...], grad_ref[...], TN)
    dscore_scr[...] = jnp.zeros_like(dscore_scr)

    def prepare(index):
        rows = rows_of(index, size)
        wide_scr[rows, :] = spread_fields(field_ref[rows, :])
        merged_scr[rows, :] = dot(grad_ref[rows, :], proj_ref[...], NT)

    tiles(SEQ // size, prepare)

    def pair(hp):
        lanes = rows_of(hp, LANES)
        table = table_ref[:, lanes]
        total = jnp.zeros((EXT, LANES), f32)
        for which in range(2):
            head = 2 * hp + which
            own = jnp.where(head_mask(EXT, which), table, jnp.zeros_like(table))
            twice = jnp.concatenate([own, own], 1)

            def tile(index):
                rows = rows_of(index, size)
                extended = [wide_scr[rows, j * LANES : (j + 1) * LANES] for j in range(PIX)]
                weight = mix_weights(extended, query_scr, head, valid_ref[...])
                mixing = jnp.concatenate([weight * extended[j] for j in range(PIX)] + [weight], 1)
                high, low = halves(mixing)
                high_scr[rows, :] = high
                low_scr[rows, :] = low
                grad_high, grad_low = halves(merged_scr[rows, lanes])
                dmix = dot(jnp.concatenate([grad_high, grad_low], 1), twice, NT)
                dweight = dmix[:, PIX * LANES :]
                for j in range(PIX):
                    dweight = dweight + dmix[:, j * LANES : (j + 1) * LANES] * extended[j]
                dscore = weight * (dweight - jnp.sum(weight * dweight, -1, keepdims=True))
                for j in range(PIX + 1):
                    piece = dscore * extended[j] if j < PIX else dscore
                    at = pl.ds(j * 8 + head, 1)
                    dscore_scr[at, :] = dscore_scr[at, :] + jnp.sum(piece, 0, keepdims=True)

            tiles(SEQ // size, tile)
            grad_high, grad_low = halves(merged_scr[:, lanes])
            keep = head_mask(SEQ, which)
            grad_high = jnp.where(keep, grad_high, jnp.zeros_like(grad_high))
            grad_low = jnp.where(keep, grad_low, jnp.zeros_like(grad_low))
            both = dot(high_scr[...], jnp.concatenate([grad_high, grad_low], 1), TN)
            total = total + both[:, :LANES] + both[:, LANES:] + dot(low_scr[...], grad_high, TN)
        dtable_ref[:, lanes] = total

    tiles(PAIRS, pair)
    dquery = jnp.zeros((1, D), f32)
    head = lax.broadcasted_iota(jnp.int32, (8, D), 0)
    lane = lax.broadcasted_iota(jnp.int32, (8, D), 1)
    for j in range(PIX + 1):
        part = dscore_scr[j * 8 : (j + 1) * 8, :]
        block = slice(j * LANES, (j + 1) * LANES)
        dtable_ref[block, :] = dtable_ref[block, :] + lax.dot_general(
            part, mask, TN, precision=highest, preferred_element_type=f32
        )
        spread = lax.dot_general(
            part, table_ref[block, :].astype(f32), NN, precision=highest, preferred_element_type=f32
        )
        dquery = dquery + jnp.sum(jnp.where(lane // HDIM == head, spread, 0.0), 0, keepdims=True)
    dquery_ref[...] = dquery * HDIM ** (-0.5)


def embed_back(field_rows, table, query_row, valid, proj, agg, grad):
    return call(
        embed_back_body,
        (shape((EXT, D)), shape((1, D)), shape((D, D))),
        [
            pltpu.VMEM((40, LANES), f32),
            pltpu.VMEM((SEQ, PIX * LANES), f32),
            pltpu.VMEM((SEQ, D), f32),
            pltpu.VMEM((SEQ, EXT), bf16),
            pltpu.VMEM((SEQ, EXT), bf16),
            pltpu.VMEM((40, LANES), f32),
        ],
        flops=12_000_000_000,
        traffic=6_000_000,
    )(field_rows, table, query_row, valid, proj, agg, grad)


def block_body(x_ref, gain_ref, wqkv_ref, wout_ref, wfc1_ref, wfc2_ref,
               h_ref, qkv_ref, o_ref, lse_ref, m_ref, h2_ref, y_ref):
    size = 256

    def enter(index):
        rows = rows_of(index, size)
        unit, unused = norm_parts(x_ref[rows, :].astype(f32))
        hidden = (unit * gain_ref[0:1, :]).astype(bf16)
        h_ref[rows, :] = hidden
        qkv_ref[rows, :] = dot(hidden, wqkv_ref[...]).astype(bf16)

    tiles(SEQ // size, enter)
    lse_ref[...] = jnp.zeros_like(lse_ref)

    def pair(hp):
        keys = qkv_ref[:, pl.ds(pl.multiple_of(D + hp * LANES, LANES), LANES)]
        values = qkv_ref[:, pl.ds(pl.multiple_of(2 * D + hp * LANES, LANES), LANES)]

        def tile(index):
            rows = rows_of(index, size)
            queries = qkv_ref[rows, rows_of(hp, LANES)]
            parts = []
            for which in range(2):
                own = jnp.where(head_mask(size, which), queries, jnp.zeros_like(queries))
                score = dot(keys, own, NT) * SCALE2
                peak = jnp.max(score, 0, keepdims=True)
                power = jnp.exp2(score - peak)
                total = jnp.sum(power, 0, keepdims=True)
                chance = (power * (1.0 / total)).astype(bf16)
                mixed = dot(values, chance, TN)
                parts.append(mixed[which * HDIM : (which + 1) * HDIM, :])
                lse_ref[pl.ds(2 * hp + which, 1), rows] = peak + jnp.log2(total)
            o_ref[rows, rows_of(hp, LANES)] = jnp.concatenate(parts, 0).T.astype(bf16)

        tiles(SEQ // size, tile)

    tiles(PAIRS, pair)

    def leave(index):
        rows = rows_of(index, size)
        middle = x_ref[rows, :].astype(f32) + dot(o_ref[rows, :], wout_ref[...])
        m_ref[rows, :] = middle
        unit, unused = norm_parts(middle)
        hidden = (unit * gain_ref[1:2, :]).astype(bf16)
        h2_ref[rows, :] = hidden
        before = dot(hidden, wfc1_ref[...])
        active = (0.5 * before * (1.0 + lax.erf(before * math.sqrt(0.5)))).astype(bf16)
        y_ref[rows, :] = (middle + dot(active, wfc2_ref[...])).astype(bf16)

    tiles(SEQ // size, leave)


def block_forward(x, gains, wqkv, wout, wfc1, wfc2):
    return call(
        block_body,
        (
            shape((SEQ, D), bf16),
            shape((SEQ, 3 * D), bf16),
            shape((SEQ, D), bf16),
            shape((8, SEQ)),
            shape((SEQ, D)),
            shape((SEQ, D), bf16),
            shape((SEQ, D), bf16),
        ),
        flops=12_000_000_000,
        traffic=12_000_000,
    )(x, gains, wqkv, wout, wfc1, wfc2)


def block_back_body(x_ref, h_ref, qkv_ref, o_ref, lse_ref, m_ref, h2_ref, dy_ref, gain_ref,
                    wqkv_ref, wout_ref, wfc1_ref, wfc2_ref,
                    dx_ref, dgain_ref, dwqkv_ref, dwout_ref, dwfc1_ref, dwfc2_ref,
                    r_scr, df_scr, dm_scr, db_scr, do_scr, dqkv_scr, dkv_scr):
    size = 256
    dgain_ref[...] = jnp.zeros_like(dgain_ref)

    def first(index):
        rows = rows_of(index, size)
        before = dot(h2_ref[rows, :], wfc1_ref[...])
        upper = 0.5 * (1.0 + lax.erf(before * math.sqrt(0.5)))
        r_scr[rows, :] = (before * upper).astype(bf16)
        slope = upper + before * (jnp.exp2(before * before * (-0.5 * LOG2E)) * (1.0 / math.sqrt(2 * math.pi)))
        grad_next = dy_ref[rows, :]
        grad_before = (dot(grad_next, wfc2_ref[...], NT) * slope).astype(bf16)
        df_scr[rows, :] = grad_before
        back, dgain = norm_back(m_ref[rows, :], gain_ref[1:2, :], dot(grad_before, wfc1_ref[...], NT))
        dgain_ref[1:2, :] = dgain_ref[1:2, :] + dgain
        middle = grad_next.astype(f32) + back
        dm_scr[rows, :] = middle
        branch = middle.astype(bf16)
        db_scr[rows, :] = branch
        do_scr[rows, :] = dot(branch, wout_ref[...], NT).astype(bf16)

    tiles(SEQ // size, first)

    def wide(index):
        cols = rows_of(index, D)
        dwfc2_ref[cols, :] = dot(r_scr[:, cols], dy_ref[...], TN)
        dwfc1_ref[:, cols] = dot(h2_ref[...], df_scr[:, cols], TN)

    tiles(FF // D, wide)
    dwout_ref[...] = dot(o_ref[...], db_scr[...], TN)

    def pair(hp):
        lanes = rows_of(hp, LANES)
        klanes = pl.ds(pl.multiple_of(D + hp * LANES, LANES), LANES)
        vlanes = pl.ds(pl.multiple_of(2 * D + hp * LANES, LANES), LANES)
        keys = qkv_ref[:, klanes]
        values = qkv_ref[:, vlanes]
        dkv_scr[...] = jnp.zeros_like(dkv_scr)

        def tile(index):
            rows = rows_of(index, size)
            queries = qkv_ref[rows, lanes]
            upstream = do_scr[rows, lanes]
            parts = []
            for which in range(2):
                keep = head_mask(size, which)
                own = jnp.where(keep, queries, jnp.zeros_like(queries))
                own_up = jnp.where(keep, upstream, jnp.zeros_like(upstream))
                score = dot(keys, own, NT) * SCALE2
                chance = jnp.exp2(score - lse_ref[pl.ds(2 * hp + which, 1), rows])
                dchance = dot(values, own_up, NT)
                shift = jnp.sum(dchance * chance, 0, keepdims=True)
                dscore = (chance * (dchance - shift)).astype(bf16)
                dkv_scr[:, :LANES] = dkv_scr[:, :LANES] + dot(dscore, own)
                dkv_scr[:, LANES:] = dkv_scr[:, LANES:] + dot(chance.astype(bf16), own_up)
                dquery = dot(keys, dscore, TN)
                parts.append(dquery[which * HDIM : (which + 1) * HDIM, :])
            dqkv_scr[rows, lanes] = (jnp.concatenate(parts, 0).T * HDIM ** (-0.5)).astype(bf16)

        tiles(SEQ // size, tile)
        dqkv_scr[:, klanes] = (dkv_scr[:, :LANES] * HDIM ** (-0.5)).astype(bf16)
        dqkv_scr[:, vlanes] = dkv_scr[:, LANES:].astype(bf16)

    tiles(PAIRS, pair)

    def third(index):
        cols = rows_of(index, D)
        dwqkv_ref[:, cols] = dot(h_ref[...], dqkv_scr[:, cols], TN)

    tiles(3, third)

    def last(index):
        rows = rows_of(index, size)
        back, dgain = norm_back(
            x_ref[rows, :].astype(f32), gain_ref[0:1, :], dot(dqkv_scr[rows, :], wqkv_ref[...], NT)
        )
        dgain_ref[0:1, :] = dgain_ref[0:1, :] + dgain
        dx_ref[rows, :] = (dm_scr[rows, :] + back).astype(bf16)

    tiles(SEQ // size, last)


def block_back(x, kept, dy, gains, wqkv, wout, wfc1, wfc2):
    return call(
        block_back_body,
        (
            shape((SEQ, D), bf16),
            shape((2, D)),
            shape((D, 3 * D)),
            shape((D, D)),
            shape((D, FF)),
            shape((FF, D)),
        ),
        [
            pltpu.VMEM((SEQ, FF), bf16),
            pltpu.VMEM((SEQ, FF), bf16),
            pltpu.VMEM((SEQ, D), f32),
            pltpu.VMEM((SEQ, D), bf16),
            pltpu.VMEM((SEQ, D), bf16),
            pltpu.VMEM((SEQ, 3 * D), bf16),
            pltpu.VMEM((SEQ, 2 * LANES), f32),
        ],
        flops=30_000_000_000,
        traffic=20_000_000,
    )(x, *kept, dy, gains, wqkv, wout, wfc1, wfc2)


def head_body(y_ref, gain_ref, head_ref, target_ref, cos_ref, valid_ref,
              dy_ref, dhead_ref, dgain_ref, error_ref, h_scr, dp_scr):
    size = 256
    dgain_ref[...] = jnp.zeros_like(dgain_ref)
    error_ref[...] = jnp.zeros_like(error_ref)

    def tile(index):
        rows = rows_of(index, size)
        values = y_ref[rows, :].astype(f32)
        unit, unused = norm_parts(values)
        hidden = (unit * gain_ref[...]).astype(bf16)
        h_scr[rows, :] = hidden
        residual = dot(hidden, head_ref[...], NT) - target_ref[rows, :].astype(f32)
        lane = lax.broadcasted_iota(jnp.int32, (size, VP), 1)
        cosine = jnp.where(lane % PIX < 2, cos_ref[rows, 0:1], cos_ref[rows, 1:2])
        weight = cosine * valid_ref[...]
        error_ref[...] = error_ref[...] + jnp.sum(weight * residual * residual, 0, keepdims=True)
        grad = (2.0 * weight * residual).astype(bf16)
        dp_scr[rows, :] = grad
        back, dgain = norm_back(values, gain_ref[...], dot(grad, head_ref[...]))
        dgain_ref[...] = dgain_ref[...] + dgain
        dy_ref[rows, :] = back.astype(bf16)

    tiles(SEQ // size, tile)
    dhead_ref[...] = dot(dp_scr[...], h_scr[...], TN)


def head_step(y, gain, head_rows, target, cosines, valid):
    return call(
        head_body,
        (shape((SEQ, D), bf16), shape((VP, D)), shape((1, D)), shape((1, VP))),
        [pltpu.VMEM((SEQ, D), bf16), pltpu.VMEM((SEQ, VP), bf16)],
        flops=700_000_000,
        traffic=4_000_000,
    )(y, gain, head_rows, target, cosines, valid)


def valid_flags(counts):
    var_index = jnp.arange(VARS)
    level_index = (var_index - SURF) % LEVELS
    inside = (var_index[None, :] < SURF) | (level_index[None, :] < counts[:, None])
    return jnp.where(inside, 1.0, 0.0).astype(f32)


def cosine_table():
    pixel_rows = 2 * LAT_ROWS
    latitude = (np.arange(pixel_rows) + 0.5) * (np.pi / pixel_rows) - 0.5 * np.pi
    cosine = np.cos(latitude)
    cosine = cosine / np.mean(cosine)
    by_row = cosine.reshape(LAT_ROWS, 2).repeat(LON_COLS, 0)
    return by_row.astype(np.float32), float(by_row.sum() * (PIX // 2))


def adam_update(weight, moment_one, moment_two, gradient, learn_rate, decay_rate, steps_done):
    first = beta_first * moment_one + (1.0 - beta_first) * gradient
    second = beta_second * moment_two + (1.0 - beta_second) * gradient * gradient
    first_hat = first / (1.0 - jnp.power(beta_first, steps_done))
    second_hat = second / (1.0 - jnp.power(beta_second, steps_done))
    updated = weight - learn_rate * (
        first_hat / (jnp.sqrt(second_hat) + adam_eps) + decay_rate * weight
    )
    return (updated, first, second)


def average(old_state, new_state):
    return ema_beta * old_state + (1.0 - ema_beta) * new_state


def per_device(
    fields, targets, level_count, step_count,
    dense, dense_m, dense_v, dense_ema, vectors, vectors_m, vectors_v, vectors_ema,
    w_qkv, w_out, w_fc1, w_fc2, ema_qkv, ema_out, ema_fc1, ema_fc2,
    stat_small, stat_qkv, stat_wide, root_small, root_qkv, root_wide,
):
    def gather(part, axis=1):
        return lax.all_gather(part.astype(bf16), "dp", axis=axis, tiled=True)

    full_dense = gather(dense)
    gain_rows = gather(vectors).astype(f32)
    layer_weights = [
        [gather(part[layer], 0) for part in (w_qkv, w_out, w_fc1, w_fc2)] for layer in range(LAYERS)
    ]
    micro_count = fields.shape[0]
    section = lax.axis_index("section")
    sections = lax.axis_size("section")
    table = full_dense[:TABLE].reshape(VARS, PIX + 1, D).transpose(1, 0, 2)
    table = jnp.pad(table, ((0, 0), (0, LANES - VARS), (0, 0))).reshape(EXT, D)
    position = full_dense[TABLE : TABLE + SEQ]
    proj = full_dense[TABLE + SEQ : TABLE + SEQ + D]
    head_rows = full_dense[TABLE + SEQ + D :]
    flags = valid_flags(level_count)
    by_row, row_total = cosine_table()
    weight_local = jnp.sum(flags) * row_total
    cosines = jnp.asarray(by_row)

    gradients = None
    for turn in range(-(-micro_count // sections)):
        index = turn * sections + section
        active = jnp.where(index < micro_count, 1.0, 0.0).astype(f32)
        index = jnp.minimum(index, micro_count - 1)
        field_rows = lax.dynamic_index_in_dim(fields, index, 0, False)
        target = lax.dynamic_index_in_dim(targets, index, 0, False)
        flag_row = lax.dynamic_index_in_dim(flags, index, 0, True)
        valid_vars = jnp.pad(flag_row, ((0, 0), (0, LANES - VARS)), constant_values=-1.0)
        valid_values = jnp.repeat(flag_row * active, PIX, axis=1)
        x, agg = embed_forward(field_rows, table, gain_rows[0:1], valid_vars, proj, position)
        kept = []
        for layer in range(LAYERS):
            gains = gain_rows[1 + 2 * layer : 3 + 2 * layer]
            *saved, y = block_forward(x, gains, *layer_weights[layer])
            kept.append((x, saved))
            x = y
        grad, d_head, d_final, errors = head_step(
            x, gain_rows[2 * LAYERS + 1 :], head_rows, target, cosines, valid_values
        )
        d_gains, d_mats = [None] * LAYERS, [None] * LAYERS
        for layer in reversed(range(LAYERS)):
            gains = gain_rows[1 + 2 * layer : 3 + 2 * layer]
            x, saved = kept[layer]
            grad, d_gains[layer], *mats = block_back(x, saved, grad, gains, *layer_weights[layer])
            d_mats[layer] = mats
        d_table, d_query, d_proj = embed_back(
            field_rows, table, gain_rows[0:1], valid_vars, proj, agg, grad
        )
        found = (
            jnp.concatenate([d_table, grad.astype(f32), d_proj, d_head], 0),
            jnp.concatenate([d_query, *d_gains, d_final], 0),
            d_mats,
            jnp.sum(errors),
        )
        gradients = found if gradients is None else jax.tree.map(jnp.add, gradients, found)

    g_dense, g_vectors, g_mats, error_sum = gradients
    both = ("section", "dp")
    whole = [[lax.psum(part, both) for part in g_mats[layer]] for layer in range(LAYERS)]
    dp_index = lax.axis_index("dp")
    parts = lax.axis_size("dp")
    r_dense = lax.psum(lax.psum_scatter(g_dense, "dp", scatter_dimension=1, tiled=True), "section")
    r_table = r_dense[:EXT].reshape(PIX + 1, LANES, -1)[:, :VARS].transpose(1, 0, 2).reshape(TABLE, -1)
    r_dense = jnp.concatenate([r_table, r_dense[EXT:]], 0)
    g_vectors = lax.psum(g_vectors, both)
    width = D // parts
    r_vectors = lax.dynamic_slice_in_dim(g_vectors, dp_index * width, width, 1)
    dense_square = jnp.sum(r_dense * r_dense)
    square_total, weight_total = lax.psum((dense_square, weight_local), "dp")
    error_total = lax.psum(error_sum, both)
    square_total = square_total + jnp.sum(g_vectors * g_vectors)
    square_total = square_total + sum(jnp.sum(part * part) for mats in whole for part in mats)
    grad_norm = jnp.sqrt(square_total) / weight_total
    factor = jnp.minimum(1.0, clip_level / grad_norm) / weight_total
    steps_done = step_count[0].astype(f32)
    dense_new, dense_m_new, dense_v_new = adam_update(
        dense, dense_m, dense_v, r_dense * factor, rate_dense, weight_decay, steps_done
    )
    vectors_new, vectors_m_new, vectors_v_new = adam_update(
        vectors, vectors_m, vectors_v, r_vectors * factor, rate_vector, 0.0, steps_done
    )
    right_roots = [root_qkv, root_small[:, 2], root_wide[:, 0], root_small[:, 4]]
    left_roots = [root_small[:, 0], root_small[:, 1], root_small[:, 3], root_wide[:, 1]]
    lefts = [stat_small[:, 0], stat_small[:, 1], stat_small[:, 3], stat_wide[:, 1]]
    rights = [stat_qkv, stat_small[:, 2], stat_wide[:, 0], stat_small[:, 4]]
    matrices = [w_qkv, w_out, w_fc1, w_fc2]
    new_lefts, new_rights, new_weights = [], [], []
    for at in range(4):
        wide_root = lax.all_gather(right_roots[at], "dp", axis=1, tiled=True)
        whole_grad = jnp.stack([whole[layer][at] for layer in range(LAYERS)]) * factor
        rows = whole_grad.shape[1] // parts
        cols = whole_grad.shape[2] // parts
        own_rows = lax.dynamic_slice_in_dim(whole_grad, dp_index * rows, rows, 1)
        own_cols = lax.dynamic_slice_in_dim(whole_grad, dp_index * cols, cols, 2)
        new_lefts.append(
            stat_beta * lefts[at]
            + (1.0 - stat_beta) * jnp.einsum("kin,kjn->kij", own_rows, whole_grad, precision=highest)
        )
        new_rights.append(
            stat_beta * rights[at]
            + (1.0 - stat_beta) * jnp.einsum("kmi,kmj->kij", own_cols, whole_grad, precision=highest)
        )
        step = jnp.einsum(
            "kin,knj->kij",
            jnp.einsum("kim,kmn->kin", left_roots[at], whole_grad, precision=highest),
            wide_root,
            precision=highest,
        )
        new_weights.append(matrices[at] - rate_matrix * step)
    stat_small_new = jnp.stack(
        [new_lefts[0], new_lefts[1], new_rights[1], new_lefts[2], new_rights[3]], axis=1
    )
    stat_wide_new = jnp.stack([new_rights[2], new_lefts[3]], axis=1)
    return (
        error_total / weight_total,
        grad_norm,
        dense_new,
        dense_m_new,
        dense_v_new,
        average(dense_ema, dense_new),
        vectors_new,
        vectors_m_new,
        vectors_v_new,
        average(vectors_ema, vectors_new),
        new_weights[0],
        new_weights[1],
        new_weights[2],
        new_weights[3],
        average(ema_qkv, new_weights[0]),
        average(ema_out, new_weights[1]),
        average(ema_fc1, new_weights[2]),
        average(ema_fc2, new_weights[3]),
        stat_small_new,
        new_rights[0],
        stat_wide_new,
    )


def solution(mesh):
    items = P("dp", None, None)
    columns = P(None, "dp")
    matrix = P(None, "dp", None)
    stacked = P(None, None, "dp", None)
    return jax.shard_map(
        per_device,
        mesh=mesh,
        in_specs=(
            (items, items, P("dp"), P())
            + (columns,) * 8
            + (matrix,) * 8
            + (stacked, matrix, stacked) * 2
        ),
        out_specs=(P(), P()) + (columns,) * 8 + (matrix,) * 8 + (stacked, matrix, stacked),
        check_vma=False,
    )
```

```python
import functools
import math

import jax
import jax.numpy as jnp
import numpy as np
from jax import lax
from jax.experimental import pallas as pl
from jax.experimental.pallas import tpu as pltpu
from jax.sharding import PartitionSpec as P

D = 384
HEADS = 6
HDIM = 64
SURF = 4
LEVELS = 13
VARS = 69
PIX = 4
VP = 276
LAT_ROWS = 64
LON_COLS = 16
SEQ = 1024
LAYERS = 2
FF = 1536
BLOCKS = 4 + 2 * (FF // D)

LANES = 128
PAIRS = HEADS // 2
EXT = (PIX + 1) * LANES
TABLE = VARS * (PIX + 1)

AT_PROJ = SEQ
AT_HEAD = AT_PROJ + D
AT_TABLE = AT_HEAD + 3 * LANES
AT_VECTOR = AT_TABLE + EXT
SLOTS = AT_VECTOR + LANES

highest = lax.Precision.HIGHEST
f32 = jnp.float32
bf16 = jnp.bfloat16
norm_eps = 1e-05
clip_level = 0.001
rate_dense = 0.05
rate_vector = 0.2
rate_matrix = 0.5
beta_first = 0.9
beta_second = 0.95
adam_eps = 1e-08
weight_decay = 0.1
stat_beta = 0.95
ema_beta = 0.9
LOG2E = math.log2(math.e)
SCALE2 = LOG2E * HDIM ** (-0.5)

NN = (((1,), (0,)), ((), ()))
NT = (((1,), (1,)), ((), ()))
TN = (((0,), (0,)), ((), ()))


def dot(left, right, dims=NN):
    return lax.dot_general(left, right, dims, preferred_element_type=f32)


def halves(value):
    high = value.astype(bf16)
    return high, (value - high.astype(f32)).astype(bf16)


def call(body, out_shape, scratch=(), vmem=60 << 20, flops=0, traffic=0):
    return pl.pallas_call(
        body,
        out_shape=out_shape,
        scratch_shapes=list(scratch),
        compiler_params=pltpu.CompilerParams(vmem_limit_bytes=vmem),
        cost_estimate=pl.CostEstimate(flops=flops, bytes_accessed=traffic, transcendentals=0),
    )


def shape(dims, kind=f32):
    return jax.ShapeDtypeStruct(dims, kind)


def norm_parts(values):
    center = values - jnp.mean(values, -1, keepdims=True)
    spread = jnp.mean(center * center, -1, keepdims=True)
    inverse = lax.rsqrt(spread + norm_eps)
    return center * inverse, inverse


def norm_back(values, gain, upstream):
    unit, inverse = norm_parts(values)
    scaled = upstream * gain
    back = inverse * (
        scaled
        - jnp.mean(scaled, -1, keepdims=True)
        - unit * jnp.mean(scaled * unit, -1, keepdims=True)
    )
    return back, jnp.sum(upstream * unit, 0, keepdims=True)


def tiles(count, body):
    def step(index, carry):
        body(index)
        return carry

    lax.fori_loop(0, count, step, 0)


def rows_of(index, size):
    return pl.ds(pl.multiple_of(index * size, size), size)


def head_mask(rows, which):
    lane = lax.broadcasted_iota(jnp.int32, (rows, LANES), 1)
    return (lane >= which * HDIM) & (lane < (which + 1) * HDIM)


def spread_fields(field_rows):
    row = lax.broadcasted_iota(jnp.int32, (VP, PIX * LANES), 0)
    col = lax.broadcasted_iota(jnp.int32, (VP, PIX * LANES), 1)
    var, pixel = col % LANES, col // LANES
    chosen = (row == PIX * var + pixel) & (var < VARS)
    return dot(field_rows, jnp.where(chosen, 1.0, 0.0).astype(bf16))


def query_mask(query_row):
    head = lax.broadcasted_iota(jnp.int32, (8, D), 0)
    lane = lax.broadcasted_iota(jnp.int32, (8, D), 1)
    return jnp.where(lane // HDIM == head, query_row * HDIM ** (-0.5), 0.0)


def query_scores(table_ref, mask, query_scr):
    for j in range(PIX + 1):
        part = table_ref[j * LANES : (j + 1) * LANES, :]
        query_scr[j * 8 : (j + 1) * 8, :] = dot(mask.astype(bf16), part, NT)


def mix_weights(extended, query_scr, head, valid):
    score = query_scr[pl.ds(PIX * 8 + head, 1), :]
    for j in range(PIX):
        score = score + extended[j] * query_scr[pl.ds(j * 8 + head, 1), :]
    score = jnp.where(valid > 0, score, jnp.where(valid < 0, -jnp.inf, -1e9))
    peak = jnp.max(score, -1, keepdims=True)
    weight = jnp.exp(score - peak)
    return weight / jnp.sum(weight, -1, keepdims=True)


def embed_body(field_ref, table_ref, query_ref, valid_ref, proj_ref, pos_ref, out_ref, agg_ref, query_scr):
    size = 256
    query_scores(table_ref, query_mask(query_ref[...]), query_scr)

    def tile(index):
        rows = rows_of(index, size)
        wide = spread_fields(field_ref[rows, :])
        extended = [wide[:, j * LANES : (j + 1) * LANES] for j in range(PIX)]
        valid = valid_ref[...]

        def pair(hp, carry):
            lanes = rows_of(hp, LANES)
            table = table_ref[:, lanes]
            total = jnp.zeros((size, LANES), f32)
            for which in range(2):
                weight = mix_weights(extended, query_scr, 2 * hp + which, valid)
                mixing = jnp.concatenate([weight * extended[j] for j in range(PIX)] + [weight], 1)
                own = jnp.where(head_mask(EXT, which), table, jnp.zeros_like(table))
                high, low = halves(mixing)
                total = total + dot(high, own) + dot(low, own)
            agg_ref[rows, lanes] = total.astype(bf16)
            return carry

        lax.fori_loop(0, PAIRS, pair, 0)
        out_ref[rows, :] = (dot(agg_ref[rows, :], proj_ref[...]) + pos_ref[rows, :].astype(f32)).astype(bf16)

    tiles(SEQ // size, tile)


def embed_forward(field_rows, table, query_row, valid, proj, position):
    return call(
        embed_body,
        (shape((SEQ, D), bf16), shape((SEQ, D), bf16)),
        [pltpu.VMEM((40, LANES), f32)],
        flops=4_000_000_000,
        traffic=4_000_000,
    )(field_rows, table, query_row, valid, proj, position)


def embed_back_body(
    field_ref, table_ref, query_ref, valid_ref, proj_ref, agg_ref, grad_ref, dhead_ref, dvector_ref,
    out_ref, vector_scr, query_scr, wide_scr, merged_scr, high_scr, low_scr, dscore_scr,
):
    size = 256
    mask = query_mask(query_ref[...])
    query_scores(table_ref, mask, query_scr)
    out_ref[:, AT_PROJ : AT_PROJ + D] = dot(grad_ref[...], agg_ref[...], TN)
    out_ref[:, AT_HEAD:AT_TABLE] = jnp.zeros((D, AT_TABLE - AT_HEAD), f32)
    out_ref[:, AT_HEAD : AT_HEAD + VP] = dhead_ref[...]
    dscore_scr[...] = jnp.zeros_like(dscore_scr)

    def prepare(index):
        rows = rows_of(index, size)
        wide_scr[rows, :] = spread_fields(field_ref[rows, :])
        merged_scr[rows, :] = dot(grad_ref[rows, :], proj_ref[...], NT)
        out_ref[:, rows] = grad_ref[rows, :].astype(f32).T

    tiles(SEQ // size, prepare)

    def pair(hp):
        lanes = rows_of(hp, LANES)
        table = table_ref[:, lanes]
        total = jnp.zeros((LANES, EXT), f32)
        for which in range(2):
            head = 2 * hp + which
            own = jnp.where(head_mask(EXT, which), table, jnp.zeros_like(table))
            twice = jnp.concatenate([own, own], 1)

            def tile(index):
                rows = rows_of(index, size)
                extended = [wide_scr[rows, j * LANES : (j + 1) * LANES] for j in range(PIX)]
                weight = mix_weights(extended, query_scr, head, valid_ref[...])
                mixing = jnp.concatenate([weight * extended[j] for j in range(PIX)] + [weight], 1)
                high, low = halves(mixing)
                high_scr[rows, :] = high
                low_scr[rows, :] = low
                grad_high, grad_low = halves(merged_scr[rows, lanes])
                dmix = dot(jnp.concatenate([grad_high, grad_low], 1), twice, NT)
                dweight = dmix[:, PIX * LANES :]
                for j in range(PIX):
                    dweight = dweight + dmix[:, j * LANES : (j + 1) * LANES] * extended[j]
                dscore = weight * (dweight - jnp.sum(weight * dweight, -1, keepdims=True))
                for j in range(PIX + 1):
                    piece = dscore * extended[j] if j < PIX else dscore
                    at = pl.ds(j * 8 + head, 1)
                    dscore_scr[at, :] = dscore_scr[at, :] + jnp.sum(piece, 0, keepdims=True)

            tiles(SEQ // size, tile)
            grad_high, grad_low = halves(merged_scr[:, lanes])
            keep = head_mask(SEQ, which)
            grad_high = jnp.where(keep, grad_high, jnp.zeros_like(grad_high))
            grad_low = jnp.where(keep, grad_low, jnp.zeros_like(grad_low))
            both = dot(jnp.concatenate([grad_high, grad_low], 1), high_scr[...], TN)
            total = total + both[:LANES, :] + both[LANES:, :] + dot(grad_high, low_scr[...], TN)
        out_ref[lanes, AT_TABLE:AT_VECTOR] = total

    tiles(PAIRS, pair)
    dquery = jnp.zeros((1, D), f32)
    head = lax.broadcasted_iota(jnp.int32, (8, D), 0)
    lane = lax.broadcasted_iota(jnp.int32, (8, D), 1)
    for j in range(PIX + 1):
        part = dscore_scr[j * 8 : (j + 1) * 8, :]
        block = slice(j * LANES, (j + 1) * LANES)
        lanes = slice(AT_TABLE + j * LANES, AT_TABLE + (j + 1) * LANES)
        out_ref[:, lanes] = out_ref[:, lanes] + lax.dot_general(
            mask, part, TN, precision=highest, preferred_element_type=f32
        )
        spread = lax.dot_general(
            part, table_ref[block, :].astype(f32), NN, precision=highest, preferred_element_type=f32
        )
        dquery = dquery + jnp.sum(jnp.where(lane // HDIM == head, spread, 0.0), 0, keepdims=True)
    vector_scr[...] = jnp.zeros_like(vector_scr)
    vector_scr[0:8, :] = dvector_ref[...]
    vector_scr[0:1, :] = dquery * HDIM ** (-0.5)
    out_ref[:, AT_VECTOR:SLOTS] = vector_scr[...].T


def embed_back(field_rows, table, query_row, valid, proj, agg, grad, dhead, dvector):
    return call(
        embed_back_body,
        shape((D, SLOTS)),
        [
            pltpu.VMEM((LANES, D), f32),
            pltpu.VMEM((40, LANES), f32),
            pltpu.VMEM((SEQ, PIX * LANES), f32),
            pltpu.VMEM((SEQ, D), f32),
            pltpu.VMEM((SEQ, EXT), bf16),
            pltpu.VMEM((SEQ, EXT), bf16),
            pltpu.VMEM((40, LANES), f32),
        ],
        flops=12_000_000_000,
        traffic=6_000_000,
    )(field_rows, table, query_row, valid, proj, agg, grad, dhead, dvector)


def square(ref, index):
    return ref[index * D : (index + 1) * D, :]


def block_body(x_ref, gain_ref, w_ref,
               h_ref, qkv_ref, o_ref, lse_ref, m_ref, h2_ref, y_ref):
    size = 256

    def enter(index):
        rows = rows_of(index, size)
        unit, unused = norm_parts(x_ref[rows, :].astype(f32))
        hidden = (unit * gain_ref[0:1, :]).astype(bf16)
        h_ref[rows, :] = hidden
        for b in range(3):
            qkv_ref[rows, b * D : (b + 1) * D] = dot(hidden, square(w_ref, b)).astype(bf16)

    tiles(SEQ // size, enter)
    lse_ref[...] = jnp.zeros_like(lse_ref)

    def pair(hp):
        keys = qkv_ref[:, pl.ds(pl.multiple_of(D + hp * LANES, LANES), LANES)]
        values = qkv_ref[:, pl.ds(pl.multiple_of(2 * D + hp * LANES, LANES), LANES)]

        def tile(index):
            rows = rows_of(index, size)
            queries = qkv_ref[rows, rows_of(hp, LANES)]
            parts = []
            for which in range(2):
                own = jnp.where(head_mask(size, which), queries, jnp.zeros_like(queries))
                score = dot(keys, own, NT) * SCALE2
                peak = jnp.max(score, 0, keepdims=True)
                power = jnp.exp2(score - peak)
                total = jnp.sum(power, 0, keepdims=True)
                chance = (power * (1.0 / total)).astype(bf16)
                mixed = dot(values, chance, TN)
                parts.append(mixed[which * HDIM : (which + 1) * HDIM, :])
                lse_ref[pl.ds(2 * hp + which, 1), rows] = peak + jnp.log2(total)
            o_ref[rows, rows_of(hp, LANES)] = jnp.concatenate(parts, 0).T.astype(bf16)

        tiles(SEQ // size, tile)

    tiles(PAIRS, pair)

    def leave(index):
        rows = rows_of(index, size)
        middle = x_ref[rows, :].astype(f32) + dot(o_ref[rows, :], square(w_ref, 3))
        m_ref[rows, :] = middle
        unit, unused = norm_parts(middle)
        hidden = (unit * gain_ref[1:2, :]).astype(bf16)
        h2_ref[rows, :] = hidden
        total = jnp.zeros((size, D), f32)
        for b in range(FF // D):
            before = dot(hidden, square(w_ref, 4 + b))
            active = (0.5 * before * (1.0 + lax.erf(before * math.sqrt(0.5)))).astype(bf16)
            total = total + dot(active, square(w_ref, 8 + b))
        y_ref[rows, :] = (middle + total).astype(bf16)

    tiles(SEQ // size, leave)


def block_forward(x, gains, weights):
    return call(
        block_body,
        (
            shape((SEQ, D), bf16),
            shape((SEQ, 3 * D), bf16),
            shape((SEQ, D), bf16),
            shape((8, SEQ)),
            shape((SEQ, D)),
            shape((SEQ, D), bf16),
            shape((SEQ, D), bf16),
        ),
        flops=12_000_000_000,
        traffic=12_000_000,
    )(x, gains, weights)


def feed_back_body(h2_ref, m_ref, dy_ref, gain_ref, w_ref, dm_ref, do_ref, dgain_ref, dw_ref, r_scr, df_scr):
    size = 256
    dgain_ref[...] = jnp.zeros_like(dgain_ref)

    def first(index):
        rows = rows_of(index, size)
        grad_next = dy_ref[rows, :]
        hidden = h2_ref[rows, :]
        upstream = jnp.zeros((size, D), f32)
        for b in range(FF // D):
            cols = slice(b * D, (b + 1) * D)
            before = dot(hidden, square(w_ref, 4 + b))
            upper = 0.5 * (1.0 + lax.erf(before * math.sqrt(0.5)))
            r_scr[rows, cols] = (before * upper).astype(bf16)
            slope = upper + before * (jnp.exp2(before * before * (-0.5 * LOG2E)) * (1.0 / math.sqrt(2 * math.pi)))
            grad_before = (dot(grad_next, square(w_ref, 8 + b), NT) * slope).astype(bf16)
            df_scr[rows, cols] = grad_before
            upstream = upstream + dot(grad_before, square(w_ref, 4 + b), NT)
        back, dgain = norm_back(m_ref[rows, :], gain_ref[1:2, :], upstream)
        dgain_ref[...] = dgain_ref[...] + dgain
        middle = grad_next.astype(f32) + back
        dm_ref[rows, :] = middle
        do_ref[rows, :] = dot(middle.astype(bf16), square(w_ref, 3), NT).astype(bf16)

    tiles(SEQ // size, first)

    def wide(index):
        cols = rows_of(index, D)
        dw_ref[rows_of(index, D), :] = dot(h2_ref[...], df_scr[:, cols], TN)
        dw_ref[rows_of(FF // D + index, D), :] = dot(r_scr[:, cols], dy_ref[...], TN)

    tiles(FF // D, wide)


def feed_back(h2, m, dy, gains, weights):
    return call(
        feed_back_body,
        (shape((SEQ, D)), shape((SEQ, D), bf16), shape((1, D)), shape((2 * FF, D))),
        [pltpu.VMEM((SEQ, FF), bf16), pltpu.VMEM((SEQ, FF), bf16)],
        flops=17_000_000_000,
        traffic=14_000_000,
    )(h2, m, dy, gains, weights)


def mix_back_body(x_ref, h_ref, qkv_ref, o_ref, lse_ref, dm_ref, do_ref, gain_ref, w_ref,
                  dx_ref, dgain_ref, dw_ref, dqkv_scr, dkv_scr):
    size = 256
    dgain_ref[...] = jnp.zeros_like(dgain_ref)
    dw_ref[3 * D : 4 * D, :] = dot(o_ref[...], dm_ref[...].astype(bf16), TN)

    def pair(hp):
        lanes = rows_of(hp, LANES)
        klanes = pl.ds(pl.multiple_of(D + hp * LANES, LANES), LANES)
        vlanes = pl.ds(pl.multiple_of(2 * D + hp * LANES, LANES), LANES)
        keys = qkv_ref[:, klanes]
        values = qkv_ref[:, vlanes]
        dkv_scr[...] = jnp.zeros_like(dkv_scr)

        def tile(index):
            rows = rows_of(index, size)
            queries = qkv_ref[rows, lanes]
            upstream = do_ref[rows, lanes]
            parts = []
            for which in range(2):
                keep = head_mask(size, which)
                own = jnp.where(keep, queries, jnp.zeros_like(queries))
                own_up = jnp.where(keep, upstream, jnp.zeros_like(upstream))
                score = dot(keys, own, NT) * SCALE2
                chance = jnp.exp2(score - lse_ref[pl.ds(2 * hp + which, 1), rows])
                dchance = dot(values, own_up, NT)
                shift = jnp.sum(dchance * chance, 0, keepdims=True)
                dscore = (chance * (dchance - shift)).astype(bf16)
                dkv_scr[:, :LANES] = dkv_scr[:, :LANES] + dot(dscore, own)
                dkv_scr[:, LANES:] = dkv_scr[:, LANES:] + dot(chance.astype(bf16), own_up)
                dquery = dot(keys, dscore, TN)
                parts.append(dquery[which * HDIM : (which + 1) * HDIM, :])
            dqkv_scr[rows, lanes] = (jnp.concatenate(parts, 0).T * HDIM ** (-0.5)).astype(bf16)

        tiles(SEQ // size, tile)
        dqkv_scr[:, klanes] = (dkv_scr[:, :LANES] * HDIM ** (-0.5)).astype(bf16)
        dqkv_scr[:, vlanes] = dkv_scr[:, LANES:].astype(bf16)

    tiles(PAIRS, pair)

    def third(index):
        cols = rows_of(index, D)
        dw_ref[cols, :] = dot(h_ref[...], dqkv_scr[:, cols], TN)

    tiles(3, third)

    def last(index):
        rows = rows_of(index, size)
        upstream = jnp.zeros((size, D), f32)
        for b in range(3):
            upstream = upstream + dot(dqkv_scr[rows, b * D : (b + 1) * D], square(w_ref, b), NT)
        back, dgain = norm_back(x_ref[rows, :].astype(f32), gain_ref[0:1, :], upstream)
        dgain_ref[...] = dgain_ref[...] + dgain
        dx_ref[rows, :] = (dm_ref[rows, :] + back).astype(bf16)

    tiles(SEQ // size, last)


def mix_back(x, kept, dm, do, gains, weights):
    return call(
        mix_back_body,
        (shape((SEQ, D), bf16), shape((1, D)), shape((4 * D, D))),
        [pltpu.VMEM((SEQ, 3 * D), bf16), pltpu.VMEM((SEQ, 2 * LANES), f32)],
        flops=17_000_000_000,
        traffic=14_000_000,
    )(x, *kept, dm, do, gains, weights)


def head_body(y_ref, gain_ref, head_ref, target_ref, cos_ref, valid_ref,
              dy_ref, dhead_ref, dgain_ref, error_ref, h_scr, dp_scr):
    size = 256
    dgain_ref[...] = jnp.zeros_like(dgain_ref)
    error_ref[...] = jnp.zeros_like(error_ref)

    def tile(index):
        rows = rows_of(index, size)
        values = y_ref[rows, :].astype(f32)
        unit, unused = norm_parts(values)
        hidden = (unit * gain_ref[...]).astype(bf16)
        h_scr[rows, :] = hidden
        residual = dot(hidden, head_ref[...], NT) - target_ref[rows, :].astype(f32)
        lane = lax.broadcasted_iota(jnp.int32, (size, VP), 1)
        cosine = jnp.where(lane % PIX < 2, cos_ref[rows, 0:1], cos_ref[rows, 1:2])
        weight = cosine * valid_ref[...]
        error_ref[...] = error_ref[...] + jnp.sum(weight * residual * residual, 0, keepdims=True)
        grad = (2.0 * weight * residual).astype(bf16)
        dp_scr[rows, :] = grad
        back, dgain = norm_back(values, gain_ref[...], dot(grad, head_ref[...]))
        dgain_ref[...] = dgain_ref[...] + dgain
        dy_ref[rows, :] = back.astype(bf16)

    tiles(SEQ // size, tile)
    dhead_ref[...] = dot(h_scr[...], dp_scr[...], TN)


def head_step(y, gain, head_rows, target, cosines, valid):
    return call(
        head_body,
        (shape((SEQ, D), bf16), shape((D, VP)), shape((1, D)), shape((1, VP))),
        [pltpu.VMEM((SEQ, D), bf16), pltpu.VMEM((SEQ, VP), bf16)],
        flops=700_000_000,
        traffic=4_000_000,
    )(y, gain, head_rows, target, cosines, valid)


def dot3(left, right, dims=NN):
    return dot(left[0], right[0], dims) + dot(left[0], right[1], dims) + dot(left[1], right[0], dims)


def chosen_rows(count, width, start, offset):
    row = lax.broadcasted_iota(jnp.int32, (count, width), 0)
    col = lax.broadcasted_iota(jnp.int32, (count, width), 1)
    return jnp.where(col + offset == row + start, 1.0, 0.0).astype(bf16)


def pick(selector, pair, dims=NN):
    return [dot(selector, part, dims).astype(bf16) for part in pair]


def shampoo_body(pieces, along, index_ref, factor_ref, small_ref, qkv_ref, wide_ref, around_ref,
                 left_out_ref, left_fc2_ref, right_qkv_ref, right_fc1_ref,
                 wout_ref, wfc2_ref, eout_ref, efc2_ref, *rest):
    piece_refs, rest = rest[:pieces], rest[pieces:]
    rest = rest[7:]
    (nsmall_ref, nqkv_ref, nwide_ref, nout_ref, nfc2_ref, meout_ref, mefc2_ref,
     step_ref, high_scr, low_scr) = rest
    me = index_ref[0]
    factor = factor_ref[0]
    wide_rows, tall_rows = 2 * FF // (pieces * along), 4 * D // (pieces * along)
    for k in range(pieces):
        block = jnp.bitwise_xor(index_ref[1], k) * along
        for j in range(along):
            place = block + jnp.bitwise_xor(index_ref[2], j)
            at = j * (wide_rows + tall_rows)
            high, low = halves(piece_refs[k][at : at + wide_rows, :])
            rows = pl.ds(pl.multiple_of(4 * D + place * wide_rows, 16), wide_rows)
            high_scr[rows, :] = high
            low_scr[rows, :] = low
            high, low = halves(piece_refs[k][at + wide_rows : at + wide_rows + tall_rows, :])
            rows = pl.ds(pl.multiple_of(place * tall_rows, 16), tall_rows)
            high_scr[rows, :] = high
            low_scr[rows, :] = low

    def grad(b):
        return square(high_scr, b), square(low_scr, b)

    def mixed(old, product):
        return stat_beta * old + (1.0 - stat_beta) * (factor * (factor * product))

    def root(k):
        return halves(around_ref[0, k])

    rows = small_ref.shape[2]
    own_row = chosen_rows(rows, D, me * rows, 0)
    place = 0
    for first, count, left, right_ref, nright_ref, right_root_ref, left_root in (
        (0, 3, 0, qkv_ref, nqkv_ref, right_qkv_ref, 0),
        (4, FF // D, 3, wide_ref, nwide_ref, right_fc1_ref, 2),
    ):
        take = (0, 0) if first else (0,)
        cols = right_ref.shape[-2]
        total = jnp.zeros((rows, D), f32)
        own_cols = [jnp.zeros((cols, D), f32)] * 2
        share = right_root_ref.shape[-2]
        reach = jnp.zeros((D, share), f32)
        for b in range(count):
            block = grad(first + b)
            total = total + dot3(pick(own_row, block), block, NT)
            selector = chosen_rows(cols, D, me * cols, b * D)
            own_cols = [own + dot(selector, part, NT) for own, part in zip(own_cols, block)]
            reach = reach + dot3(block, halves(right_root_ref[take + (slice(None), slice(b * D, (b + 1) * D))]), NT)
        nsmall_ref[0, left] = mixed(small_ref[0, left], total)
        own_cols = [own.astype(bf16) for own in own_cols]
        for b in range(count):
            lanes = slice(b * D, (b + 1) * D)
            nright_ref[take + (slice(None), lanes)] = mixed(
                right_ref[take + (slice(None), lanes)], dot3(own_cols, grad(first + b))
            )
        step_ref[:, place : place + share] = dot3(root(left_root), halves(reach))
        place = place + share

    block = grad(3)
    nsmall_ref[0, 1] = mixed(small_ref[0, 1], dot3(pick(own_row, block), block, NT))
    nsmall_ref[0, 2] = mixed(small_ref[0, 2], dot3(pick(own_row, block, NT), block))
    moved = dot3(halves(dot3(halves(left_out_ref[0, 0]), block)), root(1))
    updated = wout_ref[0] - rate_matrix * factor * moved
    nout_ref[0] = updated
    meout_ref[0] = average(eout_ref[0], updated)

    tall = wide_ref.shape[2]
    total = jnp.zeros((rows, D), f32)
    own = [jnp.zeros((tall, D), f32)] * 2
    reach = jnp.zeros((tall, D), f32)
    for b in range(FF // D):
        block = grad(8 + b)
        total = total + dot3(pick(own_row, block, NT), block)
        selector = chosen_rows(tall, D, me * tall, b * D)
        own = [o + dot(selector, part) for o, part in zip(own, block)]
        reach = reach + dot3(halves(left_fc2_ref[0, 0, :, b * D : (b + 1) * D]), block)
    nsmall_ref[0, 4] = mixed(small_ref[0, 4], total)
    own = [o.astype(bf16) for o in own]
    for b in range(FF // D):
        lanes = slice(b * D, (b + 1) * D)
        nwide_ref[0, 1, :, lanes] = mixed(wide_ref[0, 1, :, lanes], dot3(own, grad(8 + b), NT))
    updated = wfc2_ref[0] - rate_matrix * factor * dot3(halves(reach), root(3))
    nfc2_ref[0] = updated
    mefc2_ref[0] = average(efc2_ref[0], updated)


def layer_block(array, layer):
    return pl.BlockSpec(
        (1,) + array.shape[1:], lambda i: (layer,) + (0,) * (array.ndim - 1), pipeline_mode=pl.Buffered(1)
    )


def whole_block(array):
    return pl.BlockSpec(array.shape, lambda i: (0,) * array.ndim, pipeline_mode=pl.Buffered(1))


def shampoo(layer, pieces, along, index, factor, stats, around, roots, weights, averages, previous):
    small, qkv, wide = stats
    root_small, root_qkv, root_wide = roots
    scalar = pl.BlockSpec(memory_space=pltpu.SMEM)
    rows, tall = small.shape[2], wide.shape[2]
    root_out = pl.BlockSpec((1, 1, rows, D), lambda i: (layer, 1, 0, 0), pipeline_mode=pl.Buffered(1))
    root_fc2 = pl.BlockSpec((1, 1, tall, FF), lambda i: (layer, 1, 0, 0), pipeline_mode=pl.Buffered(1))
    layered = [small, qkv, wide, around]
    root_fc1 = pl.BlockSpec((1, 1, tall, FF), lambda i: (layer, 0, 0, 0), pipeline_mode=pl.Buffered(1))
    tails = [*weights, *averages]
    results = [small, qkv, wide, *weights, *averages]
    operands = [index, factor, *layered, root_small, root_wide, root_qkv, root_wide, *tails, *pieces]
    specs = [scalar, scalar] + [layer_block(x, layer) for x in layered] + [root_out, root_fc2, layer_block(root_qkv, layer), root_fc1]
    specs += [layer_block(x, layer) for x in tails] + [whole_block(x) for x in pieces]
    aliases = {}
    if previous is not None:
        aliases = {len(operands) + k: k for k in range(len(results))}
    else:
        previous = [jnp.zeros((8, LANES), f32)] * len(results)
    operands += previous
    specs += [pl.BlockSpec(memory_space=pl.ANY)] * len(results)
    width = root_qkv.shape[1] + tall
    *new, step = pl.pallas_call(
        functools.partial(shampoo_body, len(pieces), along),
        grid=(1,),
        in_specs=specs,
        out_specs=[layer_block(x, layer) for x in results]
        + [pl.BlockSpec((D, width), lambda i: (0, 0), pipeline_mode=pl.Buffered(1))],
        out_shape=[shape(x.shape) for x in results] + [shape((D, width))],
        scratch_shapes=[pltpu.VMEM((BLOCKS * D, D), bf16)] * 2,
        input_output_aliases=aliases,
        compiler_params=pltpu.CompilerParams(vmem_limit_bytes=60 << 20),
        cost_estimate=pl.CostEstimate(flops=5_000_000_000, bytes_accessed=30_000_000, transcendentals=0),
    )(*operands)
    return new, step


def finish_body(parts, index_ref, factor_ref, *refs):
    found, refs = refs[:LAYERS], refs[LAYERS:]
    (wqkv_ref, wfc1_ref, eqkv_ref, efc1_ref, nqkv_ref, nfc1_ref, mqkv_ref, mfc1_ref) = refs
    scale = rate_matrix * factor_ref[0]
    for layer in range(LAYERS):
        place = 0
        for w_ref, e_ref, n_ref, a_ref in (
            (wqkv_ref, eqkv_ref, nqkv_ref, mqkv_ref), (wfc1_ref, efc1_ref, nfc1_ref, mfc1_ref)
        ):
            share = w_ref.shape[2] // parts
            for j in range(parts):
                which = jnp.bitwise_xor(index_ref[0], j)
                lanes = slice(j * share, (j + 1) * share)
                step = found[layer][which, :, place : place + share]
                updated = w_ref[layer, :, lanes] - scale * step
                n_ref[layer, :, lanes] = updated
                a_ref[layer, :, lanes] = average(e_ref[layer, :, lanes], updated)
            place = place + share


def finish(parts, index, factor, found, weights, averages):
    scalar = pl.BlockSpec(memory_space=pltpu.SMEM)
    operands = [*found, *weights, *averages]
    return pl.pallas_call(
        functools.partial(finish_body, parts),
        in_specs=[scalar, scalar] + [pl.BlockSpec(memory_space=pltpu.VMEM)] * len(operands),
        out_shape=[shape(x.shape) for x in (*weights, *averages)],
        compiler_params=pltpu.CompilerParams(vmem_limit_bytes=40 << 20),
        cost_estimate=pl.CostEstimate(flops=10_000_000, bytes_accessed=6_000_000, transcendentals=0),
    )(index, factor, *operands)


def adam_body(index_ref, scalar_ref, *refs):
    pieces, refs = refs[:-17], refs[-17:]
    dense, vectors, new_dense, new_vectors, turned_scr = refs[:4], refs[4:8], refs[8:12], refs[12:16], refs[16]
    width = dense[0].shape[1]
    span = pieces[0].shape[1]
    for k, piece in enumerate(pieces):
        place = jnp.bitwise_xor(index_ref[3], k)
        turned_scr[pl.ds(pl.multiple_of(place * span, LANES), span), :] = piece[...].T

    def update(refs, news, target, source, count, rate, decay):
        old = [ref[target, :] for ref in refs]
        gradient = turned_scr[source : source + count, :][:, :width] * scalar_ref[0]
        first = beta_first * old[1] + (1.0 - beta_first) * gradient
        second = beta_second * old[2] + (1.0 - beta_second) * gradient * gradient
        first_hat = first / scalar_ref[1]
        second_hat = second / scalar_ref[2]
        updated = old[0] - rate * (first_hat / (jnp.sqrt(second_hat) + adam_eps) + decay * old[0])
        for ref, value in zip(news, (updated, first, second, average(old[3], updated))):
            ref[target, :] = value

    args = (dense, new_dense)
    for j in range(PIX + 1):
        update(*args, pl.ds(j, VARS, PIX + 1), AT_TABLE + j * LANES, VARS, rate_dense, weight_decay)
    update(*args, slice(TABLE, TABLE + SEQ + D), 0, SEQ + D, rate_dense, weight_decay)
    update(*args, slice(TABLE + SEQ + D, TABLE + SEQ + D + VP), AT_HEAD, VP, rate_dense, weight_decay)
    update(vectors, new_vectors, slice(0, 2 * LAYERS + 2), AT_VECTOR, 2 * LAYERS + 2, rate_vector, 0.0)


def adam(index, scalars, pieces, dense, vectors):
    scalar = pl.BlockSpec(memory_space=pltpu.SMEM)
    operands = [*pieces, *dense, *vectors]
    return pl.pallas_call(
        adam_body,
        in_specs=[scalar, scalar] + [pl.BlockSpec(memory_space=pltpu.VMEM)] * len(operands),
        out_shape=[shape(x.shape) for x in (*dense, *vectors)],
        scratch_shapes=[pltpu.VMEM((SLOTS, pieces[0].shape[0]), f32)],
        compiler_params=pltpu.CompilerParams(vmem_limit_bytes=40 << 20),
        cost_estimate=pl.CostEstimate(flops=10_000_000, bytes_accessed=8_000_000, transcendentals=0),
    )(index, scalars, *operands)


def digits(count, start=1):
    found = []
    while start < count:
        radix = min(4, count // start)
        found.append((start, radix))
        start *= radix
    return found


def swap(values, axis, bits):
    return lax.ppermute(values, axis, [(k, k ^ bits) for k in range(lax.axis_size(axis))])


def digit(axis, bit, radix):
    return (lax.axis_index(axis) // bit) % radix


def share_out(values, dim, axis, bit, radix):
    size = values.shape[dim] // radix
    mine = digit(axis, bit, radix)

    def part(k):
        return lax.dynamic_slice_in_dim(values, jnp.bitwise_xor(mine, k) * size, size, dim)

    arrived = [swap(part(k), axis, k * bit) for k in range(1, radix)]
    total = part(0)
    for other in arrived:
        total = total + other
    return total


def collect(values, axis, bit, radix):
    return [values] + [swap(values, axis, k * bit) for k in range(1, radix)]


def in_order(found, place):
    low = 1
    while low < len(found):
        even = (place // low) % 2 == 0
        found = [jnp.where(even, found[k], found[k ^ low]) for k in range(len(found))]
        low *= 2
    return found


def gate(values, first):
    return lax.optimization_barrier((values, first))


def advance(values, sums):
    moved = [share_out(part, 0, *stages[0]) if stages else part for part, stages in sums]
    values, moved = gate(values, moved)
    return values, [[part, stages[1:]] for part, (unused, stages) in zip(moved, sums)]


def total_of(values, stages):
    for axis, bit, radix in stages:
        values = sum(in_order(collect(values, axis, bit, radix), digit(axis, bit, radix)))
    return values


def valid_flags(counts):
    var_index = jnp.arange(VARS)
    level_index = (var_index - SURF) % LEVELS
    inside = (var_index[None, :] < SURF) | (level_index[None, :] < counts[:, None])
    return jnp.where(inside, 1.0, 0.0).astype(f32)


def cosine_table():
    pixel_rows = 2 * LAT_ROWS
    latitude = (np.arange(pixel_rows) + 0.5) * (np.pi / pixel_rows) - 0.5 * np.pi
    cosine = np.cos(latitude)
    cosine = cosine / np.mean(cosine)
    by_row = cosine.reshape(LAT_ROWS, 2).repeat(LON_COLS, 0)
    return by_row.astype(np.float32), float(by_row.sum() * (PIX // 2))


def average(old_state, new_state):
    return ema_beta * old_state + (1.0 - ema_beta) * new_state


def column_blocks(part):
    rows, cols = part.shape
    return part.reshape(rows, cols // D, D).transpose(1, 0, 2).reshape(-1, D)


def pack_layer(parts):
    qkv, out, fc1, fc2 = [part.astype(bf16) for part in parts]
    return jnp.concatenate([column_blocks(qkv), out, column_blocks(fc1), fc2], 0)


def unpack_layer(full, rows):
    above = full[:, : rows * 8].reshape(-1, 8, rows, D).transpose(1, 0, 2, 3).reshape(8 * D, D)
    return jnp.concatenate([above, full[:, rows * 8 :].reshape(FF, D)], 0)


def per_device(
    fields, targets, level_count, step_count,
    dense, dense_m, dense_v, dense_ema, vectors, vectors_m, vectors_v, vectors_ema,
    w_qkv, w_out, w_fc1, w_fc2, ema_qkv, ema_out, ema_fc1, ema_fc2,
    stat_small, stat_qkv, stat_wide, root_small, root_qkv, root_wide,
):
    section = lax.axis_index("section")
    sections = lax.axis_size("section")
    dp_index = lax.axis_index("dp")
    parts = lax.axis_size("dp")
    rows_dense = dense.shape[0]
    both_rows = jnp.concatenate([dense, vectors], 0).astype(bf16)
    full_dense = lax.all_gather(both_rows, "dp", axis=1, tiled=True)
    gain_rows = full_dense[rows_dense:].astype(f32)
    layer_weights, before = [], full_dense
    for layer in range(LAYERS):
        packed = pack_layer([part[layer] for part in (w_qkv, w_out, w_fc1, w_fc2)])
        packed, before = gate(packed, before)
        if layer == 0:
            full_dense = before
        else:
            layer_weights[-1] = before
        before = lax.all_gather(packed, "dp", axis=0)
        layer_weights.append(before)
    near, layer_weights[-1] = gate(root_small, layer_weights[-1])
    around = lax.all_gather(near[:, np.array([0, 2, 3, 4])], "dp", axis=2, tiled=True)
    layer_weights = [unpack_layer(full, w_qkv.shape[1]) for full in layer_weights]
    micro_count = fields.shape[0]
    table = full_dense[:TABLE].reshape(VARS, PIX + 1, D).transpose(1, 0, 2)
    table = jnp.pad(table, ((0, 0), (0, LANES - VARS), (0, 0))).reshape(EXT, D)
    position = full_dense[TABLE : TABLE + SEQ]
    proj = full_dense[TABLE + SEQ : TABLE + SEQ + D]
    head_rows = full_dense[TABLE + SEQ + D : rows_dense]
    flags = valid_flags(level_count)
    by_row, row_total = cosine_table()
    weight_local = jnp.sum(flags) * row_total
    cosines = jnp.asarray(by_row)

    core = [("dp", 1, 2)]
    cross = [("section", bit, radix) for bit, radix in digits(sections)]
    along = [("dp", bit, radix) for bit, radix in digits(parts, 2)]
    turns = -(-micro_count // sections)
    turned, error_sum, d_mats = 0.0, 0.0, [0.0] * (2 * LAYERS)
    pending, ready = [], []
    for turn in range(turns):
        index = turn * sections + section
        active = jnp.where(index < micro_count, 1.0, 0.0).astype(f32)
        index = jnp.minimum(index, micro_count - 1)
        field_rows = lax.dynamic_index_in_dim(fields, index, 0, False)
        target = lax.dynamic_index_in_dim(targets, index, 0, False)
        flag_row = lax.dynamic_index_in_dim(flags, index, 0, True)
        valid_vars = jnp.pad(flag_row, ((0, 0), (0, LANES - VARS)), constant_values=-1.0)
        valid_values = jnp.repeat(flag_row * active, PIX, axis=1)
        x, agg = embed_forward(field_rows, table, gain_rows[0:1], valid_vars, proj, position)
        kept = []
        for layer in range(LAYERS):
            gains = gain_rows[1 + 2 * layer : 3 + 2 * layer]
            *saved, y = block_forward(x, gains, layer_weights[layer])
            kept.append((x, saved))
            x = y
        grad, d_head, d_final, errors = head_step(
            x, gain_rows[2 * LAYERS + 1 :], head_rows, target, cosines, valid_values
        )
        d_gains = [None] * (2 * LAYERS)
        for layer in reversed(range(LAYERS)):
            gains = gain_rows[1 + 2 * layer : 3 + 2 * layer]
            x, (h, qkv, o, lse, m, h2) = kept[layer]
            grad, pending = advance(grad, pending)
            pending, ready = pending + ready, []
            dm, do, d_gains[2 * layer + 1], found = feed_back(h2, m, grad, gains, layer_weights[layer])
            d_mats[2 * layer + 1] = d_mats[2 * layer + 1] + found if turn else found
            if turn == turns - 1:
                ready = [[d_mats[2 * layer + 1], core + cross + along]]
            do, pending = advance(do, pending)
            pending, ready = pending + ready, []
            grad, d_gains[2 * layer], found = mix_back(
                x, (h, qkv, o, lse), dm, do, gains, layer_weights[layer]
            )
            d_mats[2 * layer] = d_mats[2 * layer] + found if turn else found
            if turn == turns - 1:
                ready = [[d_mats[2 * layer], core + cross + along]]
        grad, pending = advance(grad, pending)
        pending, ready = pending + ready, []
        d_vectors = jnp.concatenate(
            [jnp.zeros((1, D), f32), *d_gains, d_final, jnp.zeros((6 - 2 * LAYERS, D), f32)], 0
        )
        found = embed_back(
            field_rows, table, gain_rows[0:1], valid_vars, proj, agg, grad, d_head, d_vectors
        )
        turned = turned + found if turn else found
        error_sum = error_sum + jnp.sum(errors)

    turned, pending = advance(turned, pending)
    own_mats = []
    for part, stages in pending:
        for stage in stages:
            part = share_out(part, 0, *stage)
        own_mats.append(part)
    width = D // parts
    own_dense = turned
    for axis, bit, radix in core:
        own_dense = share_out(own_dense.reshape(-1, radix, width, SLOTS), 1, axis, bit, radix)
    for axis, bit, radix in cross:
        own_dense = share_out(own_dense, 3, axis, bit, radix)
    for axis, bit, radix in along:
        own_dense = share_out(own_dense.reshape(-1, radix, width, own_dense.shape[3]), 1, axis, bit, radix)
    own_dense = own_dense.reshape(width, -1)

    square_own = sum(jnp.sum(part * part) for part in [own_dense] + own_mats)
    scalars = jnp.stack([square_own, error_sum, jnp.where(section == 0, weight_local, 0.0)])
    scalars = jnp.broadcast_to(jnp.pad(scalars, (0, LANES - 3))[None], (8, LANES))
    scalars = total_of(scalars, core + cross + along)

    pieces = []
    for tall_part, wide_part in zip(own_mats[1::2], own_mats[::2]):
        if len(along) == 1 and wide_part.shape[0] % 16 == 0 and tall_part.shape[0] % 16 == 0:
            runs = along[0][2]
            part = jnp.concatenate(collect(jnp.concatenate([wide_part, tall_part], 0), *along[0]), 0)
        else:
            runs = 1
            for stage in reversed(along):
                place = digit(*stage)
                wide_part = jnp.concatenate(in_order(collect(wide_part, *stage), place), 0)
                tall_part = jnp.concatenate(in_order(collect(tall_part, *stage), place), 0)
            part = jnp.concatenate([wide_part, tall_part], 0)
        found = [part]
        for stage in (cross + core if len(cross) == 1 else cross[::-1] + core):
            rounds = [collect(part, *stage) for part in found]
            found = [rounds[j][k] for k in range(stage[2]) for j in range(len(rounds))]
        pieces.insert(0, found)
    fill = -width % 8
    dense_pieces = [jnp.pad(own_dense, ((0, fill), (0, 0)))]
    for stage in cross[::-1]:
        rounds = [collect(part, *stage) for part in dense_pieces]
        dense_pieces = [rounds[j][k] for k in range(stage[2]) for j in range(len(rounds))]

    square_total, error_total, weight_total = scalars[0, 0], scalars[0, 1], scalars[0, 2]
    grad_norm = jnp.sqrt(square_total) / weight_total
    factor = jnp.minimum(1.0, clip_level / grad_norm) / weight_total
    steps_done = step_count[0].astype(f32)
    corrections = [1.0 - jnp.power(beta, steps_done) for beta in (beta_first, beta_second)]
    place = (dp_index % 2) * sections + section
    index = jnp.stack([dp_index, place, dp_index // 2 if runs > 1 else 0, section]).astype(jnp.int32)
    (
        dense_new, dense_m_new, dense_v_new, dense_ema_new,
        vectors_new, vectors_m_new, vectors_v_new, vectors_ema_new,
    ) = adam(
        index, jnp.stack([factor, *corrections]), dense_pieces,
        (dense, dense_m, dense_v, dense_ema), (vectors, vectors_m, vectors_v, vectors_ema),
    )

    new, arrived = None, [None] * LAYERS
    for layer in reversed(range(LAYERS)):
        new, step = shampoo(
            layer, pieces[layer], runs, index, factor.reshape(1), (stat_small, stat_qkv, stat_wide), around,
            (root_small, root_qkv, root_wide), (w_out, w_fc2), (ema_out, ema_fc2), new,
        )
        step = step.reshape(parts, width, -1)
        sent = [
            lax.dynamic_index_in_dim(step, jnp.bitwise_xor(dp_index, k), 0, False) for k in range(parts)
        ]
        arrived[layer] = jnp.stack([swap(part, "dp", k) if k else part for k, part in enumerate(sent)])
    stat_small_new, stat_qkv_new, stat_wide_new, out_new, fc2_new, ema_out_new, ema_fc2_new = new
    qkv_new, fc1_new, ema_qkv_new, ema_fc1_new = finish(
        parts, index, factor.reshape(1), arrived, (w_qkv, w_fc1), (ema_qkv, ema_fc1)
    )
    return (
        error_total / weight_total,
        grad_norm,
        dense_new,
        dense_m_new,
        dense_v_new,
        dense_ema_new,
        vectors_new,
        vectors_m_new,
        vectors_v_new,
        vectors_ema_new,
        qkv_new,
        out_new,
        fc1_new,
        fc2_new,
        ema_qkv_new,
        ema_out_new,
        ema_fc1_new,
        ema_fc2_new,
        stat_small_new,
        stat_qkv_new,
        stat_wide_new,
    )


def solution(mesh):
    items = P("dp", None, None)
    columns = P(None, "dp")
    matrix = P(None, "dp", None)
    stacked = P(None, None, "dp", None)
    return jax.shard_map(
        per_device,
        mesh=mesh,
        in_specs=(
            (items, items, P("dp"), P())
            + (columns,) * 8
            + (matrix,) * 8
            + (stacked, matrix, stacked) * 2
        ),
        out_specs=(P(), P()) + (columns,) * 8 + (matrix,) * 8 + (stacked, matrix, stacked),
        check_vma=False,
    )
```

```python
import functools
import math

import jax
import jax.numpy as jnp
import numpy as np
from jax import lax
from jax.experimental import pallas as pl
from jax.experimental.pallas import tpu as pltpu
from jax.sharding import PartitionSpec as P

D = 384
HEADS = 6
HDIM = 64
SURF = 4
LEVELS = 13
VARS = 69
PIX = 4
VP = 276
LAT_ROWS = 64
LON_COLS = 16
SEQ = 1024
LAYERS = 2
FF = 1536
BLOCKS = 4 + 2 * (FF // D)

LANES = 128
PAIRS = HEADS // 2
EXT = (PIX + 1) * LANES
TABLE = VARS * (PIX + 1)

AT_PROJ = SEQ
AT_HEAD = AT_PROJ + D
AT_TABLE = AT_HEAD + 3 * LANES
AT_VECTOR = AT_TABLE + EXT
SLOTS = AT_VECTOR + LANES

highest = lax.Precision.HIGHEST
f32 = jnp.float32
bf16 = jnp.bfloat16
norm_eps = 1e-05
clip_level = 0.001
rate_dense = 0.05
rate_vector = 0.2
rate_matrix = 0.5
beta_first = 0.9
beta_second = 0.95
adam_eps = 1e-08
weight_decay = 0.1
stat_beta = 0.95
ema_beta = 0.9
LOG2E = math.log2(math.e)
SCALE2 = LOG2E * HDIM ** (-0.5)

NN = (((1,), (0,)), ((), ()))
NT = (((1,), (1,)), ((), ()))
TN = (((0,), (0,)), ((), ()))


def dot(left, right, dims=NN):
    return lax.dot_general(left, right, dims, preferred_element_type=f32)


def halves(value):
    high = value.astype(bf16)
    return high, (value - high.astype(f32)).astype(bf16)


def call(body, out_shape, scratch=(), vmem=60 << 20, flops=0, traffic=0):
    return pl.pallas_call(
        body,
        out_shape=out_shape,
        scratch_shapes=list(scratch),
        compiler_params=pltpu.CompilerParams(vmem_limit_bytes=vmem),
        cost_estimate=pl.CostEstimate(flops=flops, bytes_accessed=traffic, transcendentals=0),
    )


def shape(dims, kind=f32):
    return jax.ShapeDtypeStruct(dims, kind)


def norm_parts(values):
    center = values - jnp.mean(values, -1, keepdims=True)
    spread = jnp.mean(center * center, -1, keepdims=True)
    inverse = lax.rsqrt(spread + norm_eps)
    return center * inverse, inverse


def norm_back(values, gain, upstream):
    unit, inverse = norm_parts(values)
    scaled = upstream * gain
    back = inverse * (
        scaled
        - jnp.mean(scaled, -1, keepdims=True)
        - unit * jnp.mean(scaled * unit, -1, keepdims=True)
    )
    return back, jnp.sum(upstream * unit, 0, keepdims=True)


def tiles(count, body):
    def step(index, carry):
        body(index)
        return carry

    lax.fori_loop(0, count, step, 0)


def rows_of(index, size):
    return pl.ds(pl.multiple_of(index * size, size), size)


def head_mask(rows, which):
    lane = lax.broadcasted_iota(jnp.int32, (rows, LANES), 1)
    return (lane >= which * HDIM) & (lane < (which + 1) * HDIM)


def spread_fields(field_rows):
    row = lax.broadcasted_iota(jnp.int32, (VP, PIX * LANES), 0)
    col = lax.broadcasted_iota(jnp.int32, (VP, PIX * LANES), 1)
    var, pixel = col % LANES, col // LANES
    chosen = (row == PIX * var + pixel) & (var < VARS)
    return dot(field_rows, jnp.where(chosen, 1.0, 0.0).astype(bf16))


def query_mask(query_row):
    head = lax.broadcasted_iota(jnp.int32, (8, D), 0)
    lane = lax.broadcasted_iota(jnp.int32, (8, D), 1)
    return jnp.where(lane // HDIM == head, query_row * HDIM ** (-0.5), 0.0)


def query_scores(table_ref, mask, query_scr):
    for j in range(PIX + 1):
        part = table_ref[j * LANES : (j + 1) * LANES, :]
        query_scr[j * 8 : (j + 1) * 8, :] = dot(mask.astype(bf16), part, NT)


def mix_weights(extended, query_scr, head, valid):
    score = query_scr[pl.ds(PIX * 8 + head, 1), :]
    for j in range(PIX):
        score = score + extended[j] * query_scr[pl.ds(j * 8 + head, 1), :]
    score = jnp.where(valid > 0, score, jnp.where(valid < 0, -jnp.inf, -1e9))
    peak = jnp.max(score, -1, keepdims=True)
    weight = jnp.exp(score - peak)
    return weight / jnp.sum(weight, -1, keepdims=True)


def embed_body(field_ref, table_ref, query_ref, valid_ref, proj_ref, pos_ref, out_ref, agg_ref, query_scr):
    size = 256
    query_scores(table_ref, query_mask(query_ref[...]), query_scr)

    def tile(index):
        rows = rows_of(index, size)
        wide = spread_fields(field_ref[rows, :])
        extended = [wide[:, j * LANES : (j + 1) * LANES] for j in range(PIX)]
        valid = valid_ref[...]

        def pair(hp, carry):
            lanes = rows_of(hp, LANES)
            table = table_ref[:, lanes]
            total = jnp.zeros((size, LANES), f32)
            for which in range(2):
                weight = mix_weights(extended, query_scr, 2 * hp + which, valid)
                mixing = jnp.concatenate([weight * extended[j] for j in range(PIX)] + [weight], 1)
                own = jnp.where(head_mask(EXT, which), table, jnp.zeros_like(table))
                high, low = halves(mixing)
                total = total + dot(high, own) + dot(low, own)
            agg_ref[rows, lanes] = total.astype(bf16)
            return carry

        lax.fori_loop(0, PAIRS, pair, 0)
        out_ref[rows, :] = (dot(agg_ref[rows, :], proj_ref[...]) + pos_ref[rows, :].astype(f32)).astype(bf16)

    tiles(SEQ // size, tile)


def embed_forward(field_rows, table, query_row, valid, proj, position):
    return call(
        embed_body,
        (shape((SEQ, D), bf16), shape((SEQ, D), bf16)),
        [pltpu.VMEM((40, LANES), f32)],
        flops=4_000_000_000,
        traffic=4_000_000,
    )(field_rows, table, query_row, valid, proj, position)


def embed_back_body(
    field_ref, table_ref, query_ref, valid_ref, proj_ref, agg_ref, grad_ref, dhead_ref, dvector_ref,
    out_ref, vector_scr, query_scr, wide_scr, merged_scr, high_scr, low_scr, dscore_scr,
):
    size = 256
    mask = query_mask(query_ref[...])
    query_scores(table_ref, mask, query_scr)
    out_ref[:, AT_PROJ : AT_PROJ + D] = dot(grad_ref[...], agg_ref[...], TN)
    out_ref[:, AT_HEAD:AT_TABLE] = jnp.zeros((D, AT_TABLE - AT_HEAD), f32)
    out_ref[:, AT_HEAD : AT_HEAD + VP] = dhead_ref[...]
    dscore_scr[...] = jnp.zeros_like(dscore_scr)

    def prepare(index):
        rows = rows_of(index, size)
        wide_scr[rows, :] = spread_fields(field_ref[rows, :])
        merged_scr[rows, :] = dot(grad_ref[rows, :], proj_ref[...], NT)
        out_ref[:, rows] = grad_ref[rows, :].astype(f32).T

    tiles(SEQ // size, prepare)

    def pair(hp):
        lanes = rows_of(hp, LANES)
        table = table_ref[:, lanes]
        total = jnp.zeros((LANES, EXT), f32)
        for which in range(2):
            head = 2 * hp + which
            own = jnp.where(head_mask(EXT, which), table, jnp.zeros_like(table))
            twice = jnp.concatenate([own, own], 1)

            def tile(index):
                rows = rows_of(index, size)
                extended = [wide_scr[rows, j * LANES : (j + 1) * LANES] for j in range(PIX)]
                weight = mix_weights(extended, query_scr, head, valid_ref[...])
                mixing = jnp.concatenate([weight * extended[j] for j in range(PIX)] + [weight], 1)
                high, low = halves(mixing)
                high_scr[rows, :] = high
                low_scr[rows, :] = low
                grad_high, grad_low = halves(merged_scr[rows, lanes])
                dmix = dot(jnp.concatenate([grad_high, grad_low], 1), twice, NT)
                dweight = dmix[:, PIX * LANES :]
                for j in range(PIX):
                    dweight = dweight + dmix[:, j * LANES : (j + 1) * LANES] * extended[j]
                dscore = weight * (dweight - jnp.sum(weight * dweight, -1, keepdims=True))
                for j in range(PIX + 1):
                    piece = dscore * extended[j] if j < PIX else dscore
                    at = pl.ds(j * 8 + head, 1)
                    dscore_scr[at, :] = dscore_scr[at, :] + jnp.sum(piece, 0, keepdims=True)

            tiles(SEQ // size, tile)
            grad_high, grad_low = halves(merged_scr[:, lanes])
            keep = head_mask(SEQ, which)
            grad_high = jnp.where(keep, grad_high, jnp.zeros_like(grad_high))
            grad_low = jnp.where(keep, grad_low, jnp.zeros_like(grad_low))
            both = dot(jnp.concatenate([grad_high, grad_low], 1), high_scr[...], TN)
            total = total + both[:LANES, :] + both[LANES:, :] + dot(grad_high, low_scr[...], TN)
        out_ref[lanes, AT_TABLE:AT_VECTOR] = total

    tiles(PAIRS, pair)
    dquery = jnp.zeros((1, D), f32)
    head = lax.broadcasted_iota(jnp.int32, (8, D), 0)
    lane = lax.broadcasted_iota(jnp.int32, (8, D), 1)
    for j in range(PIX + 1):
        part = dscore_scr[j * 8 : (j + 1) * 8, :]
        block = slice(j * LANES, (j + 1) * LANES)
        lanes = slice(AT_TABLE + j * LANES, AT_TABLE + (j + 1) * LANES)
        out_ref[:, lanes] = out_ref[:, lanes] + lax.dot_general(
            mask, part, TN, precision=highest, preferred_element_type=f32
        )
        spread = lax.dot_general(
            part, table_ref[block, :].astype(f32), NN, precision=highest, preferred_element_type=f32
        )
        dquery = dquery + jnp.sum(jnp.where(lane // HDIM == head, spread, 0.0), 0, keepdims=True)
    vector_scr[...] = jnp.zeros_like(vector_scr)
    vector_scr[0:8, :] = dvector_ref[...]
    vector_scr[0:1, :] = dquery * HDIM ** (-0.5)
    out_ref[:, AT_VECTOR:SLOTS] = vector_scr[...].T


def embed_back(field_rows, table, query_row, valid, proj, agg, grad, dhead, dvector):
    return call(
        embed_back_body,
        shape((D, SLOTS)),
        [
            pltpu.VMEM((LANES, D), f32),
            pltpu.VMEM((40, LANES), f32),
            pltpu.VMEM((SEQ, PIX * LANES), f32),
            pltpu.VMEM((SEQ, D), f32),
            pltpu.VMEM((SEQ, EXT), bf16),
            pltpu.VMEM((SEQ, EXT), bf16),
            pltpu.VMEM((40, LANES), f32),
        ],
        flops=12_000_000_000,
        traffic=6_000_000,
    )(field_rows, table, query_row, valid, proj, agg, grad, dhead, dvector)


def square(ref, index):
    return ref[index * D : (index + 1) * D, :]


def block_body(x_ref, gain_ref, w_ref,
               h_ref, qkv_ref, o_ref, lse_ref, m_ref, h2_ref, y_ref):
    size = 256

    def enter(index):
        rows = rows_of(index, size)
        unit, unused = norm_parts(x_ref[rows, :].astype(f32))
        hidden = (unit * gain_ref[0:1, :]).astype(bf16)
        h_ref[rows, :] = hidden
        for b in range(3):
            qkv_ref[rows, b * D : (b + 1) * D] = dot(hidden, square(w_ref, b)).astype(bf16)

    tiles(SEQ // size, enter)
    lse_ref[...] = jnp.zeros_like(lse_ref)

    def pair(hp):
        keys = qkv_ref[:, pl.ds(pl.multiple_of(D + hp * LANES, LANES), LANES)]
        values = qkv_ref[:, pl.ds(pl.multiple_of(2 * D + hp * LANES, LANES), LANES)]

        def tile(index):
            rows = rows_of(index, size)
            queries = qkv_ref[rows, rows_of(hp, LANES)]
            parts = []
            for which in range(2):
                own = jnp.where(head_mask(size, which), queries, jnp.zeros_like(queries))
                score = dot(keys, own, NT) * SCALE2
                peak = jnp.max(score, 0, keepdims=True)
                power = jnp.exp2(score - peak)
                total = jnp.sum(power, 0, keepdims=True)
                chance = (power * (1.0 / total)).astype(bf16)
                mixed = dot(values, chance, TN)
                parts.append(mixed[which * HDIM : (which + 1) * HDIM, :])
                lse_ref[pl.ds(2 * hp + which, 1), rows] = peak + jnp.log2(total)
            o_ref[rows, rows_of(hp, LANES)] = jnp.concatenate(parts, 0).T.astype(bf16)

        tiles(SEQ // size, tile)

    tiles(PAIRS, pair)

    def leave(index):
        rows = rows_of(index, size)
        middle = x_ref[rows, :].astype(f32) + dot(o_ref[rows, :], square(w_ref, 3))
        m_ref[rows, :] = middle
        unit, unused = norm_parts(middle)
        hidden = (unit * gain_ref[1:2, :]).astype(bf16)
        h2_ref[rows, :] = hidden
        total = jnp.zeros((size, D), f32)
        for b in range(FF // D):
            before = dot(hidden, square(w_ref, 4 + b))
            active = (0.5 * before * (1.0 + lax.erf(before * math.sqrt(0.5)))).astype(bf16)
            total = total + dot(active, square(w_ref, 8 + b))
        y_ref[rows, :] = (middle + total).astype(bf16)

    tiles(SEQ // size, leave)


def block_forward(x, gains, weights):
    return call(
        block_body,
        (
            shape((SEQ, D), bf16),
            shape((SEQ, 3 * D), bf16),
            shape((SEQ, D), bf16),
            shape((8, SEQ)),
            shape((SEQ, D)),
            shape((SEQ, D), bf16),
            shape((SEQ, D), bf16),
        ),
        flops=12_000_000_000,
        traffic=12_000_000,
    )(x, gains, weights)


def feed_back_body(h2_ref, m_ref, dy_ref, gain_ref, w_ref, dm_ref, do_ref, dgain_ref, dw_ref, r_scr, df_scr):
    size = 256
    dgain_ref[...] = jnp.zeros_like(dgain_ref)

    def first(index):
        rows = rows_of(index, size)
        grad_next = dy_ref[rows, :]
        hidden = h2_ref[rows, :]
        upstream = jnp.zeros((size, D), f32)
        for b in range(FF // D):
            cols = slice(b * D, (b + 1) * D)
            before = dot(hidden, square(w_ref, 4 + b))
            upper = 0.5 * (1.0 + lax.erf(before * math.sqrt(0.5)))
            r_scr[rows, cols] = (before * upper).astype(bf16)
            slope = upper + before * (jnp.exp2(before * before * (-0.5 * LOG2E)) * (1.0 / math.sqrt(2 * math.pi)))
            grad_before = (dot(grad_next, square(w_ref, 8 + b), NT) * slope).astype(bf16)
            df_scr[rows, cols] = grad_before
            upstream = upstream + dot(grad_before, square(w_ref, 4 + b), NT)
        back, dgain = norm_back(m_ref[rows, :], gain_ref[1:2, :], upstream)
        dgain_ref[...] = dgain_ref[...] + dgain
        middle = grad_next.astype(f32) + back
        dm_ref[rows, :] = middle
        do_ref[rows, :] = dot(middle.astype(bf16), square(w_ref, 3), NT).astype(bf16)

    tiles(SEQ // size, first)

    def wide(index):
        cols = rows_of(index, D)
        dw_ref[rows_of(index, D), :] = dot(h2_ref[...], df_scr[:, cols], TN)
        dw_ref[rows_of(FF // D + index, D), :] = dot(r_scr[:, cols], dy_ref[...], TN)

    tiles(FF // D, wide)


def feed_back(h2, m, dy, gains, weights):
    return call(
        feed_back_body,
        (shape((SEQ, D)), shape((SEQ, D), bf16), shape((1, D)), shape((2 * FF, D))),
        [pltpu.VMEM((SEQ, FF), bf16), pltpu.VMEM((SEQ, FF), bf16)],
        flops=17_000_000_000,
        traffic=14_000_000,
    )(h2, m, dy, gains, weights)


def mix_back_body(x_ref, h_ref, qkv_ref, o_ref, lse_ref, dm_ref, do_ref, gain_ref, w_ref,
                  dx_ref, dgain_ref, dw_ref, dqkv_scr, dkv_scr):
    size = 256
    dgain_ref[...] = jnp.zeros_like(dgain_ref)
    dw_ref[3 * D : 4 * D, :] = dot(o_ref[...], dm_ref[...].astype(bf16), TN)

    def pair(hp):
        lanes = rows_of(hp, LANES)
        klanes = pl.ds(pl.multiple_of(D + hp * LANES, LANES), LANES)
        vlanes = pl.ds(pl.multiple_of(2 * D + hp * LANES, LANES), LANES)
        keys = qkv_ref[:, klanes]
        values = qkv_ref[:, vlanes]
        dkv_scr[...] = jnp.zeros_like(dkv_scr)

        def tile(index):
            rows = rows_of(index, size)
            queries = qkv_ref[rows, lanes]
            upstream = do_ref[rows, lanes]
            parts = []
            for which in range(2):
                keep = head_mask(size, which)
                own = jnp.where(keep, queries, jnp.zeros_like(queries))
                own_up = jnp.where(keep, upstream, jnp.zeros_like(upstream))
                score = dot(keys, own, NT) * SCALE2
                chance = jnp.exp2(score - lse_ref[pl.ds(2 * hp + which, 1), rows])
                dchance = dot(values, own_up, NT)
                shift = jnp.sum(dchance * chance, 0, keepdims=True)
                dscore = (chance * (dchance - shift)).astype(bf16)
                dkv_scr[:, :LANES] = dkv_scr[:, :LANES] + dot(dscore, own)
                dkv_scr[:, LANES:] = dkv_scr[:, LANES:] + dot(chance.astype(bf16), own_up)
                dquery = dot(keys, dscore, TN)
                parts.append(dquery[which * HDIM : (which + 1) * HDIM, :])
            dqkv_scr[rows, lanes] = (jnp.concatenate(parts, 0).T * HDIM ** (-0.5)).astype(bf16)

        tiles(SEQ // size, tile)
        dqkv_scr[:, klanes] = (dkv_scr[:, :LANES] * HDIM ** (-0.5)).astype(bf16)
        dqkv_scr[:, vlanes] = dkv_scr[:, LANES:].astype(bf16)

    tiles(PAIRS, pair)

    def third(index):
        cols = rows_of(index, D)
        dw_ref[cols, :] = dot(h_ref[...], dqkv_scr[:, cols], TN)

    tiles(3, third)

    def last(index):
        rows = rows_of(index, size)
        upstream = jnp.zeros((size, D), f32)
        for b in range(3):
            upstream = upstream + dot(dqkv_scr[rows, b * D : (b + 1) * D], square(w_ref, b), NT)
        back, dgain = norm_back(x_ref[rows, :].astype(f32), gain_ref[0:1, :], upstream)
        dgain_ref[...] = dgain_ref[...] + dgain
        dx_ref[rows, :] = (dm_ref[rows, :] + back).astype(bf16)

    tiles(SEQ // size, last)


def mix_back(x, kept, dm, do, gains, weights):
    return call(
        mix_back_body,
        (shape((SEQ, D), bf16), shape((1, D)), shape((4 * D, D))),
        [pltpu.VMEM((SEQ, 3 * D), bf16), pltpu.VMEM((SEQ, 2 * LANES), f32)],
        flops=17_000_000_000,
        traffic=14_000_000,
    )(x, *kept, dm, do, gains, weights)


def head_body(y_ref, gain_ref, head_ref, target_ref, cos_ref, valid_ref,
              dy_ref, dhead_ref, dgain_ref, error_ref, h_scr, dp_scr):
    size = 256
    dgain_ref[...] = jnp.zeros_like(dgain_ref)
    error_ref[...] = jnp.zeros_like(error_ref)

    def tile(index):
        rows = rows_of(index, size)
        values = y_ref[rows, :].astype(f32)
        unit, unused = norm_parts(values)
        hidden = (unit * gain_ref[...]).astype(bf16)
        h_scr[rows, :] = hidden
        residual = dot(hidden, head_ref[...], NT) - target_ref[rows, :].astype(f32)
        lane = lax.broadcasted_iota(jnp.int32, (size, VP), 1)
        cosine = jnp.where(lane % PIX < 2, cos_ref[rows, 0:1], cos_ref[rows, 1:2])
        weight = cosine * valid_ref[...]
        error_ref[...] = error_ref[...] + jnp.sum(weight * residual * residual, 0, keepdims=True)
        grad = (2.0 * weight * residual).astype(bf16)
        dp_scr[rows, :] = grad
        back, dgain = norm_back(values, gain_ref[...], dot(grad, head_ref[...]))
        dgain_ref[...] = dgain_ref[...] + dgain
        dy_ref[rows, :] = back.astype(bf16)

    tiles(SEQ // size, tile)
    dhead_ref[...] = dot(h_scr[...], dp_scr[...], TN)


def head_step(y, gain, head_rows, target, cosines, valid):
    return call(
        head_body,
        (shape((SEQ, D), bf16), shape((D, VP)), shape((1, D)), shape((1, VP))),
        [pltpu.VMEM((SEQ, D), bf16), pltpu.VMEM((SEQ, VP), bf16)],
        flops=700_000_000,
        traffic=4_000_000,
    )(y, gain, head_rows, target, cosines, valid)


def dot3(left, right, dims=NN):
    return dot(left[0], right[0], dims) + dot(left[0], right[1], dims) + dot(left[1], right[0], dims)


def chosen_rows(count, width, start, offset):
    row = lax.broadcasted_iota(jnp.int32, (count, width), 0)
    col = lax.broadcasted_iota(jnp.int32, (count, width), 1)
    return jnp.where(col + offset == row + start, 1.0, 0.0).astype(bf16)


def pick(selector, pair, dims=NN):
    return [dot(selector, part, dims).astype(bf16) for part in pair]


def shampoo_body(pieces, along, index_ref, factor_ref, small_ref, qkv_ref, wide_ref, around_ref,
                 left_out_ref, left_fc2_ref, right_qkv_ref, right_fc1_ref,
                 wout_ref, wfc2_ref, eout_ref, efc2_ref, *rest):
    piece_refs, rest = rest[:-17], rest[-10:]
    (nsmall_ref, nqkv_ref, nwide_ref, nout_ref, nfc2_ref, meout_ref, mefc2_ref,
     step_ref, high_scr, low_scr) = rest
    me = index_ref[0]
    factor = factor_ref[0]
    if len(piece_refs) == 1:
        piece_refs = [piece_refs[0].at[k] for k in range(pieces)]
    wide_rows, tall_rows = 2 * FF // (pieces * along), 4 * D // (pieces * along)
    for k in range(pieces):
        block = jnp.bitwise_xor(index_ref[1], k) * along
        for j in range(along):
            place = block + jnp.bitwise_xor(index_ref[2], j)
            at = j * (wide_rows + tall_rows)
            high, low = halves(piece_refs[k][at : at + wide_rows, :])
            rows = pl.ds(pl.multiple_of(4 * D + place * wide_rows, 16), wide_rows)
            high_scr[rows, :] = high
            low_scr[rows, :] = low
            high, low = halves(piece_refs[k][at + wide_rows : at + wide_rows + tall_rows, :])
            rows = pl.ds(pl.multiple_of(place * tall_rows, 16), tall_rows)
            high_scr[rows, :] = high
            low_scr[rows, :] = low

    def grad(b):
        return square(high_scr, b), square(low_scr, b)

    def mixed(old, product):
        return stat_beta * old + (1.0 - stat_beta) * (factor * (factor * product))

    def root(k):
        return halves(around_ref[0, k])

    rows = small_ref.shape[2]
    own_row = chosen_rows(rows, D, me * rows, 0)
    place = 0
    for first, count, left, right_ref, nright_ref, right_root_ref, left_root in (
        (0, 3, 0, qkv_ref, nqkv_ref, right_qkv_ref, 0),
        (4, FF // D, 3, wide_ref, nwide_ref, right_fc1_ref, 2),
    ):
        take = (0, 0) if first else (0,)
        cols = right_ref.shape[-2]
        total = jnp.zeros((rows, D), f32)
        own_cols = [jnp.zeros((cols, D), f32)] * 2
        share = right_root_ref.shape[-2]
        reach = jnp.zeros((D, share), f32)
        for b in range(count):
            block = grad(first + b)
            total = total + dot3(pick(own_row, block), block, NT)
            selector = chosen_rows(cols, D, me * cols, b * D)
            own_cols = [own + dot(selector, part, NT) for own, part in zip(own_cols, block)]
            reach = reach + dot3(block, halves(right_root_ref[take + (slice(None), slice(b * D, (b + 1) * D))]), NT)
        nsmall_ref[0, left] = mixed(small_ref[0, left], total)
        own_cols = [own.astype(bf16) for own in own_cols]
        for b in range(count):
            lanes = slice(b * D, (b + 1) * D)
            nright_ref[take + (slice(None), lanes)] = mixed(
                right_ref[take + (slice(None), lanes)], dot3(own_cols, grad(first + b))
            )
        step_ref[:, place : place + share] = dot3(root(left_root), halves(reach))
        place = place + share

    block = grad(3)
    nsmall_ref[0, 1] = mixed(small_ref[0, 1], dot3(pick(own_row, block), block, NT))
    nsmall_ref[0, 2] = mixed(small_ref[0, 2], dot3(pick(own_row, block, NT), block))
    moved = dot3(halves(dot3(halves(left_out_ref[0, 0]), block)), root(1))
    updated = wout_ref[0] - rate_matrix * factor * moved
    nout_ref[0] = updated
    meout_ref[0] = average(eout_ref[0], updated)

    tall = wide_ref.shape[2]
    total = jnp.zeros((rows, D), f32)
    own = [jnp.zeros((tall, D), f32)] * 2
    reach = jnp.zeros((tall, D), f32)
    for b in range(FF // D):
        block = grad(8 + b)
        total = total + dot3(pick(own_row, block, NT), block)
        selector = chosen_rows(tall, D, me * tall, b * D)
        own = [o + dot(selector, part) for o, part in zip(own, block)]
        reach = reach + dot3(halves(left_fc2_ref[0, 0, :, b * D : (b + 1) * D]), block)
    nsmall_ref[0, 4] = mixed(small_ref[0, 4], total)
    own = [o.astype(bf16) for o in own]
    for b in range(FF // D):
        lanes = slice(b * D, (b + 1) * D)
        nwide_ref[0, 1, :, lanes] = mixed(wide_ref[0, 1, :, lanes], dot3(own, grad(8 + b), NT))
    updated = wfc2_ref[0] - rate_matrix * factor * dot3(halves(reach), root(3))
    nfc2_ref[0] = updated
    mefc2_ref[0] = average(efc2_ref[0], updated)


def layer_block(array, layer):
    return pl.BlockSpec(
        (1,) + array.shape[1:], lambda i: (layer,) + (0,) * (array.ndim - 1), pipeline_mode=pl.Buffered(1)
    )


def whole_block(array):
    return pl.BlockSpec(array.shape, lambda i: (0,) * array.ndim, pipeline_mode=pl.Buffered(1))


def shampoo(layer, pieces, along, index, factor, stats, around, roots, weights, averages, previous):
    small, qkv, wide = stats
    root_small, root_qkv, root_wide = roots
    scalar = pl.BlockSpec(memory_space=pltpu.SMEM)
    rows, tall = small.shape[2], wide.shape[2]
    root_out = pl.BlockSpec((1, 1, rows, D), lambda i: (layer, 1, 0, 0), pipeline_mode=pl.Buffered(1))
    root_fc2 = pl.BlockSpec((1, 1, tall, FF), lambda i: (layer, 1, 0, 0), pipeline_mode=pl.Buffered(1))
    layered = [small, qkv, wide, around]
    root_fc1 = pl.BlockSpec((1, 1, tall, FF), lambda i: (layer, 0, 0, 0), pipeline_mode=pl.Buffered(1))
    tails = [*weights, *averages]
    results = [small, qkv, wide, *weights, *averages]
    operands = [index, factor, *layered, root_small, root_wide, root_qkv, root_wide, *tails, *pieces]
    specs = [scalar, scalar] + [layer_block(x, layer) for x in layered] + [root_out, root_fc2, layer_block(root_qkv, layer), root_fc1]
    specs += [layer_block(x, layer) for x in tails] + [whole_block(x) for x in pieces]
    aliases = {}
    if previous is not None:
        aliases = {len(operands) + k: k for k in range(len(results))}
    else:
        previous = [jnp.zeros((8, LANES), f32)] * len(results)
    operands += previous
    specs += [pl.BlockSpec(memory_space=pl.ANY)] * len(results)
    width = root_qkv.shape[1] + tall
    *new, step = pl.pallas_call(
        functools.partial(shampoo_body, 8 if len(pieces) == 1 else len(pieces), along),
        grid=(1,),
        in_specs=specs,
        out_specs=[layer_block(x, layer) for x in results]
        + [pl.BlockSpec((D, width), lambda i: (0, 0), pipeline_mode=pl.Buffered(1))],
        out_shape=[shape(x.shape) for x in results] + [shape((D, width))],
        scratch_shapes=[pltpu.VMEM((BLOCKS * D, D), bf16)] * 2,
        input_output_aliases=aliases,
        compiler_params=pltpu.CompilerParams(vmem_limit_bytes=60 << 20),
        cost_estimate=pl.CostEstimate(flops=5_000_000_000, bytes_accessed=30_000_000, transcendentals=0),
    )(*operands)
    return new, step


def close_body(own1_ref, feed0_ref, mix0_ref, turned_ref, scalar_ref,
               out1_ref, out0_ref, outd_ref, outs_ref,
               own0_scr, feed_scr, mix_scr, mixz_scr, dense_scr, core_scr, cross_scr, along_scr,
               mix_sum, dense_sum, own_dense, own_scalar, send_sem, recv_sem, local_sem):
    s = lax.axis_index("section")
    dp = lax.axis_index("dp")
    z, c = dp // 2, dp % 2
    mine = c * 4 + s
    rows = own1_ref.shape[0]
    feed_rows, mix_rows = feed0_ref.shape[0] // 4, mix0_ref.shape[0] // 16
    width = turned_ref.shape[2]
    span = SLOTS // 4
    peers = [{"section": s, "dp": jnp.bitwise_xor(dp, 1)}]
    peers += [{"section": jnp.bitwise_xor(s, k), "dp": dp} for k in (1, 2, 3)]
    peers += [{"section": s, "dp": jnp.bitwise_xor(dp, 2 * k)} for k in (1, 2, 3)]
    barrier = pltpu.get_barrier_semaphore()
    for peer in peers:
        pl.semaphore_signal(barrier, inc=1, device_id=peer, device_id_type=pl.DeviceIdType.MESH)
    pl.semaphore_wait(barrier, len(peers))
    count = [0, 0]
    sent = []

    def send(source, target, peer):
        n = count[0]
        count[0] = n + 1
        copy = pltpu.make_async_remote_copy(
            src_ref=source, dst_ref=target, send_sem=send_sem.at[n], recv_sem=recv_sem.at[n],
            device_id=peer, device_id_type=pl.DeviceIdType.MESH,
        )
        copy.start()
        sent.append(copy)
        return copy

    def keep(source, target):
        n = count[1]
        count[1] = n + 1
        copy = pltpu.make_async_copy(source, target, local_sem.at[n])
        copy.start()
        return copy

    def arrive(copies):
        for copy in copies:
            copy.wait_recv()

    def across(k):
        return jnp.bitwise_xor(s, k)

    def up(k):
        return jnp.bitwise_xor(z, k)

    def at(index, size, align):
        return pl.ds(pl.multiple_of(index * size, align), size)

    core, (x, y, diagonal), tower = peers[0], peers[1:4], peers[4:]
    flat = (x, y, diagonal)

    def gather_up(own_ref, out_ref):
        place = out_ref.at[mine, at(z, rows, 16), :]
        local = keep(own_ref, place)
        return local, [send(own_ref, place, peer) for peer in tower]

    def gather_flat(out_ref, started):
        local, copies = started
        local.wait()
        arrive(copies)
        block = out_ref.at[mine]
        found = [send(block, block, x), send(block, block, y)]
        send_core = [send(block, block, core)]
        return found, send_core

    def gather_turn(out_ref, started):
        (from_x, from_y), to_core = started
        half = 2 * rows
        from_x.wait_recv()
        block_x = c * 4 + across(1)
        upper = out_ref.at[block_x, pl.ds(0, half), :]
        turn_y = send(upper, upper, y)
        to_core.append(send(out_ref.at[block_x], out_ref.at[block_x], core))
        from_y.wait_recv()
        block_y = c * 4 + across(2)
        lower = out_ref.at[block_y, pl.ds(half, half), :]
        turn_x = send(lower, lower, x)
        to_core.append(send(out_ref.at[block_y], out_ref.at[block_y], core))
        return [turn_y, turn_x], to_core

    def gather_core(out_ref, started):
        turned, to_core = started
        arrive(turned)
        block = out_ref.at[c * 4 + across(3)]
        return to_core + [send(block, block, core)]

    dense_core = send(turned_ref.at[:, 1 - c], core_scr, core)
    feed_up = [send(feed0_ref.at[at(up(k), feed_rows, 16), :], feed_scr.at[k - 1], tower[k - 1]) for k in (1, 2, 3)]
    mix_flat = [
        send(mix0_ref.at[at(across(k), 4 * mix_rows, 16), :], mix_scr.at[k - 1], flat[k - 1]) for k in (1, 2, 3)
    ]
    up1 = gather_up(own1_ref, out1_ref)

    dense_core.wait_recv()

    def add_core(k):
        dense_sum[k] = turned_ref[k, c] + core_scr[k]

    tiles(4, add_core)
    dense_flat = [
        send(dense_sum.at[:, :, at(across(k), span, LANES)], cross_scr.at[k - 1], flat[k - 1]) for k in (1, 2, 3)
    ]
    arrive(mix_flat)
    mix_sum[...] = mix0_ref[at(s, 4 * mix_rows, 16), :] + mix_scr[0] + mix_scr[1] + mix_scr[2]
    mix_up = [
        send(mix_sum.at[at(up(k), mix_rows, 16), :], mixz_scr.at[k - 1], tower[k - 1]) for k in (1, 2, 3)
    ]
    arrive(feed_up)
    own0_scr[0:feed_rows, :] = feed0_ref[at(z, feed_rows, 16), :] + feed_scr[0] + feed_scr[1] + feed_scr[2]
    arrive(mix_up)
    own0_scr[feed_rows:rows, :] = mix_sum[at(z, mix_rows, 16), :] + mixz_scr[0] + mixz_scr[1] + mixz_scr[2]
    up0 = gather_up(own0_scr, out0_ref)
    flat1 = gather_flat(out1_ref, up1)
    arrive(dense_flat)

    def add_flat(k):
        mid = dense_sum[k, :, at(s, span, LANES)]
        dense_scr[k] = mid + cross_scr[0, k] + cross_scr[1, k] + cross_scr[2, k]

    tiles(4, add_flat)
    dense_up = [send(dense_scr.at[up(k)], along_scr.at[k - 1], tower[k - 1]) for k in (1, 2, 3)]
    flat0 = gather_flat(out0_ref, up0)
    turn1 = gather_turn(out1_ref, flat1)
    arrive(dense_up)
    own_dense[...] = dense_scr[z] + along_scr[0] + along_scr[1] + along_scr[2]
    home = outd_ref.at[s]
    local_dense = keep(own_dense, home)
    spread_dense = [send(own_dense, home, peer) for peer in flat]
    total = jnp.zeros((1, 1), f32)
    for part in (own1_ref[...], own0_scr[...], own_dense[...]):
        total = total + jnp.sum(jnp.sum(part * part, 0, keepdims=True), 1, keepdims=True)
    lane = lax.broadcasted_iota(jnp.int32, (8, LANES), 1)
    own_scalar[...] = jnp.where(lane == 0, total, scalar_ref[...])
    home = outs_ref.at[c, s, z]
    local_scalar = keep(own_scalar, home)
    scalar_up = [send(own_scalar, home, peer) for peer in tower]
    local_scalar.wait()
    arrive(scalar_up)
    home = outs_ref.at[c, s]
    scalar_flat = [send(home, home, peer) for peer in flat]
    turn0 = gather_turn(out0_ref, flat0)
    core1 = gather_core(out1_ref, turn1)
    arrive(scalar_flat)
    home = outs_ref.at[c]
    scalar_core = send(home, home, core)
    core0 = gather_core(out0_ref, turn0)
    local_dense.wait()
    arrive(spread_dense)
    arrive(core1)
    arrive(core0)
    scalar_core.wait_recv()
    for copy in sent:
        copy.wait_send()


def close_exchange(own1, feed0, mix0, turned, scalars):
    rows = own1.shape[0]
    feed_rows, mix_rows = feed0.shape[0] // 4, mix0.shape[0] // 16
    width, span = turned.shape[2], SLOTS // 4
    anywhere = pl.BlockSpec(memory_space=pl.ANY)
    copies = 48
    return pl.pallas_call(
        close_body,
        in_specs=[pl.BlockSpec(memory_space=pltpu.VMEM)] * 5,
        out_specs=[anywhere] * 4,
        out_shape=[
            shape((8, 4 * rows, D)), shape((8, 4 * rows, D)), shape((4, width, span)), shape((2, 4, 4, 8, LANES)),
        ],
        scratch_shapes=[
            pltpu.VMEM((rows, D), f32),
            pltpu.VMEM((3, feed_rows, D), f32),
            pltpu.VMEM((3, 4 * mix_rows, D), f32),
            pltpu.VMEM((3, mix_rows, D), f32),
            pltpu.VMEM((4, width, span), f32),
            pltpu.VMEM((4, width, SLOTS), f32),
            pltpu.VMEM((3, 4, width, span), f32),
            pltpu.VMEM((3, width, span), f32),
            pltpu.VMEM((4 * mix_rows, D), f32),
            pltpu.VMEM((4, width, SLOTS), f32),
            pltpu.VMEM((width, span), f32),
            pltpu.VMEM((8, LANES), f32),
            pltpu.SemaphoreType.DMA((copies,)),
            pltpu.SemaphoreType.DMA((copies,)),
            pltpu.SemaphoreType.DMA((4,)),
        ],
        compiler_params=pltpu.CompilerParams(
            vmem_limit_bytes=60 << 20, collective_id=0, has_side_effects=True
        ),
        cost_estimate=pl.CostEstimate(flops=10_000_000, bytes_accessed=300_000_000, transcendentals=0),
    )(own1, feed0, mix0, turned, scalars)


def finish_body(parts, index_ref, factor_ref, *refs):
    found, refs = refs[:LAYERS], refs[LAYERS:]
    (wqkv_ref, wfc1_ref, eqkv_ref, efc1_ref, nqkv_ref, nfc1_ref, mqkv_ref, mfc1_ref) = refs
    scale = rate_matrix * factor_ref[0]
    for layer in range(LAYERS):
        place = 0
        for w_ref, e_ref, n_ref, a_ref in (
            (wqkv_ref, eqkv_ref, nqkv_ref, mqkv_ref), (wfc1_ref, efc1_ref, nfc1_ref, mfc1_ref)
        ):
            share = w_ref.shape[2] // parts
            for j in range(parts):
                which = jnp.bitwise_xor(index_ref[0], j)
                lanes = slice(j * share, (j + 1) * share)
                step = found[layer][which, :, place : place + share]
                updated = w_ref[layer, :, lanes] - scale * step
                n_ref[layer, :, lanes] = updated
                a_ref[layer, :, lanes] = average(e_ref[layer, :, lanes], updated)
            place = place + share


def finish(parts, index, factor, found, weights, averages):
    scalar = pl.BlockSpec(memory_space=pltpu.SMEM)
    operands = [*found, *weights, *averages]
    return pl.pallas_call(
        functools.partial(finish_body, parts),
        in_specs=[scalar, scalar] + [pl.BlockSpec(memory_space=pltpu.VMEM)] * len(operands),
        out_shape=[shape(x.shape) for x in (*weights, *averages)],
        compiler_params=pltpu.CompilerParams(vmem_limit_bytes=40 << 20),
        cost_estimate=pl.CostEstimate(flops=10_000_000, bytes_accessed=6_000_000, transcendentals=0),
    )(index, factor, *operands)


def adam_body(index_ref, scalar_ref, *refs):
    pieces, refs = refs[0], refs[1:]
    dense, vectors, new_dense, new_vectors, turned_scr = refs[:4], refs[4:8], refs[8:12], refs[12:16], refs[16]
    width = dense[0].shape[1]
    span = pieces.shape[2]
    for k in range(pieces.shape[0]):
        place = jnp.bitwise_xor(index_ref[3], k)
        turned_scr[pl.ds(pl.multiple_of(place * span, LANES), span), :] = pieces[k].T

    def update(refs, news, target, source, count, rate, decay):
        old = [ref[target, :] for ref in refs]
        gradient = turned_scr[source : source + count, :][:, :width] * scalar_ref[0]
        first = beta_first * old[1] + (1.0 - beta_first) * gradient
        second = beta_second * old[2] + (1.0 - beta_second) * gradient * gradient
        first_hat = first / scalar_ref[1]
        second_hat = second / scalar_ref[2]
        updated = old[0] - rate * (first_hat / (jnp.sqrt(second_hat) + adam_eps) + decay * old[0])
        for ref, value in zip(news, (updated, first, second, average(old[3], updated))):
            ref[target, :] = value

    args = (dense, new_dense)
    for j in range(PIX + 1):
        update(*args, pl.ds(j, VARS, PIX + 1), AT_TABLE + j * LANES, VARS, rate_dense, weight_decay)
    update(*args, slice(TABLE, TABLE + SEQ + D), 0, SEQ + D, rate_dense, weight_decay)
    update(*args, slice(TABLE + SEQ + D, TABLE + SEQ + D + VP), AT_HEAD, VP, rate_dense, weight_decay)
    update(vectors, new_vectors, slice(0, 2 * LAYERS + 2), AT_VECTOR, 2 * LAYERS + 2, rate_vector, 0.0)


def adam(index, scalars, pieces, dense, vectors):
    scalar = pl.BlockSpec(memory_space=pltpu.SMEM)
    operands = [pieces, *dense, *vectors]
    return pl.pallas_call(
        adam_body,
        in_specs=[scalar, scalar] + [pl.BlockSpec(memory_space=pltpu.VMEM)] * len(operands),
        out_shape=[shape(x.shape) for x in (*dense, *vectors)],
        scratch_shapes=[pltpu.VMEM((SLOTS, pieces.shape[1]), f32)],
        compiler_params=pltpu.CompilerParams(vmem_limit_bytes=40 << 20),
        cost_estimate=pl.CostEstimate(flops=10_000_000, bytes_accessed=8_000_000, transcendentals=0),
    )(index, scalars, *operands)


def digits(count, start=1):
    found = []
    while start < count:
        radix = min(4, count // start)
        found.append((start, radix))
        start *= radix
    return found


def swap(values, axis, bits):
    return lax.ppermute(values, axis, [(k, k ^ bits) for k in range(lax.axis_size(axis))])


def digit(axis, bit, radix):
    return (lax.axis_index(axis) // bit) % radix


def share_out(values, dim, axis, bit, radix):
    size = values.shape[dim] // radix
    mine = digit(axis, bit, radix)

    def part(k):
        return lax.dynamic_slice_in_dim(values, jnp.bitwise_xor(mine, k) * size, size, dim)

    arrived = [swap(part(k), axis, k * bit) for k in range(1, radix)]
    total = part(0)
    for other in arrived:
        total = total + other
    return total


def collect(values, axis, bit, radix):
    return [values] + [swap(values, axis, k * bit) for k in range(1, radix)]


def in_order(found, place):
    low = 1
    while low < len(found):
        even = (place // low) % 2 == 0
        found = [jnp.where(even, found[k], found[k ^ low]) for k in range(len(found))]
        low *= 2
    return found


def gate(values, first):
    return lax.optimization_barrier((values, first))


def advance(values, sums):
    moved = [share_out(part, 0, *stages[0]) if stages else part for part, stages in sums]
    values, moved = gate(values, moved)
    return values, [[part, stages[1:]] for part, (unused, stages) in zip(moved, sums)]


def total_of(values, stages):
    for axis, bit, radix in stages:
        values = sum(in_order(collect(values, axis, bit, radix), digit(axis, bit, radix)))
    return values


def valid_flags(counts):
    var_index = jnp.arange(VARS)
    level_index = (var_index - SURF) % LEVELS
    inside = (var_index[None, :] < SURF) | (level_index[None, :] < counts[:, None])
    return jnp.where(inside, 1.0, 0.0).astype(f32)


def cosine_table():
    pixel_rows = 2 * LAT_ROWS
    latitude = (np.arange(pixel_rows) + 0.5) * (np.pi / pixel_rows) - 0.5 * np.pi
    cosine = np.cos(latitude)
    cosine = cosine / np.mean(cosine)
    by_row = cosine.reshape(LAT_ROWS, 2).repeat(LON_COLS, 0)
    return by_row.astype(np.float32), float(by_row.sum() * (PIX // 2))


def average(old_state, new_state):
    return ema_beta * old_state + (1.0 - ema_beta) * new_state


def column_blocks(part):
    rows, cols = part.shape
    return part.reshape(rows, cols // D, D).transpose(1, 0, 2).reshape(-1, D)


def pack_layer(parts):
    qkv, out, fc1, fc2 = [part.astype(bf16) for part in parts]
    return jnp.concatenate([column_blocks(qkv), out, column_blocks(fc1), fc2], 0)


def unpack_layer(full, rows):
    above = full[:, : rows * 8].reshape(-1, 8, rows, D).transpose(1, 0, 2, 3).reshape(8 * D, D)
    return jnp.concatenate([above, full[:, rows * 8 :].reshape(FF, D)], 0)


def per_device(
    fields, targets, level_count, step_count,
    dense, dense_m, dense_v, dense_ema, vectors, vectors_m, vectors_v, vectors_ema,
    w_qkv, w_out, w_fc1, w_fc2, ema_qkv, ema_out, ema_fc1, ema_fc2,
    stat_small, stat_qkv, stat_wide, root_small, root_qkv, root_wide,
):
    section = lax.axis_index("section")
    sections = lax.axis_size("section")
    dp_index = lax.axis_index("dp")
    parts = lax.axis_size("dp")
    rows_dense = dense.shape[0]
    both_rows = jnp.concatenate([dense, vectors], 0).astype(bf16)
    full_dense = lax.all_gather(both_rows, "dp", axis=1, tiled=True)
    gain_rows = full_dense[rows_dense:].astype(f32)
    layer_weights, before = [], full_dense
    for layer in range(LAYERS):
        packed = pack_layer([part[layer] for part in (w_qkv, w_out, w_fc1, w_fc2)])
        packed, before = gate(packed, before)
        if layer == 0:
            full_dense = before
        else:
            layer_weights[-1] = before
        before = lax.all_gather(packed, "dp", axis=0)
        layer_weights.append(before)
    near, layer_weights[-1] = gate(root_small, layer_weights[-1])
    around = lax.all_gather(near[:, np.array([0, 2, 3, 4])], "dp", axis=2, tiled=True)
    layer_weights = [unpack_layer(full, w_qkv.shape[1]) for full in layer_weights]
    micro_count = fields.shape[0]
    table = full_dense[:TABLE].reshape(VARS, PIX + 1, D).transpose(1, 0, 2)
    table = jnp.pad(table, ((0, 0), (0, LANES - VARS), (0, 0))).reshape(EXT, D)
    position = full_dense[TABLE : TABLE + SEQ]
    proj = full_dense[TABLE + SEQ : TABLE + SEQ + D]
    head_rows = full_dense[TABLE + SEQ + D : rows_dense]
    flags = valid_flags(level_count)
    by_row, row_total = cosine_table()
    weight_local = jnp.sum(flags) * row_total
    cosines = jnp.asarray(by_row)

    core = [("dp", 1, 2)]
    cross = [("section", bit, radix) for bit, radix in digits(sections)]
    along = [("dp", bit, radix) for bit, radix in digits(parts, 2)]
    turns = -(-micro_count // sections)
    turned, error_sum, d_mats = 0.0, 0.0, [0.0] * (2 * LAYERS)
    pending, ready = [], []
    for turn in range(turns):
        index = turn * sections + section
        active = jnp.where(index < micro_count, 1.0, 0.0).astype(f32)
        index = jnp.minimum(index, micro_count - 1)
        field_rows = lax.dynamic_index_in_dim(fields, index, 0, False)
        target = lax.dynamic_index_in_dim(targets, index, 0, False)
        flag_row = lax.dynamic_index_in_dim(flags, index, 0, True)
        valid_vars = jnp.pad(flag_row, ((0, 0), (0, LANES - VARS)), constant_values=-1.0)
        valid_values = jnp.repeat(flag_row * active, PIX, axis=1)
        x, agg = embed_forward(field_rows, table, gain_rows[0:1], valid_vars, proj, position)
        kept = []
        for layer in range(LAYERS):
            gains = gain_rows[1 + 2 * layer : 3 + 2 * layer]
            *saved, y = block_forward(x, gains, layer_weights[layer])
            kept.append((x, saved))
            x = y
        grad, d_head, d_final, errors = head_step(
            x, gain_rows[2 * LAYERS + 1 :], head_rows, target, cosines, valid_values
        )
        d_gains = [None] * (2 * LAYERS)
        for layer in reversed(range(LAYERS)):
            gains = gain_rows[1 + 2 * layer : 3 + 2 * layer]
            x, (h, qkv, o, lse, m, h2) = kept[layer]
            grad, pending = advance(grad, pending)
            pending, ready = pending + ready, []
            dm, do, d_gains[2 * layer + 1], found = feed_back(h2, m, grad, gains, layer_weights[layer])
            d_mats[2 * layer + 1] = d_mats[2 * layer + 1] + found if turn else found
            if turn == turns - 1:
                ready = [[d_mats[2 * layer + 1], core + cross + along]]
            do, pending = advance(do, pending)
            pending, ready = pending + ready, []
            grad, d_gains[2 * layer], found = mix_back(
                x, (h, qkv, o, lse), dm, do, gains, layer_weights[layer]
            )
            d_mats[2 * layer] = d_mats[2 * layer] + found if turn else found
            if turn == turns - 1:
                ready = [[d_mats[2 * layer], core + cross + along]]
        grad, pending = advance(grad, pending)
        pending, ready = pending + ready, []
        d_vectors = jnp.concatenate(
            [jnp.zeros((1, D), f32), *d_gains, d_final, jnp.zeros((6 - 2 * LAYERS, D), f32)], 0
        )
        found = embed_back(
            field_rows, table, gain_rows[0:1], valid_vars, proj, agg, grad, d_head, d_vectors
        )
        turned = turned + found if turn else found
        error_sum = error_sum + jnp.sum(errors)

    turned, pending = advance(turned, pending)
    width = D // parts
    scalars = jnp.stack([jnp.zeros((), f32), error_sum, jnp.where(section == 0, weight_local, 0.0)])
    scalars = jnp.broadcast_to(jnp.pad(scalars, (0, LANES - 3))[None], (8, LANES))
    if sections == 4 and parts == 8:
        feed1, mix1, feed0, mix0 = [part for part, unused in pending]
        whole1, whole0, dense_pieces, scalars = close_exchange(
            jnp.concatenate([feed1, mix1], 0), feed0, mix0, turned.reshape(parts // 2, 2, width, SLOTS), scalars
        )
        scalars = jnp.sum(scalars, (0, 1, 2))
        pieces, runs, places = [[whole0], [whole1]], parts // 2, [0, 0, 0]
    else:
        own_mats = []
        for part, stages in pending:
            for stage in stages:
                part = share_out(part, 0, *stage)
            own_mats.append(part)
        own_dense = turned
        for axis, bit, radix in core:
            own_dense = share_out(own_dense.reshape(-1, radix, width, SLOTS), 1, axis, bit, radix)
        for axis, bit, radix in cross:
            own_dense = share_out(own_dense, 3, axis, bit, radix)
        for axis, bit, radix in along:
            own_dense = share_out(own_dense.reshape(-1, radix, width, own_dense.shape[3]), 1, axis, bit, radix)
        own_dense = own_dense.reshape(width, -1)

        square_own = sum(jnp.sum(part * part) for part in [own_dense] + own_mats)
        scalars = jnp.where(jnp.arange(LANES) == 0, square_own, scalars)
        scalars = total_of(scalars, core + cross + along)

        pieces = []
        for tall_part, wide_part in zip(own_mats[1::2], own_mats[::2]):
            if len(along) == 1 and wide_part.shape[0] % 16 == 0 and tall_part.shape[0] % 16 == 0:
                runs = along[0][2]
                part = jnp.concatenate(collect(jnp.concatenate([wide_part, tall_part], 0), *along[0]), 0)
            else:
                runs = 1
                for stage in reversed(along):
                    turn_at = digit(*stage)
                    wide_part = jnp.concatenate(in_order(collect(wide_part, *stage), turn_at), 0)
                    tall_part = jnp.concatenate(in_order(collect(tall_part, *stage), turn_at), 0)
                part = jnp.concatenate([wide_part, tall_part], 0)
            found = [part]
            for stage in (cross + core if len(cross) == 1 else cross[::-1] + core):
                rounds = [collect(part, *stage) for part in found]
                found = [rounds[j][k] for k in range(stage[2]) for j in range(len(rounds))]
            pieces.insert(0, found)
        fill = -width % 8
        dense_pieces = [jnp.pad(own_dense, ((0, fill), (0, 0)))]
        for stage in cross[::-1]:
            rounds = [collect(part, *stage) for part in dense_pieces]
            dense_pieces = [rounds[j][k] for k in range(stage[2]) for j in range(len(rounds))]
        dense_pieces = jnp.stack(dense_pieces)
        places = [(dp_index % 2) * sections + section, dp_index // 2 if runs > 1 else 0, section]

    square_total, error_total, weight_total = scalars[0, 0], scalars[0, 1], scalars[0, 2]
    grad_norm = jnp.sqrt(square_total) / weight_total
    factor = jnp.minimum(1.0, clip_level / grad_norm) / weight_total
    steps_done = step_count[0].astype(f32)
    corrections = [1.0 - jnp.power(beta, steps_done) for beta in (beta_first, beta_second)]
    index = jnp.stack([jnp.asarray(k, jnp.int32) for k in (dp_index, *places)])
    (
        dense_new, dense_m_new, dense_v_new, dense_ema_new,
        vectors_new, vectors_m_new, vectors_v_new, vectors_ema_new,
    ) = adam(
        index, jnp.stack([factor, *corrections]), dense_pieces,
        (dense, dense_m, dense_v, dense_ema), (vectors, vectors_m, vectors_v, vectors_ema),
    )

    new, arrived = None, [None] * LAYERS
    for layer in reversed(range(LAYERS)):
        new, step = shampoo(
            layer, pieces[layer], runs, index, factor.reshape(1), (stat_small, stat_qkv, stat_wide), around,
            (root_small, root_qkv, root_wide), (w_out, w_fc2), (ema_out, ema_fc2), new,
        )
        step = step.reshape(parts, width, -1)
        sent = [
            lax.dynamic_index_in_dim(step, jnp.bitwise_xor(dp_index, k), 0, False) for k in range(parts)
        ]
        arrived[layer] = jnp.stack([swap(part, "dp", k) if k else part for k, part in enumerate(sent)])
    stat_small_new, stat_qkv_new, stat_wide_new, out_new, fc2_new, ema_out_new, ema_fc2_new = new
    qkv_new, fc1_new, ema_qkv_new, ema_fc1_new = finish(
        parts, index, factor.reshape(1), arrived, (w_qkv, w_fc1), (ema_qkv, ema_fc1)
    )
    return (
        error_total / weight_total,
        grad_norm,
        dense_new,
        dense_m_new,
        dense_v_new,
        dense_ema_new,
        vectors_new,
        vectors_m_new,
        vectors_v_new,
        vectors_ema_new,
        qkv_new,
        out_new,
        fc1_new,
        fc2_new,
        ema_qkv_new,
        ema_out_new,
        ema_fc1_new,
        ema_fc2_new,
        stat_small_new,
        stat_qkv_new,
        stat_wide_new,
    )


def solution(mesh):
    items = P("dp", None, None)
    columns = P(None, "dp")
    matrix = P(None, "dp", None)
    stacked = P(None, None, "dp", None)
    return jax.shard_map(
        per_device,
        mesh=mesh,
        in_specs=(
            (items, items, P("dp"), P())
            + (columns,) * 8
            + (matrix,) * 8
            + (stacked, matrix, stacked) * 2
        ),
        out_specs=(P(), P()) + (columns,) * 8 + (matrix,) * 8 + (stacked, matrix, stacked),
        check_vma=False,
    )
```

```python
import functools
import math

import jax
import jax.numpy as jnp
import numpy as np
from jax import lax
from jax.experimental import pallas as pl
from jax.experimental.pallas import tpu as pltpu
from jax.sharding import PartitionSpec as P

D = 384
HEADS = 6
HDIM = 64
SURF = 4
LEVELS = 13
VARS = 69
PIX = 4
VP = 276
LAT_ROWS = 64
LON_COLS = 16
SEQ = 1024
LAYERS = 2
FF = 1536
BLOCKS = 4 + 2 * (FF // D)

LANES = 128
PAIRS = HEADS // 2
EXT = (PIX + 1) * LANES
TABLE = VARS * (PIX + 1)

AT_PROJ = SEQ
AT_HEAD = AT_PROJ + D
AT_TABLE = AT_HEAD + 3 * LANES
AT_VECTOR = AT_TABLE + EXT
SLOTS = AT_VECTOR + LANES

highest = lax.Precision.HIGHEST
f32 = jnp.float32
bf16 = jnp.bfloat16
norm_eps = 1e-05
clip_level = 0.001
rate_dense = 0.05
rate_vector = 0.2
rate_matrix = 0.5
beta_first = 0.9
beta_second = 0.95
adam_eps = 1e-08
weight_decay = 0.1
stat_beta = 0.95
ema_beta = 0.9
LOG2E = math.log2(math.e)
SCALE2 = LOG2E * HDIM ** (-0.5)

NN = (((1,), (0,)), ((), ()))
NT = (((1,), (1,)), ((), ()))
TN = (((0,), (0,)), ((), ()))


def dot(left, right, dims=NN):
    return lax.dot_general(left, right, dims, preferred_element_type=f32)


def halves(value):
    high = value.astype(bf16)
    return high, (value - high.astype(f32)).astype(bf16)


def call(body, out_shape, scratch=(), vmem=60 << 20, flops=0, traffic=0):
    return pl.pallas_call(
        body,
        out_shape=out_shape,
        scratch_shapes=list(scratch),
        compiler_params=pltpu.CompilerParams(vmem_limit_bytes=vmem),
        cost_estimate=pl.CostEstimate(flops=flops, bytes_accessed=traffic, transcendentals=0),
    )


def shape(dims, kind=f32):
    return jax.ShapeDtypeStruct(dims, kind)


def norm_parts(values):
    center = values - jnp.mean(values, -1, keepdims=True)
    spread = jnp.mean(center * center, -1, keepdims=True)
    inverse = lax.rsqrt(spread + norm_eps)
    return center * inverse, inverse


def norm_back(values, gain, upstream):
    unit, inverse = norm_parts(values)
    scaled = upstream * gain
    back = inverse * (
        scaled
        - jnp.mean(scaled, -1, keepdims=True)
        - unit * jnp.mean(scaled * unit, -1, keepdims=True)
    )
    return back, jnp.sum(upstream * unit, 0, keepdims=True)


def tiles(count, body):
    def step(index, carry):
        body(index)
        return carry

    lax.fori_loop(0, count, step, 0)


def rows_of(index, size):
    return pl.ds(pl.multiple_of(index * size, size), size)


def head_mask(rows, which):
    lane = lax.broadcasted_iota(jnp.int32, (rows, LANES), 1)
    return (lane >= which * HDIM) & (lane < (which + 1) * HDIM)


def spread_fields(field_rows):
    row = lax.broadcasted_iota(jnp.int32, (VP, PIX * LANES), 0)
    col = lax.broadcasted_iota(jnp.int32, (VP, PIX * LANES), 1)
    var, pixel = col % LANES, col // LANES
    chosen = (row == PIX * var + pixel) & (var < VARS)
    return dot(field_rows, jnp.where(chosen, 1.0, 0.0).astype(bf16))


def query_mask(query_row):
    head = lax.broadcasted_iota(jnp.int32, (8, D), 0)
    lane = lax.broadcasted_iota(jnp.int32, (8, D), 1)
    return jnp.where(lane // HDIM == head, query_row * HDIM ** (-0.5), 0.0)


def query_scores(table_ref, mask, query_scr):
    for j in range(PIX + 1):
        part = table_ref[j * LANES : (j + 1) * LANES, :]
        query_scr[j * 8 : (j + 1) * 8, :] = dot(mask.astype(bf16), part, NT)


def mix_weights(extended, query_scr, head, valid):
    score = query_scr[pl.ds(PIX * 8 + head, 1), :]
    for j in range(PIX):
        score = score + extended[j] * query_scr[pl.ds(j * 8 + head, 1), :]
    score = jnp.where(valid > 0, score, jnp.where(valid < 0, -jnp.inf, -1e9))
    peak = jnp.max(score, -1, keepdims=True)
    weight = jnp.exp(score - peak)
    return weight / jnp.sum(weight, -1, keepdims=True)


def embed_body(field_ref, table_ref, query_ref, valid_ref, proj_ref, pos_ref, out_ref, agg_ref, query_scr):
    size = 256
    query_scores(table_ref, query_mask(query_ref[...]), query_scr)

    def tile(index):
        rows = rows_of(index, size)
        wide = spread_fields(field_ref[rows, :])
        extended = [wide[:, j * LANES : (j + 1) * LANES] for j in range(PIX)]
        valid = valid_ref[...]

        def pair(hp, carry):
            lanes = rows_of(hp, LANES)
            table = table_ref[:, lanes]
            total = jnp.zeros((size, LANES), f32)
            for which in range(2):
                weight = mix_weights(extended, query_scr, 2 * hp + which, valid)
                mixing = jnp.concatenate([weight * extended[j] for j in range(PIX)] + [weight], 1)
                own = jnp.where(head_mask(EXT, which), table, jnp.zeros_like(table))
                high, low = halves(mixing)
                total = total + dot(high, own) + dot(low, own)
            agg_ref[rows, lanes] = total.astype(bf16)
            return carry

        lax.fori_loop(0, PAIRS, pair, 0)
        out_ref[rows, :] = (dot(agg_ref[rows, :], proj_ref[...]) + pos_ref[rows, :].astype(f32)).astype(bf16)

    tiles(SEQ // size, tile)


def embed_forward(field_rows, table, query_row, valid, proj, position):
    return call(
        embed_body,
        (shape((SEQ, D), bf16), shape((SEQ, D), bf16)),
        [pltpu.VMEM((40, LANES), f32)],
        flops=4_000_000_000,
        traffic=4_000_000,
    )(field_rows, table, query_row, valid, proj, position)


def embed_back_body(
    field_ref, table_ref, query_ref, valid_ref, proj_ref, agg_ref, grad_ref, dhead_ref, dvector_ref,
    out_ref, vector_scr, query_scr, wide_scr, merged_scr, high_scr, low_scr, dscore_scr,
):
    size = 256
    mask = query_mask(query_ref[...])
    query_scores(table_ref, mask, query_scr)
    out_ref[:, AT_PROJ : AT_PROJ + D] = dot(grad_ref[...], agg_ref[...], TN)
    out_ref[:, AT_HEAD:AT_TABLE] = jnp.zeros((D, AT_TABLE - AT_HEAD), f32)
    out_ref[:, AT_HEAD : AT_HEAD + VP] = dhead_ref[...]
    dscore_scr[...] = jnp.zeros_like(dscore_scr)

    def prepare(index):
        rows = rows_of(index, size)
        wide_scr[rows, :] = spread_fields(field_ref[rows, :])
        merged_scr[rows, :] = dot(grad_ref[rows, :], proj_ref[...], NT)
        out_ref[:, rows] = grad_ref[rows, :].astype(f32).T

    tiles(SEQ // size, prepare)

    def pair(hp):
        lanes = rows_of(hp, LANES)
        table = table_ref[:, lanes]
        total = jnp.zeros((LANES, EXT), f32)
        for which in range(2):
            head = 2 * hp + which
            own = jnp.where(head_mask(EXT, which), table, jnp.zeros_like(table))
            twice = jnp.concatenate([own, own], 1)

            def tile(index):
                rows = rows_of(index, size)
                extended = [wide_scr[rows, j * LANES : (j + 1) * LANES] for j in range(PIX)]
                weight = mix_weights(extended, query_scr, head, valid_ref[...])
                mixing = jnp.concatenate([weight * extended[j] for j in range(PIX)] + [weight], 1)
                high, low = halves(mixing)
                high_scr[rows, :] = high
                low_scr[rows, :] = low
                grad_high, grad_low = halves(merged_scr[rows, lanes])
                dmix = dot(jnp.concatenate([grad_high, grad_low], 1), twice, NT)
                dweight = dmix[:, PIX * LANES :]
                for j in range(PIX):
                    dweight = dweight + dmix[:, j * LANES : (j + 1) * LANES] * extended[j]
                dscore = weight * (dweight - jnp.sum(weight * dweight, -1, keepdims=True))
                for j in range(PIX + 1):
                    piece = dscore * extended[j] if j < PIX else dscore
                    at = pl.ds(j * 8 + head, 1)
                    dscore_scr[at, :] = dscore_scr[at, :] + jnp.sum(piece, 0, keepdims=True)

            tiles(SEQ // size, tile)
            grad_high, grad_low = halves(merged_scr[:, lanes])
            keep = head_mask(SEQ, which)
            grad_high = jnp.where(keep, grad_high, jnp.zeros_like(grad_high))
            grad_low = jnp.where(keep, grad_low, jnp.zeros_like(grad_low))
            both = dot(jnp.concatenate([grad_high, grad_low], 1), high_scr[...], TN)
            total = total + both[:LANES, :] + both[LANES:, :] + dot(grad_high, low_scr[...], TN)
        out_ref[lanes, AT_TABLE:AT_VECTOR] = total

    tiles(PAIRS, pair)
    dquery = jnp.zeros((1, D), f32)
    head = lax.broadcasted_iota(jnp.int32, (8, D), 0)
    lane = lax.broadcasted_iota(jnp.int32, (8, D), 1)
    for j in range(PIX + 1):
        part = dscore_scr[j * 8 : (j + 1) * 8, :]
        block = slice(j * LANES, (j + 1) * LANES)
        lanes = slice(AT_TABLE + j * LANES, AT_TABLE + (j + 1) * LANES)
        out_ref[:, lanes] = out_ref[:, lanes] + lax.dot_general(
            mask, part, TN, precision=highest, preferred_element_type=f32
        )
        spread = lax.dot_general(
            part, table_ref[block, :].astype(f32), NN, precision=highest, preferred_element_type=f32
        )
        dquery = dquery + jnp.sum(jnp.where(lane // HDIM == head, spread, 0.0), 0, keepdims=True)
    vector_scr[...] = jnp.zeros_like(vector_scr)
    vector_scr[0:8, :] = dvector_ref[...]
    vector_scr[0:1, :] = dquery * HDIM ** (-0.5)
    out_ref[:, AT_VECTOR:SLOTS] = vector_scr[...].T


def embed_back(field_rows, table, query_row, valid, proj, agg, grad, dhead, dvector):
    return call(
        embed_back_body,
        shape((D, SLOTS)),
        [
            pltpu.VMEM((LANES, D), f32),
            pltpu.VMEM((40, LANES), f32),
            pltpu.VMEM((SEQ, PIX * LANES), f32),
            pltpu.VMEM((SEQ, D), f32),
            pltpu.VMEM((SEQ, EXT), bf16),
            pltpu.VMEM((SEQ, EXT), bf16),
            pltpu.VMEM((40, LANES), f32),
        ],
        flops=12_000_000_000,
        traffic=6_000_000,
    )(field_rows, table, query_row, valid, proj, agg, grad, dhead, dvector)


def square(ref, index):
    return ref[index * D : (index + 1) * D, :]


def block_body(start, x_ref, gain_ref, packed_ref, *refs):
    *refs, m_ref, h2_ref, y_ref = refs[: 7 if start is None else 8]
    if start is None:
        w_ref = packed_ref
        h_ref, qkv_ref, o_ref, lse_ref = refs
    else:
        w_ref, h_ref, qkv_ref, o_ref, lse_ref = refs
        shards = packed_ref.shape[0]
        rows, tall = D // shards, FF // shards
        above = BLOCKS - FF // D
        for k in range(shards):
            for b in range(above):
                at = start + b * rows
                w_ref[b * D + k * rows : b * D + (k + 1) * rows, :] = packed_ref[k, at : at + rows, :]
            at = start + above * rows
            to = above * D + k * tall
            w_ref[to : to + tall, :] = packed_ref[k, at : at + tall, :]
    size = 256

    def enter(index):
        rows = rows_of(index, size)
        unit, unused = norm_parts(x_ref[rows, :].astype(f32))
        hidden = (unit * gain_ref[0:1, :]).astype(bf16)
        h_ref[rows, :] = hidden
        for b in range(3):
            qkv_ref[rows, b * D : (b + 1) * D] = dot(hidden, square(w_ref, b)).astype(bf16)

    tiles(SEQ // size, enter)
    lse_ref[...] = jnp.zeros_like(lse_ref)

    def pair(hp):
        keys = qkv_ref[:, pl.ds(pl.multiple_of(D + hp * LANES, LANES), LANES)]
        values = qkv_ref[:, pl.ds(pl.multiple_of(2 * D + hp * LANES, LANES), LANES)]

        def tile(index):
            rows = rows_of(index, size)
            queries = qkv_ref[rows, rows_of(hp, LANES)]
            parts = []
            for which in range(2):
                own = jnp.where(head_mask(size, which), queries, jnp.zeros_like(queries))
                score = dot(keys, own, NT) * SCALE2
                peak = jnp.max(score, 0, keepdims=True)
                power = jnp.exp2(score - peak)
                total = jnp.sum(power, 0, keepdims=True)
                chance = (power * (1.0 / total)).astype(bf16)
                mixed = dot(values, chance, TN)
                parts.append(mixed[which * HDIM : (which + 1) * HDIM, :])
                lse_ref[pl.ds(2 * hp + which, 1), rows] = peak + jnp.log2(total)
            o_ref[rows, rows_of(hp, LANES)] = jnp.concatenate(parts, 0).T.astype(bf16)

        tiles(SEQ // size, tile)

    tiles(PAIRS, pair)

    def leave(index):
        rows = rows_of(index, size)
        middle = x_ref[rows, :].astype(f32) + dot(o_ref[rows, :], square(w_ref, 3))
        m_ref[rows, :] = middle
        unit, unused = norm_parts(middle)
        hidden = (unit * gain_ref[1:2, :]).astype(bf16)
        h2_ref[rows, :] = hidden
        total = jnp.zeros((size, D), f32)
        for b in range(FF // D):
            before = dot(hidden, square(w_ref, 4 + b))
            active = (0.5 * before * (1.0 + lax.erf(before * math.sqrt(0.5)))).astype(bf16)
            total = total + dot(active, square(w_ref, 8 + b))
        y_ref[rows, :] = (middle + total).astype(bf16)

    tiles(SEQ // size, leave)


def block_forward(x, gains, weights, start=None):
    return call(
        functools.partial(block_body, start),
        (() if start is None else (shape((BLOCKS * D, D), bf16),))
        + (
            shape((SEQ, D), bf16),
            shape((SEQ, 3 * D), bf16),
            shape((SEQ, D), bf16),
            shape((8, SEQ)),
            shape((SEQ, D)),
            shape((SEQ, D), bf16),
            shape((SEQ, D), bf16),
        ),
        flops=12_000_000_000,
        traffic=12_000_000,
    )(x, gains, weights)


def feed_back_body(h2_ref, m_ref, dy_ref, gain_ref, w_ref, dm_ref, do_ref, dgain_ref, dw_ref, r_scr, df_scr):
    size = 256
    dgain_ref[...] = jnp.zeros_like(dgain_ref)

    def first(index):
        rows = rows_of(index, size)
        grad_next = dy_ref[rows, :]
        hidden = h2_ref[rows, :]
        upstream = jnp.zeros((size, D), f32)
        for b in range(FF // D):
            cols = slice(b * D, (b + 1) * D)
            before = dot(hidden, square(w_ref, 4 + b))
            upper = 0.5 * (1.0 + lax.erf(before * math.sqrt(0.5)))
            r_scr[rows, cols] = (before * upper).astype(bf16)
            slope = upper + before * (jnp.exp2(before * before * (-0.5 * LOG2E)) * (1.0 / math.sqrt(2 * math.pi)))
            grad_before = (dot(grad_next, square(w_ref, 8 + b), NT) * slope).astype(bf16)
            df_scr[rows, cols] = grad_before
            upstream = upstream + dot(grad_before, square(w_ref, 4 + b), NT)
        back, dgain = norm_back(m_ref[rows, :], gain_ref[1:2, :], upstream)
        dgain_ref[...] = dgain_ref[...] + dgain
        middle = grad_next.astype(f32) + back
        dm_ref[rows, :] = middle
        do_ref[rows, :] = dot(middle.astype(bf16), square(w_ref, 3), NT).astype(bf16)

    tiles(SEQ // size, first)

    def wide(index):
        cols = rows_of(index, D)
        dw_ref[rows_of(index, D), :] = dot(h2_ref[...], df_scr[:, cols], TN)
        dw_ref[rows_of(FF // D + index, D), :] = dot(r_scr[:, cols], dy_ref[...], TN)

    tiles(FF // D, wide)


def feed_back(h2, m, dy, gains, weights):
    return call(
        feed_back_body,
        (shape((SEQ, D)), shape((SEQ, D), bf16), shape((1, D)), shape((2 * FF, D))),
        [pltpu.VMEM((SEQ, FF), bf16), pltpu.VMEM((SEQ, FF), bf16)],
        flops=17_000_000_000,
        traffic=14_000_000,
    )(h2, m, dy, gains, weights)


def mix_back_body(x_ref, h_ref, qkv_ref, o_ref, lse_ref, dm_ref, do_ref, gain_ref, w_ref,
                  dx_ref, dgain_ref, dw_ref, dqkv_scr, dkv_scr):
    size = 256
    dgain_ref[...] = jnp.zeros_like(dgain_ref)
    dw_ref[3 * D : 4 * D, :] = dot(o_ref[...], dm_ref[...].astype(bf16), TN)

    def pair(hp):
        lanes = rows_of(hp, LANES)
        klanes = pl.ds(pl.multiple_of(D + hp * LANES, LANES), LANES)
        vlanes = pl.ds(pl.multiple_of(2 * D + hp * LANES, LANES), LANES)
        keys = qkv_ref[:, klanes]
        values = qkv_ref[:, vlanes]
        dkv_scr[...] = jnp.zeros_like(dkv_scr)

        def tile(index):
            rows = rows_of(index, size)
            queries = qkv_ref[rows, lanes]
            upstream = do_ref[rows, lanes]
            parts = []
            for which in range(2):
                keep = head_mask(size, which)
                own = jnp.where(keep, queries, jnp.zeros_like(queries))
                own_up = jnp.where(keep, upstream, jnp.zeros_like(upstream))
                score = dot(keys, own, NT) * SCALE2
                chance = jnp.exp2(score - lse_ref[pl.ds(2 * hp + which, 1), rows])
                dchance = dot(values, own_up, NT)
                shift = jnp.sum(dchance * chance, 0, keepdims=True)
                dscore = (chance * (dchance - shift)).astype(bf16)
                dkv_scr[:, :LANES] = dkv_scr[:, :LANES] + dot(dscore, own)
                dkv_scr[:, LANES:] = dkv_scr[:, LANES:] + dot(chance.astype(bf16), own_up)
                dquery = dot(keys, dscore, TN)
                parts.append(dquery[which * HDIM : (which + 1) * HDIM, :])
            dqkv_scr[rows, lanes] = (jnp.concatenate(parts, 0).T * HDIM ** (-0.5)).astype(bf16)

        tiles(SEQ // size, tile)
        dqkv_scr[:, klanes] = (dkv_scr[:, :LANES] * HDIM ** (-0.5)).astype(bf16)
        dqkv_scr[:, vlanes] = dkv_scr[:, LANES:].astype(bf16)

    tiles(PAIRS, pair)

    def third(index):
        cols = rows_of(index, D)
        dw_ref[cols, :] = dot(h_ref[...], dqkv_scr[:, cols], TN)

    tiles(3, third)

    def last(index):
        rows = rows_of(index, size)
        upstream = jnp.zeros((size, D), f32)
        for b in range(3):
            upstream = upstream + dot(dqkv_scr[rows, b * D : (b + 1) * D], square(w_ref, b), NT)
        back, dgain = norm_back(x_ref[rows, :].astype(f32), gain_ref[0:1, :], upstream)
        dgain_ref[...] = dgain_ref[...] + dgain
        dx_ref[rows, :] = (dm_ref[rows, :] + back).astype(bf16)

    tiles(SEQ // size, last)


def mix_back(x, kept, dm, do, gains, weights):
    return call(
        mix_back_body,
        (shape((SEQ, D), bf16), shape((1, D)), shape((4 * D, D))),
        [pltpu.VMEM((SEQ, 3 * D), bf16), pltpu.VMEM((SEQ, 2 * LANES), f32)],
        flops=17_000_000_000,
        traffic=14_000_000,
    )(x, *kept, dm, do, gains, weights)


def head_body(y_ref, gain_ref, head_ref, target_ref, cos_ref, valid_ref,
              dy_ref, dhead_ref, dgain_ref, error_ref, h_scr, dp_scr):
    size = 256
    dgain_ref[...] = jnp.zeros_like(dgain_ref)
    error_ref[...] = jnp.zeros_like(error_ref)

    def tile(index):
        rows = rows_of(index, size)
        values = y_ref[rows, :].astype(f32)
        unit, unused = norm_parts(values)
        hidden = (unit * gain_ref[...]).astype(bf16)
        h_scr[rows, :] = hidden
        residual = dot(hidden, head_ref[...], NT) - target_ref[rows, :].astype(f32)
        lane = lax.broadcasted_iota(jnp.int32, (size, VP), 1)
        cosine = jnp.where(lane % PIX < 2, cos_ref[rows, 0:1], cos_ref[rows, 1:2])
        weight = cosine * valid_ref[...]
        error_ref[...] = error_ref[...] + jnp.sum(weight * residual * residual, 0, keepdims=True)
        grad = (2.0 * weight * residual).astype(bf16)
        dp_scr[rows, :] = grad
        back, dgain = norm_back(values, gain_ref[...], dot(grad, head_ref[...]))
        dgain_ref[...] = dgain_ref[...] + dgain
        dy_ref[rows, :] = back.astype(bf16)

    tiles(SEQ // size, tile)
    dhead_ref[...] = dot(h_scr[...], dp_scr[...], TN)


def head_step(y, gain, head_rows, target, cosines, valid):
    return call(
        head_body,
        (shape((SEQ, D), bf16), shape((D, VP)), shape((1, D)), shape((1, VP))),
        [pltpu.VMEM((SEQ, D), bf16), pltpu.VMEM((SEQ, VP), bf16)],
        flops=700_000_000,
        traffic=4_000_000,
    )(y, gain, head_rows, target, cosines, valid)


def dot3(left, right, dims=NN):
    return dot(left[0], right[0], dims) + dot(left[0], right[1], dims) + dot(left[1], right[0], dims)


def chosen_rows(count, width, start, offset):
    row = lax.broadcasted_iota(jnp.int32, (count, width), 0)
    col = lax.broadcasted_iota(jnp.int32, (count, width), 1)
    return jnp.where(col + offset == row + start, 1.0, 0.0).astype(bf16)


def pick(selector, pair, dims=NN):
    return [dot(selector, part, dims).astype(bf16) for part in pair]


def shampoo_body(along, index_ref, factor_ref, small_ref, qkv_ref, wide_ref, around_ref,
                 left_out_ref, left_fc2_ref, right_qkv_ref, right_fc1_ref,
                 wout_ref, wfc2_ref, eout_ref, efc2_ref, piece_ref,
                 nsmall_ref, nqkv_ref, nwide_ref, nout_ref, nfc2_ref, meout_ref, mefc2_ref,
                 step_ref, high_scr, low_scr):
    pieces = piece_ref.shape[1]
    me = index_ref[0]
    factor = factor_ref[0]
    wide_rows, tall_rows = 2 * FF // (pieces * along), 4 * D // (pieces * along)
    for k in range(pieces):
        block = jnp.bitwise_xor(index_ref[1], k) * along
        for j in range(along):
            place = block + jnp.bitwise_xor(index_ref[2], j)
            at = j * (wide_rows + tall_rows)
            high, low = halves(piece_ref[0, k, at : at + wide_rows, :])
            rows = pl.ds(pl.multiple_of(4 * D + place * wide_rows, 16), wide_rows)
            high_scr[rows, :] = high
            low_scr[rows, :] = low
            high, low = halves(piece_ref[0, k, at + wide_rows : at + wide_rows + tall_rows, :])
            rows = pl.ds(pl.multiple_of(place * tall_rows, 16), tall_rows)
            high_scr[rows, :] = high
            low_scr[rows, :] = low

    def grad(b):
        return square(high_scr, b), square(low_scr, b)

    def mixed(old, product):
        return stat_beta * old + (1.0 - stat_beta) * (factor * (factor * product))

    def root(k):
        return halves(around_ref[0, k])

    rows = small_ref.shape[2]
    own_row = chosen_rows(rows, D, me * rows, 0)
    place = 0
    for first, count, left, right_ref, nright_ref, right_root_ref, left_root in (
        (0, 3, 0, qkv_ref, nqkv_ref, right_qkv_ref, 0),
        (4, FF // D, 3, wide_ref, nwide_ref, right_fc1_ref, 2),
    ):
        take = (0, 0) if first else (0,)
        cols = right_ref.shape[-2]
        total = jnp.zeros((rows, D), f32)
        own_cols = [jnp.zeros((cols, D), f32)] * 2
        share = right_root_ref.shape[-2]
        reach = jnp.zeros((D, share), f32)
        for b in range(count):
            block = grad(first + b)
            total = total + dot3(pick(own_row, block), block, NT)
            selector = chosen_rows(cols, D, me * cols, b * D)
            own_cols = [own + dot(selector, part, NT) for own, part in zip(own_cols, block)]
            reach = reach + dot3(block, halves(right_root_ref[take + (slice(None), slice(b * D, (b + 1) * D))]), NT)
        nsmall_ref[0, left] = mixed(small_ref[0, left], total)
        own_cols = [own.astype(bf16) for own in own_cols]
        for b in range(count):
            lanes = slice(b * D, (b + 1) * D)
            nright_ref[take + (slice(None), lanes)] = mixed(
                right_ref[take + (slice(None), lanes)], dot3(own_cols, grad(first + b))
            )
        step_ref[0, :, place : place + share] = dot3(root(left_root), halves(reach))
        place = place + share

    block = grad(3)
    nsmall_ref[0, 1] = mixed(small_ref[0, 1], dot3(pick(own_row, block), block, NT))
    nsmall_ref[0, 2] = mixed(small_ref[0, 2], dot3(pick(own_row, block, NT), block))
    moved = dot3(halves(dot3(halves(left_out_ref[0, 0]), block)), root(1))
    updated = wout_ref[0] - rate_matrix * factor * moved
    nout_ref[0] = updated
    meout_ref[0] = average(eout_ref[0], updated)

    tall = wide_ref.shape[2]
    total = jnp.zeros((rows, D), f32)
    own = [jnp.zeros((tall, D), f32)] * 2
    reach = jnp.zeros((tall, D), f32)
    for b in range(FF // D):
        block = grad(8 + b)
        total = total + dot3(pick(own_row, block, NT), block)
        selector = chosen_rows(tall, D, me * tall, b * D)
        own = [o + dot(selector, part) for o, part in zip(own, block)]
        reach = reach + dot3(halves(left_fc2_ref[0, 0, :, b * D : (b + 1) * D]), block)
    nsmall_ref[0, 4] = mixed(small_ref[0, 4], total)
    own = [o.astype(bf16) for o in own]
    for b in range(FF // D):
        lanes = slice(b * D, (b + 1) * D)
        nwide_ref[0, 1, :, lanes] = mixed(wide_ref[0, 1, :, lanes], dot3(own, grad(8 + b), NT))
    updated = wfc2_ref[0] - rate_matrix * factor * dot3(halves(reach), root(3))
    nfc2_ref[0] = updated
    mefc2_ref[0] = average(efc2_ref[0], updated)


def layer_block(array, *second):
    lead = len(second)
    dims = (1,) * (1 + lead) + array.shape[1 + lead :]
    return pl.BlockSpec(dims, lambda i: (i,) + second + (0,) * (array.ndim - 1 - lead))


def shampoo(pieces, along, index, factor, stats, around, roots, weights, averages):
    small, qkv, wide = stats
    root_small, root_qkv, root_wide = roots
    scalar = pl.BlockSpec(memory_space=pltpu.SMEM)
    layered = [small, qkv, wide, around]
    tails = [*weights, *averages, pieces]
    results = [small, qkv, wide, *weights, *averages]
    specs = [scalar, scalar] + [layer_block(x) for x in layered]
    specs += [layer_block(root_small, 1), layer_block(root_wide, 1), layer_block(root_qkv), layer_block(root_wide, 0)]
    specs += [layer_block(x) for x in tails]
    step = shape((LAYERS, D, root_qkv.shape[1] + root_wide.shape[2]))
    return pl.pallas_call(
        functools.partial(shampoo_body, along),
        grid=(LAYERS,),
        in_specs=specs,
        out_specs=[layer_block(x) for x in [*results, step]],
        out_shape=[shape(x.shape) for x in results] + [step],
        scratch_shapes=[pltpu.VMEM((BLOCKS * D, D), bf16)] * 2,
        compiler_params=pltpu.CompilerParams(vmem_limit_bytes=62 << 20),
        cost_estimate=pl.CostEstimate(flops=10_000_000_000, bytes_accessed=60_000_000, transcendentals=0),
    )(index, factor, *layered, root_small, root_wide, root_qkv, root_wide, *tails)


def close_body(feed1_ref, mix1_ref, feed0_ref, mix0_ref, turned_ref, scalar_ref,
               out_ref, outd_ref, outs_ref,
               own1_scr, own0_scr, feed1_scr, mix1_scr, feed_scr, mix_scr, mixz_scr, dense_scr, core_scr, cross_scr, along_scr,
               mix_sum, dense_sum, own_dense, own_scalar, send_sem, recv_sem, local_sem):
    s = lax.axis_index("section")
    dp = lax.axis_index("dp")
    z, c = dp // 2, dp % 2
    mine = c * 4 + s
    rows = own0_scr.shape[0]
    out0_ref, out1_ref = out_ref.at[0], out_ref.at[1]
    feed_rows, mix_rows = feed0_ref.shape[0] // 4, mix0_ref.shape[0] // 16
    width = turned_ref.shape[2]
    span = SLOTS // 4
    peers = [{"section": s, "dp": jnp.bitwise_xor(dp, 1)}]
    peers += [{"section": jnp.bitwise_xor(s, k), "dp": dp} for k in (1, 2, 3)]
    peers += [{"section": s, "dp": jnp.bitwise_xor(dp, 2 * k)} for k in (1, 2, 3)]
    barrier = pltpu.get_barrier_semaphore()
    for peer in peers:
        pl.semaphore_signal(barrier, inc=1, device_id=peer, device_id_type=pl.DeviceIdType.MESH)
    pl.semaphore_wait(barrier, len(peers))
    count = [0, 0]
    sent = []

    def send(source, target, peer):
        n = count[0]
        count[0] = n + 1
        copy = pltpu.make_async_remote_copy(
            src_ref=source, dst_ref=target, send_sem=send_sem.at[n], recv_sem=recv_sem.at[n],
            device_id=peer, device_id_type=pl.DeviceIdType.MESH,
        )
        copy.start()
        sent.append(copy)
        return copy

    def keep(source, target):
        n = count[1]
        count[1] = n + 1
        copy = pltpu.make_async_copy(source, target, local_sem.at[n])
        copy.start()
        return copy

    def arrive(copies):
        for copy in copies:
            copy.wait_recv()

    def across(k):
        return jnp.bitwise_xor(s, k)

    def up(k):
        return jnp.bitwise_xor(z, k)

    def at(index, size, align):
        return pl.ds(pl.multiple_of(index * size, align), size)

    core, (x, y, diagonal), tower = peers[0], peers[1:4], peers[4:]
    flat = (x, y, diagonal)

    def gather_up(own_ref, out_ref):
        place = out_ref.at[mine, at(z, rows, 16), :]
        local = keep(own_ref, place)
        return local, [send(own_ref, place, peer) for peer in tower]

    def gather_flat(out_ref, started):
        local, copies = started
        local.wait()
        arrive(copies)
        block = out_ref.at[mine]
        found = [send(block, block, x), send(block, block, y)]
        send_core = [send(block, block, core)]
        return found, send_core

    def gather_turn(out_ref, started):
        (from_x, from_y), to_core = started
        half = 2 * rows
        from_x.wait_recv()
        block_x = c * 4 + across(1)
        upper = out_ref.at[block_x, pl.ds(0, half), :]
        turn_y = send(upper, upper, y)
        to_core.append(send(out_ref.at[block_x], out_ref.at[block_x], core))
        from_y.wait_recv()
        block_y = c * 4 + across(2)
        lower = out_ref.at[block_y, pl.ds(half, half), :]
        turn_x = send(lower, lower, x)
        to_core.append(send(out_ref.at[block_y], out_ref.at[block_y], core))
        return [turn_y, turn_x], to_core

    def gather_core(out_ref, started):
        turned, to_core = started
        arrive(turned)
        block = out_ref.at[c * 4 + across(3)]
        return to_core + [send(block, block, core)]

    feed1_up = [send(feed1_ref.at[at(up(k), feed_rows, 16), :], feed1_scr.at[k - 1], tower[k - 1]) for k in (1, 2, 3)]
    mix1_up = [send(mix1_ref.at[at(up(k), mix_rows, 16), :], mix1_scr.at[k - 1], tower[k - 1]) for k in (1, 2, 3)]
    dense_core = send(turned_ref.at[:, 1 - c], core_scr, core)
    feed_up = [send(feed0_ref.at[at(up(k), feed_rows, 16), :], feed_scr.at[k - 1], tower[k - 1]) for k in (1, 2, 3)]
    mix_flat = [
        send(mix0_ref.at[at(across(k), 4 * mix_rows, 16), :], mix_scr.at[k - 1], flat[k - 1]) for k in (1, 2, 3)
    ]
    dense_core.wait_recv()

    def add_core(k):
        dense_sum[k] = turned_ref[k, c] + core_scr[k]

    tiles(4, add_core)
    dense_flat = [
        send(dense_sum.at[:, :, at(across(k), span, LANES)], cross_scr.at[k - 1], flat[k - 1]) for k in (1, 2, 3)
    ]
    arrive(feed1_up)
    arrive(mix1_up)
    own1_scr[0:feed_rows, :] = feed1_ref[at(z, feed_rows, 16), :] + feed1_scr[0] + feed1_scr[1] + feed1_scr[2]
    own1_scr[feed_rows:rows, :] = mix1_ref[at(z, mix_rows, 16), :] + mix1_scr[0] + mix1_scr[1] + mix1_scr[2]
    up1 = gather_up(own1_scr, out1_ref)
    arrive(mix_flat)
    mix_sum[...] = mix0_ref[at(s, 4 * mix_rows, 16), :] + mix_scr[0] + mix_scr[1] + mix_scr[2]
    mix_up = [
        send(mix_sum.at[at(up(k), mix_rows, 16), :], mixz_scr.at[k - 1], tower[k - 1]) for k in (1, 2, 3)
    ]
    arrive(feed_up)
    own0_scr[0:feed_rows, :] = feed0_ref[at(z, feed_rows, 16), :] + feed_scr[0] + feed_scr[1] + feed_scr[2]
    arrive(mix_up)
    own0_scr[feed_rows:rows, :] = mix_sum[at(z, mix_rows, 16), :] + mixz_scr[0] + mixz_scr[1] + mixz_scr[2]
    up0 = gather_up(own0_scr, out0_ref)
    flat1 = gather_flat(out1_ref, up1)
    arrive(dense_flat)

    def add_flat(k):
        mid = dense_sum[k, :, at(s, span, LANES)]
        dense_scr[k] = mid + cross_scr[0, k] + cross_scr[1, k] + cross_scr[2, k]

    tiles(4, add_flat)
    dense_up = [send(dense_scr.at[up(k)], along_scr.at[k - 1], tower[k - 1]) for k in (1, 2, 3)]
    flat0 = gather_flat(out0_ref, up0)
    turn1 = gather_turn(out1_ref, flat1)
    arrive(dense_up)
    own_dense[...] = dense_scr[z] + along_scr[0] + along_scr[1] + along_scr[2]
    home = outd_ref.at[s]
    local_dense = keep(own_dense, home)
    spread_dense = [send(own_dense, home, peer) for peer in flat]
    total = jnp.zeros((1, 1), f32)
    for part in (own1_scr[...], own0_scr[...], own_dense[...]):
        total = total + jnp.sum(jnp.sum(part * part, 0, keepdims=True), 1, keepdims=True)
    lane = lax.broadcasted_iota(jnp.int32, (8, LANES), 1)
    own_scalar[...] = jnp.where(lane == 0, total, scalar_ref[...])
    home = outs_ref.at[c, s, z]
    local_scalar = keep(own_scalar, home)
    scalar_up = [send(own_scalar, home, peer) for peer in tower]
    local_scalar.wait()
    arrive(scalar_up)
    home = outs_ref.at[c, s]
    scalar_flat = [send(home, home, peer) for peer in flat]
    turn0 = gather_turn(out0_ref, flat0)
    core1 = gather_core(out1_ref, turn1)
    arrive(scalar_flat)
    home = outs_ref.at[c]
    scalar_core = send(home, home, core)
    core0 = gather_core(out0_ref, turn0)
    local_dense.wait()
    arrive(spread_dense)
    arrive(core1)
    arrive(core0)
    scalar_core.wait_recv()
    for copy in sent:
        copy.wait_send()


def close_exchange(feed1, mix1, feed0, mix0, turned, scalars):
    feed_rows, mix_rows = feed0.shape[0] // 4, mix0.shape[0] // 16
    rows = feed_rows + mix_rows
    width, span = turned.shape[2], SLOTS // 4
    anywhere = pl.BlockSpec(memory_space=pl.ANY)
    copies = 54
    return pl.pallas_call(
        close_body,
        in_specs=[pl.BlockSpec(memory_space=pltpu.VMEM)] * 6,
        out_specs=[anywhere] * 3,
        out_shape=[
            shape((2, 8, 4 * rows, D)), shape((4, width, span)), shape((2, 4, 4, 8, LANES)),
        ],
        scratch_shapes=[
            pltpu.VMEM((rows, D), f32),
            pltpu.VMEM((rows, D), f32),
            pltpu.VMEM((3, feed_rows, D), f32),
            pltpu.VMEM((3, mix_rows, D), f32),
            pltpu.VMEM((3, feed_rows, D), f32),
            pltpu.VMEM((3, 4 * mix_rows, D), f32),
            pltpu.VMEM((3, mix_rows, D), f32),
            pltpu.VMEM((4, width, span), f32),
            pltpu.VMEM((4, width, SLOTS), f32),
            pltpu.VMEM((3, 4, width, span), f32),
            pltpu.VMEM((3, width, span), f32),
            pltpu.VMEM((4 * mix_rows, D), f32),
            pltpu.VMEM((4, width, SLOTS), f32),
            pltpu.VMEM((width, span), f32),
            pltpu.VMEM((8, LANES), f32),
            pltpu.SemaphoreType.DMA((copies,)),
            pltpu.SemaphoreType.DMA((copies,)),
            pltpu.SemaphoreType.DMA((4,)),
        ],
        compiler_params=pltpu.CompilerParams(
            vmem_limit_bytes=60 << 20, collective_id=0, has_side_effects=True
        ),
        cost_estimate=pl.CostEstimate(flops=10_000_000, bytes_accessed=300_000_000, transcendentals=0),
    )(feed1, mix1, feed0, mix0, turned, scalars)


def turn_body(step_ref, out_ref, send_sem, recv_sem, local_sem):
    s = lax.axis_index("section")
    dp = lax.axis_index("dp")
    width = out_ref.shape[2]
    barrier = pltpu.get_barrier_semaphore()
    peers = [{"section": s, "dp": jnp.bitwise_xor(dp, k)} for k in range(8)]
    for peer in peers[1:]:
        pl.semaphore_signal(barrier, inc=1, device_id=peer, device_id_type=pl.DeviceIdType.MESH)
    pl.semaphore_wait(barrier, len(peers) - 1)

    def source(k):
        start = pl.multiple_of(jnp.bitwise_xor(dp, k) * width, 8)
        return step_ref.at[:, pl.ds(start, width), :]

    local = pltpu.make_async_copy(source(0), out_ref.at[0], local_sem)
    local.start()
    copies = []
    for k in (4, 6, 5, 7, 2, 3, 1):
        copy = pltpu.make_async_remote_copy(
            src_ref=source(k), dst_ref=out_ref.at[k], send_sem=send_sem.at[k], recv_sem=recv_sem.at[k],
            device_id=peers[k], device_id_type=pl.DeviceIdType.MESH,
        )
        copy.start()
        copies.append(copy)
    local.wait()
    for copy in copies:
        copy.wait()


def turn_exchange(step):
    layers, rows, lanes = step.shape
    return pl.pallas_call(
        turn_body,
        in_specs=[pl.BlockSpec(memory_space=pl.ANY)],
        out_specs=pl.BlockSpec(memory_space=pl.ANY),
        out_shape=shape((8, layers, rows // 8, lanes)),
        scratch_shapes=[
            pltpu.SemaphoreType.DMA((8,)), pltpu.SemaphoreType.DMA((8,)), pltpu.SemaphoreType.DMA,
        ],
        compiler_params=pltpu.CompilerParams(vmem_limit_bytes=60 << 20, collective_id=1, has_side_effects=True),
        cost_estimate=pl.CostEstimate(flops=1000, bytes_accessed=80_000_000, transcendentals=0),
    )(step)


def open_body(part_ref, out_ref, send_sem, recv_sem, local_sem):
    s = lax.axis_index("section")
    dp = lax.axis_index("dp")
    z, c = dp // 2, dp % 2
    rows = part_ref.shape[0] // 4
    core = {"section": s, "dp": jnp.bitwise_xor(dp, 1)}
    flat = [{"section": jnp.bitwise_xor(s, k), "dp": dp} for k in (1, 2)]
    tower = [{"section": s, "dp": jnp.bitwise_xor(dp, 2 * k)} for k in (1, 2, 3)]
    peers = [core, *flat, *tower]
    barrier = pltpu.get_barrier_semaphore()
    for peer in peers:
        pl.semaphore_signal(barrier, inc=1, device_id=peer, device_id_type=pl.DeviceIdType.MESH)
    pl.semaphore_wait(barrier, len(peers))
    sent = []

    def send(source, target, peer):
        n = len(sent)
        copy = pltpu.make_async_remote_copy(
            src_ref=source, dst_ref=target, send_sem=send_sem.at[n], recv_sem=recv_sem.at[n],
            device_id=peer, device_id_type=pl.DeviceIdType.MESH,
        )
        copy.start()
        sent.append(copy)
        return copy

    def place(k, across):
        return out_ref.at[jnp.bitwise_xor(z, k), c, jnp.bitwise_xor(s, across)]

    own = part_ref.at[pl.ds(pl.multiple_of(s * rows, 16), rows), :]
    upward = [send(own, place(0, 0), peer) for peer in tower]
    local = pltpu.make_async_copy(own, place(0, 0), local_sem)
    local.start()
    local.wait()
    half = rows // 32 * 16
    crossed, ended = [], []
    for k in range(4):
        if k:
            upward[k - 1].wait_recv()
        crossed.append([send(place(k, 0), place(k, 0), peer) for peer in flat])
        ended.append(send(place(k, 0), place(k, 0), core))
    for k in range(4):
        from_x, from_y = crossed[k]
        from_x.wait_recv()
        piece = place(k, 1).at[0:half]
        turned = [send(piece, piece, flat[1])]
        ended.append(send(place(k, 1), place(k, 1), core))
        from_y.wait_recv()
        piece = place(k, 2).at[half:rows]
        turned.append(send(piece, piece, flat[0]))
        ended.append(send(place(k, 2), place(k, 2), core))
        crossed[k] = turned
    for k in range(4):
        for copy in crossed[k]:
            copy.wait_recv()
        ended.append(send(place(k, 3), place(k, 3), core))
    for copy in ended:
        copy.wait_recv()
    for copy in sent:
        copy.wait_send()


def open_exchange(part):
    rows = part.shape[0]
    copies = 3 + 8 + 8 + 16
    return pl.pallas_call(
        open_body,
        in_specs=[pl.BlockSpec(memory_space=pl.ANY)],
        out_specs=pl.BlockSpec(memory_space=pl.ANY),
        out_shape=shape((4, 2, 4, rows // 4, D), bf16),
        scratch_shapes=[
            pltpu.SemaphoreType.DMA((copies,)), pltpu.SemaphoreType.DMA((copies,)), pltpu.SemaphoreType.DMA,
        ],
        compiler_params=pltpu.CompilerParams(vmem_limit_bytes=60 << 20, collective_id=2, has_side_effects=True),
        cost_estimate=pl.CostEstimate(flops=1000, bytes_accessed=80_000_000, transcendentals=0),
    )(part).reshape(8, rows, D)


def finish_body(parts, index_ref, factor_ref, found_ref, *refs):
    (wqkv_ref, wfc1_ref, eqkv_ref, efc1_ref, nqkv_ref, nfc1_ref, mqkv_ref, mfc1_ref) = refs
    scale = rate_matrix * factor_ref[0]
    for layer in range(LAYERS):
        place = 0
        for w_ref, e_ref, n_ref, a_ref in (
            (wqkv_ref, eqkv_ref, nqkv_ref, mqkv_ref), (wfc1_ref, efc1_ref, nfc1_ref, mfc1_ref)
        ):
            share = w_ref.shape[2] // parts
            for j in range(parts):
                which = jnp.bitwise_xor(index_ref[0], j)
                lanes = slice(j * share, (j + 1) * share)
                step = found_ref[which, layer, :, place : place + share]
                updated = w_ref[layer, :, lanes] - scale * step
                n_ref[layer, :, lanes] = updated
                a_ref[layer, :, lanes] = average(e_ref[layer, :, lanes], updated)
            place = place + share


def finish(parts, index, factor, found, weights, averages):
    scalar = pl.BlockSpec(memory_space=pltpu.SMEM)
    operands = [found, *weights, *averages]
    return pl.pallas_call(
        functools.partial(finish_body, parts),
        in_specs=[scalar, scalar] + [pl.BlockSpec(memory_space=pltpu.VMEM)] * len(operands),
        out_shape=[shape(x.shape) for x in (*weights, *averages)],
        compiler_params=pltpu.CompilerParams(vmem_limit_bytes=60 << 20),
        cost_estimate=pl.CostEstimate(flops=10_000_000, bytes_accessed=6_000_000, transcendentals=0),
    )(index, factor, *operands)


def adam_body(index_ref, scalar_ref, pieces_ref, *refs):
    dense, vectors, new_dense, new_vectors, turned_scr, gradient_scr = (
        refs[:4], refs[4:8], refs[8:12], refs[12:16], refs[16], refs[17]
    )
    width, count = dense[0].shape
    span = pieces_ref.shape[2]
    for k in range(pieces_ref.shape[0]):
        place = jnp.bitwise_xor(index_ref[3], k)
        lanes = pl.ds(pl.multiple_of(place * span, LANES), span)
        turned_scr[:, lanes] = pieces_ref[k, 0:width, :]
    row = lax.broadcasted_iota(jnp.int32, (EXT, TABLE), 0)
    col = lax.broadcasted_iota(jnp.int32, (EXT, TABLE), 1)
    mixed = (row % LANES) * (PIX + 1) + row // LANES == col
    mixed = jnp.where(mixed & (row % LANES < VARS), 1.0, 0.0)
    gradient_scr[:, 0:TABLE] = lax.dot_general(
        turned_scr[:, AT_TABLE:AT_VECTOR], mixed, NN, precision=highest, preferred_element_type=f32
    )
    gradient_scr[:, TABLE : TABLE + AT_HEAD + VP] = turned_scr[:, 0 : AT_HEAD + VP]

    def update(refs, news, gradient, rate, decay):
        old = [ref[...] for ref in refs]
        gradient = gradient * scalar_ref[0]
        first = beta_first * old[1] + (1.0 - beta_first) * gradient
        second = beta_second * old[2] + (1.0 - beta_second) * gradient * gradient
        first_hat = first / scalar_ref[1]
        second_hat = second / scalar_ref[2]
        updated = old[0] - rate * (first_hat / (jnp.sqrt(second_hat) + adam_eps) + decay * old[0])
        for ref, value in zip(news, (updated, first, second, average(old[3], updated))):
            ref[...] = value

    update(dense, new_dense, gradient_scr[...], rate_dense, weight_decay)
    few = vectors[0].shape[1]
    update(vectors, new_vectors, turned_scr[:, AT_VECTOR : AT_VECTOR + few], rate_vector, 0.0)


def adam(index, scalars, pieces, dense, vectors):
    scalar = pl.BlockSpec(memory_space=pltpu.SMEM)
    states = [x.T for x in (*dense, *vectors)]
    width, count = states[0].shape
    return [
        new.T
        for new in pl.pallas_call(
            adam_body,
            in_specs=[scalar, scalar] + [pl.BlockSpec(memory_space=pltpu.VMEM)] * (1 + len(states)),
            out_shape=[shape(x.shape) for x in states],
            scratch_shapes=[pltpu.VMEM((width, SLOTS), f32), pltpu.VMEM((width, count), f32)],
            compiler_params=pltpu.CompilerParams(vmem_limit_bytes=60 << 20),
            cost_estimate=pl.CostEstimate(flops=10_000_000, bytes_accessed=8_000_000, transcendentals=0),
        )(index, scalars, pieces, *states)
    ]


def digits(count, start=1):
    found = []
    while start < count:
        radix = min(4, count // start)
        found.append((start, radix))
        start *= radix
    return found


def swap(values, axis, bits):
    return lax.ppermute(values, axis, [(k, k ^ bits) for k in range(lax.axis_size(axis))])


def digit(axis, bit, radix):
    return (lax.axis_index(axis) // bit) % radix


def share_out(values, dim, axis, bit, radix):
    size = values.shape[dim] // radix
    mine = digit(axis, bit, radix)

    def part(k):
        return lax.dynamic_slice_in_dim(values, jnp.bitwise_xor(mine, k) * size, size, dim)

    arrived = [swap(part(k), axis, k * bit) for k in range(1, radix)]
    total = part(0)
    for other in arrived:
        total = total + other
    return total


def collect(values, axis, bit, radix):
    return [values] + [swap(values, axis, k * bit) for k in range(1, radix)]


def in_order(found, place):
    low = 1
    while low < len(found):
        even = (place // low) % 2 == 0
        found = [jnp.where(even, found[k], found[k ^ low]) for k in range(len(found))]
        low *= 2
    return found


def gate(values, first):
    return lax.optimization_barrier((values, first))


def advance(values, sums):
    moved = [share_out(part, 0, *stages[0]) if stages else part for part, stages in sums]
    values, moved = gate(values, moved)
    return values, [[part, stages[1:]] for part, (unused, stages) in zip(moved, sums)]


def total_of(values, stages):
    for axis, bit, radix in stages:
        values = sum(in_order(collect(values, axis, bit, radix), digit(axis, bit, radix)))
    return values


def valid_flags(counts):
    var_index = jnp.arange(VARS)
    level_index = (var_index - SURF) % LEVELS
    inside = (var_index[None, :] < SURF) | (level_index[None, :] < counts[:, None])
    return jnp.where(inside, 1.0, 0.0).astype(f32)


def cosine_table():
    pixel_rows = 2 * LAT_ROWS
    latitude = (np.arange(pixel_rows) + 0.5) * (np.pi / pixel_rows) - 0.5 * np.pi
    cosine = np.cos(latitude)
    cosine = cosine / np.mean(cosine)
    by_row = cosine.reshape(LAT_ROWS, 2).repeat(LON_COLS, 0)
    return by_row.astype(np.float32), float(by_row.sum() * (PIX // 2))


def average(old_state, new_state):
    return ema_beta * old_state + (1.0 - ema_beta) * new_state


def column_blocks(part):
    rows, cols = part.shape
    return part.reshape(rows, cols // D, D).transpose(1, 0, 2).reshape(-1, D)


def pack_layer(parts):
    qkv, out, fc1, fc2 = [part.astype(bf16) for part in parts]
    return jnp.concatenate([column_blocks(qkv), out, column_blocks(fc1), fc2], 0)


def unpack_layer(full, rows):
    above = full[:, : rows * 8].reshape(-1, 8, rows, D).transpose(1, 0, 2, 3).reshape(8 * D, D)
    return jnp.concatenate([above, full[:, rows * 8 :].reshape(FF, D)], 0)


def per_device(
    fields, targets, level_count, step_count,
    dense, dense_m, dense_v, dense_ema, vectors, vectors_m, vectors_v, vectors_ema,
    w_qkv, w_out, w_fc1, w_fc2, ema_qkv, ema_out, ema_fc1, ema_fc2,
    stat_small, stat_qkv, stat_wide, root_small, root_qkv, root_wide,
):
    section = lax.axis_index("section")
    sections = lax.axis_size("section")
    dp_index = lax.axis_index("dp")
    parts = lax.axis_size("dp")
    direct = sections == 4 and parts == 8
    rows_dense = dense.shape[0]
    width = D // parts
    both_rows = jnp.concatenate([dense, vectors], 0).astype(bf16)
    packed = [pack_layer([part[layer] for part in (w_qkv, w_out, w_fc1, w_fc2)]) for layer in range(LAYERS)]
    layer_weights = []
    if direct:
        slots = -(-both_rows.shape[0] // LANES) * LANES
        turned = jnp.pad(both_rows, ((0, slots - both_rows.shape[0]), (0, 0))).T
        first = turned.size // D
        before = open_exchange(jnp.concatenate([turned.reshape(first, D), packed[0]], 0))
        full_dense = before[:, :first].reshape(D, slots).T
        layer_weights.append(before)
        packed = packed[1:]
    else:
        full_dense = lax.all_gather(both_rows, "dp", axis=1, tiled=True)
        before = full_dense
    for part in packed:
        part, before = gate(part, before)
        if not layer_weights:
            full_dense = before
        elif not direct:
            layer_weights[-1] = before
        before = lax.all_gather(part, "dp", axis=0)
        layer_weights.append(before)
    near, layer_weights[-1] = gate(root_small, layer_weights[-1])
    around = lax.all_gather(near[:, np.array([0, 2, 3, 4])], "dp", axis=2, tiled=True)
    if direct:
        layer_weights = list(zip(layer_weights, [first] + [0] * (LAYERS - 1)))
    else:
        layer_weights = [unpack_layer(full, w_qkv.shape[1]) for full in layer_weights]
    gain_rows = full_dense[rows_dense : rows_dense + vectors.shape[0]].astype(f32)
    micro_count = fields.shape[0]
    table = full_dense[:TABLE].reshape(VARS, PIX + 1, D).transpose(1, 0, 2)
    table = jnp.pad(table, ((0, 0), (0, LANES - VARS), (0, 0))).reshape(EXT, D)
    position = full_dense[TABLE : TABLE + SEQ]
    proj = full_dense[TABLE + SEQ : TABLE + SEQ + D]
    head_rows = full_dense[TABLE + SEQ + D : rows_dense]
    flags = valid_flags(level_count)
    by_row, row_total = cosine_table()
    weight_local = jnp.sum(flags) * row_total
    cosines = jnp.asarray(by_row)

    core = [("dp", 1, 2)]
    cross = [("section", bit, radix) for bit, radix in digits(sections)]
    along = [("dp", bit, radix) for bit, radix in digits(parts, 2)]
    turns = -(-micro_count // sections)
    turned, error_sum, d_mats = 0.0, 0.0, [0.0] * (2 * LAYERS)
    pending, ready = [], []
    for turn in range(turns):
        index = turn * sections + section
        active = jnp.where(index < micro_count, 1.0, 0.0).astype(f32)
        index = jnp.minimum(index, micro_count - 1)
        field_rows = lax.dynamic_index_in_dim(fields, index, 0, False)
        target = lax.dynamic_index_in_dim(targets, index, 0, False)
        flag_row = lax.dynamic_index_in_dim(flags, index, 0, True)
        valid_vars = jnp.pad(flag_row, ((0, 0), (0, LANES - VARS)), constant_values=-1.0)
        valid_values = jnp.repeat(flag_row * active, PIX, axis=1)
        x, agg = embed_forward(field_rows, table, gain_rows[0:1], valid_vars, proj, position)
        kept = []
        for layer in range(LAYERS):
            gains = gain_rows[1 + 2 * layer : 3 + 2 * layer]
            if direct:
                layer_weights[layer], *saved, y = block_forward(x, gains, *layer_weights[layer])
            else:
                *saved, y = block_forward(x, gains, layer_weights[layer])
            kept.append((x, saved))
            x = y
        grad, d_head, d_final, errors = head_step(
            x, gain_rows[2 * LAYERS + 1 :], head_rows, target, cosines, valid_values
        )
        d_gains = [None] * (2 * LAYERS)
        for layer in reversed(range(LAYERS)):
            gains = gain_rows[1 + 2 * layer : 3 + 2 * layer]
            x, (h, qkv, o, lse, m, h2) = kept[layer]
            grad, pending = advance(grad, pending)
            pending, ready = pending + ready, []
            dm, do, d_gains[2 * layer + 1], found = feed_back(h2, m, grad, gains, layer_weights[layer])
            d_mats[2 * layer + 1] = d_mats[2 * layer + 1] + found if turn else found
            if turn == turns - 1:
                ready = [[d_mats[2 * layer + 1], core + cross]]
            do, pending = advance(do, pending)
            pending, ready = pending + ready, []
            grad, d_gains[2 * layer], found = mix_back(
                x, (h, qkv, o, lse), dm, do, gains, layer_weights[layer]
            )
            d_mats[2 * layer] = d_mats[2 * layer] + found if turn else found
            if turn == turns - 1:
                ready = [[d_mats[2 * layer], core + cross]]
        grad, pending = advance(grad, pending)
        pending, ready = pending + ready, []
        d_vectors = jnp.concatenate(
            [jnp.zeros((1, D), f32), *d_gains, d_final, jnp.zeros((6 - 2 * LAYERS, D), f32)], 0
        )
        found = embed_back(
            field_rows, table, gain_rows[0:1], valid_vars, proj, agg, grad, d_head, d_vectors
        )
        turned = turned + found if turn else found
        error_sum = error_sum + jnp.sum(errors)

    turned, pending = advance(turned, pending)
    width = D // parts
    scalars = jnp.stack([jnp.zeros((), f32), error_sum, jnp.where(section == 0, weight_local, 0.0)])
    scalars = jnp.broadcast_to(jnp.pad(scalars, (0, LANES - 3))[None], (8, LANES))
    if direct:
        feed1, mix1, feed0, mix0 = [part for part, unused in pending]
        pieces, dense_pieces, scalars = close_exchange(
            feed1, mix1, feed0, mix0, turned.reshape(parts // 2, 2, width, SLOTS), scalars
        )
        scalars = jnp.sum(scalars, (0, 1, 2))
        runs, places = parts // 2, [0, 0, 0]
    else:
        own_mats = []
        for part, stages in pending:
            for stage in stages + along:
                part = share_out(part, 0, *stage)
            own_mats.append(part)
        own_dense = turned
        for axis, bit, radix in core:
            own_dense = share_out(own_dense.reshape(-1, radix, width, SLOTS), 1, axis, bit, radix)
        for axis, bit, radix in cross:
            own_dense = share_out(own_dense, 3, axis, bit, radix)
        for axis, bit, radix in along:
            own_dense = share_out(own_dense.reshape(-1, radix, width, own_dense.shape[3]), 1, axis, bit, radix)
        own_dense = own_dense.reshape(width, -1)

        square_own = sum(jnp.sum(part * part) for part in [own_dense] + own_mats)
        scalars = jnp.where(jnp.arange(LANES) == 0, square_own, scalars)
        scalars = total_of(scalars, core + cross + along)

        pieces = []
        for tall_part, wide_part in zip(own_mats[1::2], own_mats[::2]):
            if len(along) == 1 and wide_part.shape[0] % 16 == 0 and tall_part.shape[0] % 16 == 0:
                runs = along[0][2]
                part = jnp.concatenate(collect(jnp.concatenate([wide_part, tall_part], 0), *along[0]), 0)
            else:
                runs = 1
                for stage in reversed(along):
                    turn_at = digit(*stage)
                    wide_part = jnp.concatenate(in_order(collect(wide_part, *stage), turn_at), 0)
                    tall_part = jnp.concatenate(in_order(collect(tall_part, *stage), turn_at), 0)
                part = jnp.concatenate([wide_part, tall_part], 0)
            found = [part]
            for stage in (cross + core if len(cross) == 1 else cross[::-1] + core):
                rounds = [collect(part, *stage) for part in found]
                found = [rounds[j][k] for k in range(stage[2]) for j in range(len(rounds))]
            pieces.insert(0, found)
        fill = -width % 8
        dense_pieces = [jnp.pad(own_dense, ((0, fill), (0, 0)))]
        for stage in cross[::-1]:
            rounds = [collect(part, *stage) for part in dense_pieces]
            dense_pieces = [rounds[j][k] for k in range(stage[2]) for j in range(len(rounds))]
        dense_pieces = jnp.stack(dense_pieces)
        pieces = jnp.stack([jnp.stack(found) for found in pieces])
        places = [(dp_index % 2) * sections + section, dp_index // 2 if runs > 1 else 0, section]

    square_total, error_total, weight_total = scalars[0, 0], scalars[0, 1], scalars[0, 2]
    grad_norm = jnp.sqrt(square_total) / weight_total
    factor = jnp.minimum(1.0, clip_level / grad_norm) / weight_total
    steps_done = step_count[0].astype(f32)
    corrections = [1.0 - jnp.power(beta, steps_done) for beta in (beta_first, beta_second)]
    index = jnp.stack([jnp.asarray(k, jnp.int32) for k in (dp_index, *places)])
    (
        dense_new, dense_m_new, dense_v_new, dense_ema_new,
        vectors_new, vectors_m_new, vectors_v_new, vectors_ema_new,
    ) = adam(
        index, jnp.stack([factor, *corrections]), dense_pieces,
        (dense, dense_m, dense_v, dense_ema), (vectors, vectors_m, vectors_v, vectors_ema),
    )

    (
        stat_small_new, stat_qkv_new, stat_wide_new, out_new, fc2_new, ema_out_new, ema_fc2_new, step,
    ) = shampoo(
        pieces, runs, index, factor.reshape(1), (stat_small, stat_qkv, stat_wide), around,
        (root_small, root_qkv, root_wide), (w_out, w_fc2), (ema_out, ema_fc2),
    )
    if direct:
        arrived = turn_exchange(step)
    else:
        step = step.reshape(LAYERS, parts, width, -1)
        sent = [
            lax.dynamic_index_in_dim(step, jnp.bitwise_xor(dp_index, k), 1, False) for k in range(parts)
        ]
        arrived = jnp.stack([swap(part, "dp", k) if k else part for k, part in enumerate(sent)])
    qkv_new, fc1_new, ema_qkv_new, ema_fc1_new = finish(
        parts, index, factor.reshape(1), arrived, (w_qkv, w_fc1), (ema_qkv, ema_fc1)
    )
    return (
        error_total / weight_total,
        grad_norm,
        dense_new,
        dense_m_new,
        dense_v_new,
        dense_ema_new,
        vectors_new,
        vectors_m_new,
        vectors_v_new,
        vectors_ema_new,
        qkv_new,
        out_new,
        fc1_new,
        fc2_new,
        ema_qkv_new,
        ema_out_new,
        ema_fc1_new,
        ema_fc2_new,
        stat_small_new,
        stat_qkv_new,
        stat_wide_new,
    )


def solution(mesh):
    items = P("dp", None, None)
    columns = P(None, "dp")
    matrix = P(None, "dp", None)
    stacked = P(None, None, "dp", None)
    return jax.shard_map(
        per_device,
        mesh=mesh,
        in_specs=(
            (items, items, P("dp"), P())
            + (columns,) * 8
            + (matrix,) * 8
            + (stacked, matrix, stacked) * 2
        ),
        out_specs=(P(), P()) + (columns,) * 8 + (matrix,) * 8 + (stacked, matrix, stacked),
        check_vma=False,
    )
```

```python
import functools
import math

import jax
import jax.numpy as jnp
import numpy as np
from jax import lax
from jax.experimental import pallas as pl
from jax.experimental.pallas import tpu as pltpu
from jax.sharding import PartitionSpec as P

D = 384
HEADS = 6
HDIM = 64
SURF = 4
LEVELS = 13
VARS = 69
PIX = 4
VP = 276
LAT_ROWS = 64
LON_COLS = 16
SEQ = 1024
LAYERS = 2
FF = 1536
BLOCKS = 4 + 2 * (FF // D)

LANES = 128
PAIRS = HEADS // 2
EXT = (PIX + 1) * LANES
TABLE = VARS * (PIX + 1)

AT_PROJ = SEQ
AT_HEAD = AT_PROJ + D
AT_TABLE = AT_HEAD + 3 * LANES
AT_VECTOR = AT_TABLE + EXT
SLOTS = AT_VECTOR + LANES

highest = lax.Precision.HIGHEST
f32 = jnp.float32
bf16 = jnp.bfloat16
norm_eps = 1e-05
clip_level = 0.001
rate_dense = 0.05
rate_vector = 0.2
rate_matrix = 0.5
beta_first = 0.9
beta_second = 0.95
adam_eps = 1e-08
weight_decay = 0.1
stat_beta = 0.95
ema_beta = 0.9
LOG2E = math.log2(math.e)
SCALE2 = LOG2E * HDIM ** (-0.5)

NN = (((1,), (0,)), ((), ()))
NT = (((1,), (1,)), ((), ()))
TN = (((0,), (0,)), ((), ()))


def dot(left, right, dims=NN):
    return lax.dot_general(left, right, dims, preferred_element_type=f32)


def halves(value):
    high = value.astype(bf16)
    return high, (value - high.astype(f32)).astype(bf16)


def call(body, out_shape, scratch=(), vmem=60 << 20, flops=0, traffic=0):
    return pl.pallas_call(
        body,
        out_shape=out_shape,
        scratch_shapes=list(scratch),
        compiler_params=pltpu.CompilerParams(vmem_limit_bytes=vmem),
        cost_estimate=pl.CostEstimate(flops=flops, bytes_accessed=traffic, transcendentals=0),
    )


def shape(dims, kind=f32):
    return jax.ShapeDtypeStruct(dims, kind)


def norm_parts(values):
    center = values - jnp.mean(values, -1, keepdims=True)
    spread = jnp.mean(center * center, -1, keepdims=True)
    inverse = lax.rsqrt(spread + norm_eps)
    return center * inverse, inverse


def norm_back(values, gain, upstream):
    unit, inverse = norm_parts(values)
    scaled = upstream * gain
    back = inverse * (
        scaled
        - jnp.mean(scaled, -1, keepdims=True)
        - unit * jnp.mean(scaled * unit, -1, keepdims=True)
    )
    return back, jnp.sum(upstream * unit, 0, keepdims=True)


def tiles(count, body):
    def step(index, carry):
        body(index)
        return carry

    lax.fori_loop(0, count, step, 0)


def rows_of(index, size):
    return pl.ds(pl.multiple_of(index * size, size), size)


def head_mask(rows, which):
    lane = lax.broadcasted_iota(jnp.int32, (rows, LANES), 1)
    return (lane >= which * HDIM) & (lane < (which + 1) * HDIM)


def spread_fields(field_rows):
    row = lax.broadcasted_iota(jnp.int32, (VP, PIX * LANES), 0)
    col = lax.broadcasted_iota(jnp.int32, (VP, PIX * LANES), 1)
    var, pixel = col % LANES, col // LANES
    chosen = (row == PIX * var + pixel) & (var < VARS)
    return dot(field_rows, jnp.where(chosen, 1.0, 0.0).astype(bf16))


def query_mask(query_row):
    head = lax.broadcasted_iota(jnp.int32, (8, D), 0)
    lane = lax.broadcasted_iota(jnp.int32, (8, D), 1)
    return jnp.where(lane // HDIM == head, query_row * HDIM ** (-0.5), 0.0)


def query_scores(table_ref, mask, query_scr):
    for j in range(PIX + 1):
        part = table_ref[j * LANES : (j + 1) * LANES, :]
        query_scr[j * 8 : (j + 1) * 8, :] = dot(mask.astype(bf16), part, NT)


def mix_weights(extended, query_scr, head, valid):
    score = query_scr[pl.ds(PIX * 8 + head, 1), :]
    for j in range(PIX):
        score = score + extended[j] * query_scr[pl.ds(j * 8 + head, 1), :]
    score = jnp.where(valid > 0, score, jnp.where(valid < 0, -jnp.inf, -1e9))
    peak = jnp.max(score, -1, keepdims=True)
    weight = jnp.exp(score - peak)
    return weight / jnp.sum(weight, -1, keepdims=True)


def embed_body(field_ref, table_ref, query_ref, valid_ref, proj_ref, pos_ref, out_ref, agg_ref, query_scr):
    size = 256
    query_scores(table_ref, query_mask(query_ref[...]), query_scr)

    def tile(index):
        rows = rows_of(index, size)
        wide = spread_fields(field_ref[rows, :])
        extended = [wide[:, j * LANES : (j + 1) * LANES] for j in range(PIX)]
        valid = valid_ref[...]

        def pair(hp, carry):
            lanes = rows_of(hp, LANES)
            table = table_ref[:, lanes]
            total = jnp.zeros((size, LANES), f32)
            for which in range(2):
                weight = mix_weights(extended, query_scr, 2 * hp + which, valid)
                mixing = jnp.concatenate([weight * extended[j] for j in range(PIX)] + [weight], 1)
                own = jnp.where(head_mask(EXT, which), table, jnp.zeros_like(table))
                high, low = halves(mixing)
                total = total + dot(high, own) + dot(low, own)
            agg_ref[rows, lanes] = total.astype(bf16)
            return carry

        lax.fori_loop(0, PAIRS, pair, 0)
        out_ref[rows, :] = (dot(agg_ref[rows, :], proj_ref[...]) + pos_ref[rows, :].astype(f32)).astype(bf16)

    tiles(SEQ // size, tile)


def embed_forward(field_rows, table, query_row, valid, proj, position):
    return call(
        embed_body,
        (shape((SEQ, D), bf16), shape((SEQ, D), bf16)),
        [pltpu.VMEM((40, LANES), f32)],
        flops=4_000_000_000,
        traffic=4_000_000,
    )(field_rows, table, query_row, valid, proj, position)


def embed_back_body(
    field_ref, table_ref, query_ref, valid_ref, proj_ref, agg_ref, grad_ref, dhead_ref, dvector_ref,
    out_ref, vector_scr, query_scr, wide_scr, merged_scr, high_scr, low_scr, dscore_scr,
):
    size = 256
    mask = query_mask(query_ref[...])
    query_scores(table_ref, mask, query_scr)
    out_ref[:, AT_PROJ : AT_PROJ + D] = dot(grad_ref[...], agg_ref[...], TN)
    out_ref[:, AT_HEAD:AT_TABLE] = jnp.zeros((D, AT_TABLE - AT_HEAD), f32)
    out_ref[:, AT_HEAD : AT_HEAD + VP] = dhead_ref[...]
    dscore_scr[...] = jnp.zeros_like(dscore_scr)

    def prepare(index):
        rows = rows_of(index, size)
        wide_scr[rows, :] = spread_fields(field_ref[rows, :])
        merged_scr[rows, :] = dot(grad_ref[rows, :], proj_ref[...], NT)
        out_ref[:, rows] = grad_ref[rows, :].astype(f32).T

    tiles(SEQ // size, prepare)

    def pair(hp):
        lanes = rows_of(hp, LANES)
        table = table_ref[:, lanes]
        total = jnp.zeros((LANES, EXT), f32)
        for which in range(2):
            head = 2 * hp + which
            own = jnp.where(head_mask(EXT, which), table, jnp.zeros_like(table))
            twice = jnp.concatenate([own, own], 1)

            def tile(index):
                rows = rows_of(index, size)
                extended = [wide_scr[rows, j * LANES : (j + 1) * LANES] for j in range(PIX)]
                weight = mix_weights(extended, query_scr, head, valid_ref[...])
                mixing = jnp.concatenate([weight * extended[j] for j in range(PIX)] + [weight], 1)
                high, low = halves(mixing)
                high_scr[rows, :] = high
                low_scr[rows, :] = low
                grad_high, grad_low = halves(merged_scr[rows, lanes])
                dmix = dot(jnp.concatenate([grad_high, grad_low], 1), twice, NT)
                dweight = dmix[:, PIX * LANES :]
                for j in range(PIX):
                    dweight = dweight + dmix[:, j * LANES : (j + 1) * LANES] * extended[j]
                dscore = weight * (dweight - jnp.sum(weight * dweight, -1, keepdims=True))
                for j in range(PIX + 1):
                    piece = dscore * extended[j] if j < PIX else dscore
                    at = pl.ds(j * 8 + head, 1)
                    dscore_scr[at, :] = dscore_scr[at, :] + jnp.sum(piece, 0, keepdims=True)

            tiles(SEQ // size, tile)
            grad_high, grad_low = halves(merged_scr[:, lanes])
            keep = head_mask(SEQ, which)
            grad_high = jnp.where(keep, grad_high, jnp.zeros_like(grad_high))
            grad_low = jnp.where(keep, grad_low, jnp.zeros_like(grad_low))
            both = dot(jnp.concatenate([grad_high, grad_low], 1), high_scr[...], TN)
            total = total + both[:LANES, :] + both[LANES:, :] + dot(grad_high, low_scr[...], TN)
        out_ref[lanes, AT_TABLE:AT_VECTOR] = total

    tiles(PAIRS, pair)
    dquery = jnp.zeros((1, D), f32)
    head = lax.broadcasted_iota(jnp.int32, (8, D), 0)
    lane = lax.broadcasted_iota(jnp.int32, (8, D), 1)
    for j in range(PIX + 1):
        part = dscore_scr[j * 8 : (j + 1) * 8, :]
        block = slice(j * LANES, (j + 1) * LANES)
        lanes = slice(AT_TABLE + j * LANES, AT_TABLE + (j + 1) * LANES)
        out_ref[:, lanes] = out_ref[:, lanes] + lax.dot_general(
            mask, part, TN, precision=highest, preferred_element_type=f32
        )
        spread = lax.dot_general(
            part, table_ref[block, :].astype(f32), NN, precision=highest, preferred_element_type=f32
        )
        dquery = dquery + jnp.sum(jnp.where(lane // HDIM == head, spread, 0.0), 0, keepdims=True)
    vector_scr[...] = jnp.zeros_like(vector_scr)
    vector_scr[0:8, :] = dvector_ref[...]
    vector_scr[0:1, :] = dquery * HDIM ** (-0.5)
    out_ref[:, AT_VECTOR:SLOTS] = vector_scr[...].T


def embed_back(field_rows, table, query_row, valid, proj, agg, grad, dhead, dvector):
    return call(
        embed_back_body,
        shape((D, SLOTS)),
        [
            pltpu.VMEM((LANES, D), f32),
            pltpu.VMEM((40, LANES), f32),
            pltpu.VMEM((SEQ, PIX * LANES), f32),
            pltpu.VMEM((SEQ, D), f32),
            pltpu.VMEM((SEQ, EXT), bf16),
            pltpu.VMEM((SEQ, EXT), bf16),
            pltpu.VMEM((40, LANES), f32),
        ],
        flops=12_000_000_000,
        traffic=6_000_000,
    )(field_rows, table, query_row, valid, proj, agg, grad, dhead, dvector)


def square(ref, index):
    return ref[index * D : (index + 1) * D, :]


def block_body(start, x_ref, gain_ref, packed_ref, *refs):
    *refs, m_ref, h2_ref, y_ref = refs[: 7 if start is None else 8]
    if start is None:
        w_ref = packed_ref
        h_ref, qkv_ref, o_ref, lse_ref = refs
    else:
        w_ref, h_ref, qkv_ref, o_ref, lse_ref = refs
        shards = packed_ref.shape[0]
        rows, tall = D // shards, FF // shards
        above = BLOCKS - FF // D
        for k in range(shards):
            for b in range(above):
                at = start + b * rows
                w_ref[b * D + k * rows : b * D + (k + 1) * rows, :] = packed_ref[k, at : at + rows, :]
            at = start + above * rows
            to = above * D + k * tall
            w_ref[to : to + tall, :] = packed_ref[k, at : at + tall, :]
    size = 256

    def enter(index):
        rows = rows_of(index, size)
        unit, unused = norm_parts(x_ref[rows, :].astype(f32))
        hidden = (unit * gain_ref[0:1, :]).astype(bf16)
        h_ref[rows, :] = hidden
        for b in range(3):
            qkv_ref[rows, b * D : (b + 1) * D] = dot(hidden, square(w_ref, b)).astype(bf16)

    tiles(SEQ // size, enter)
    lse_ref[...] = jnp.zeros_like(lse_ref)

    def pair(hp):
        keys = qkv_ref[:, pl.ds(pl.multiple_of(D + hp * LANES, LANES), LANES)]
        values = qkv_ref[:, pl.ds(pl.multiple_of(2 * D + hp * LANES, LANES), LANES)]

        def tile(index):
            rows = rows_of(index, size)
            queries = qkv_ref[rows, rows_of(hp, LANES)]
            parts = []
            for which in range(2):
                own = jnp.where(head_mask(size, which), queries, jnp.zeros_like(queries))
                score = dot(keys, own, NT) * SCALE2
                peak = jnp.max(score, 0, keepdims=True)
                power = jnp.exp2(score - peak)
                total = jnp.sum(power, 0, keepdims=True)
                chance = (power * (1.0 / total)).astype(bf16)
                mixed = dot(values, chance, TN)
                parts.append(mixed[which * HDIM : (which + 1) * HDIM, :])
                lse_ref[pl.ds(2 * hp + which, 1), rows] = peak + jnp.log2(total)
            o_ref[rows, rows_of(hp, LANES)] = jnp.concatenate(parts, 0).T.astype(bf16)

        tiles(SEQ // size, tile)

    tiles(PAIRS, pair)

    def leave(index):
        rows = rows_of(index, size)
        middle = x_ref[rows, :].astype(f32) + dot(o_ref[rows, :], square(w_ref, 3))
        m_ref[rows, :] = middle
        unit, unused = norm_parts(middle)
        hidden = (unit * gain_ref[1:2, :]).astype(bf16)
        h2_ref[rows, :] = hidden
        total = jnp.zeros((size, D), f32)
        for b in range(FF // D):
            before = dot(hidden, square(w_ref, 4 + b))
            active = (0.5 * before * (1.0 + lax.erf(before * math.sqrt(0.5)))).astype(bf16)
            total = total + dot(active, square(w_ref, 8 + b))
        y_ref[rows, :] = (middle + total).astype(bf16)

    tiles(SEQ // size, leave)


def block_forward(x, gains, weights, start=None):
    return call(
        functools.partial(block_body, start),
        (() if start is None else (shape((BLOCKS * D, D), bf16),))
        + (
            shape((SEQ, D), bf16),
            shape((SEQ, 3 * D), bf16),
            shape((SEQ, D), bf16),
            shape((8, SEQ)),
            shape((SEQ, D)),
            shape((SEQ, D), bf16),
            shape((SEQ, D), bf16),
        ),
        flops=12_000_000_000,
        traffic=12_000_000,
    )(x, gains, weights)


def feed_back_body(h2_ref, m_ref, dy_ref, gain_ref, w_ref, dm_ref, do_ref, dgain_ref, dw_ref, r_scr, df_scr):
    size = 256
    dgain_ref[...] = jnp.zeros_like(dgain_ref)

    def first(index):
        rows = rows_of(index, size)
        grad_next = dy_ref[rows, :]
        hidden = h2_ref[rows, :]
        upstream = jnp.zeros((size, D), f32)
        for b in range(FF // D):
            cols = slice(b * D, (b + 1) * D)
            before = dot(hidden, square(w_ref, 4 + b))
            upper = 0.5 * (1.0 + lax.erf(before * math.sqrt(0.5)))
            r_scr[rows, cols] = (before * upper).astype(bf16)
            slope = upper + before * (jnp.exp2(before * before * (-0.5 * LOG2E)) * (1.0 / math.sqrt(2 * math.pi)))
            grad_before = (dot(grad_next, square(w_ref, 8 + b), NT) * slope).astype(bf16)
            df_scr[rows, cols] = grad_before
            upstream = upstream + dot(grad_before, square(w_ref, 4 + b), NT)
        back, dgain = norm_back(m_ref[rows, :], gain_ref[1:2, :], upstream)
        dgain_ref[...] = dgain_ref[...] + dgain
        middle = grad_next.astype(f32) + back
        dm_ref[rows, :] = middle
        do_ref[rows, :] = dot(middle.astype(bf16), square(w_ref, 3), NT).astype(bf16)

    tiles(SEQ // size, first)

    def wide(index):
        cols = rows_of(index, D)
        dw_ref[rows_of(index, D), :] = dot(h2_ref[...], df_scr[:, cols], TN)
        dw_ref[rows_of(FF // D + index, D), :] = dot(r_scr[:, cols], dy_ref[...], TN)

    tiles(FF // D, wide)


def feed_back(h2, m, dy, gains, weights):
    return call(
        feed_back_body,
        (shape((SEQ, D)), shape((SEQ, D), bf16), shape((1, D)), shape((2 * FF, D))),
        [pltpu.VMEM((SEQ, FF), bf16), pltpu.VMEM((SEQ, FF), bf16)],
        flops=17_000_000_000,
        traffic=14_000_000,
    )(h2, m, dy, gains, weights)


def mix_back_body(x_ref, h_ref, qkv_ref, o_ref, lse_ref, dm_ref, do_ref, gain_ref, w_ref,
                  dx_ref, dgain_ref, dw_ref, dqkv_scr, dkv_scr):
    size = 256
    dgain_ref[...] = jnp.zeros_like(dgain_ref)
    dw_ref[3 * D : 4 * D, :] = dot(o_ref[...], dm_ref[...].astype(bf16), TN)

    def pair(hp):
        lanes = rows_of(hp, LANES)
        klanes = pl.ds(pl.multiple_of(D + hp * LANES, LANES), LANES)
        vlanes = pl.ds(pl.multiple_of(2 * D + hp * LANES, LANES), LANES)
        keys = qkv_ref[:, klanes]
        values = qkv_ref[:, vlanes]
        dkv_scr[...] = jnp.zeros_like(dkv_scr)

        def tile(index):
            rows = rows_of(index, size)
            queries = qkv_ref[rows, lanes]
            upstream = do_ref[rows, lanes]
            parts = []
            for which in range(2):
                keep = head_mask(size, which)
                own = jnp.where(keep, queries, jnp.zeros_like(queries))
                own_up = jnp.where(keep, upstream, jnp.zeros_like(upstream))
                score = dot(keys, own, NT) * SCALE2
                chance = jnp.exp2(score - lse_ref[pl.ds(2 * hp + which, 1), rows])
                dchance = dot(values, own_up, NT)
                shift = jnp.sum(dchance * chance, 0, keepdims=True)
                dscore = (chance * (dchance - shift)).astype(bf16)
                dkv_scr[:, :LANES] = dkv_scr[:, :LANES] + dot(dscore, own)
                dkv_scr[:, LANES:] = dkv_scr[:, LANES:] + dot(chance.astype(bf16), own_up)
                dquery = dot(keys, dscore, TN)
                parts.append(dquery[which * HDIM : (which + 1) * HDIM, :])
            dqkv_scr[rows, lanes] = (jnp.concatenate(parts, 0).T * HDIM ** (-0.5)).astype(bf16)

        tiles(SEQ // size, tile)
        dqkv_scr[:, klanes] = (dkv_scr[:, :LANES] * HDIM ** (-0.5)).astype(bf16)
        dqkv_scr[:, vlanes] = dkv_scr[:, LANES:].astype(bf16)

    tiles(PAIRS, pair)

    def third(index):
        cols = rows_of(index, D)
        dw_ref[cols, :] = dot(h_ref[...], dqkv_scr[:, cols], TN)

    tiles(3, third)

    def last(index):
        rows = rows_of(index, size)
        upstream = jnp.zeros((size, D), f32)
        for b in range(3):
            upstream = upstream + dot(dqkv_scr[rows, b * D : (b + 1) * D], square(w_ref, b), NT)
        back, dgain = norm_back(x_ref[rows, :].astype(f32), gain_ref[0:1, :], upstream)
        dgain_ref[...] = dgain_ref[...] + dgain
        dx_ref[rows, :] = (dm_ref[rows, :] + back).astype(bf16)

    tiles(SEQ // size, last)


def mix_back(x, kept, dm, do, gains, weights):
    return call(
        mix_back_body,
        (shape((SEQ, D), bf16), shape((1, D)), shape((4 * D, D))),
        [pltpu.VMEM((SEQ, 3 * D), bf16), pltpu.VMEM((SEQ, 2 * LANES), f32)],
        flops=17_000_000_000,
        traffic=14_000_000,
    )(x, *kept, dm, do, gains, weights)


def head_body(y_ref, gain_ref, head_ref, target_ref, cos_ref, valid_ref,
              dy_ref, dhead_ref, dgain_ref, error_ref, h_scr, dp_scr):
    size = 256
    dgain_ref[...] = jnp.zeros_like(dgain_ref)
    error_ref[...] = jnp.zeros_like(error_ref)

    def tile(index):
        rows = rows_of(index, size)
        values = y_ref[rows, :].astype(f32)
        unit, unused = norm_parts(values)
        hidden = (unit * gain_ref[...]).astype(bf16)
        h_scr[rows, :] = hidden
        residual = dot(hidden, head_ref[...], NT) - target_ref[rows, :].astype(f32)
        lane = lax.broadcasted_iota(jnp.int32, (size, VP), 1)
        cosine = jnp.where(lane % PIX < 2, cos_ref[rows, 0:1], cos_ref[rows, 1:2])
        weight = cosine * valid_ref[...]
        error_ref[...] = error_ref[...] + jnp.sum(weight * residual * residual, 0, keepdims=True)
        grad = (2.0 * weight * residual).astype(bf16)
        dp_scr[rows, :] = grad
        back, dgain = norm_back(values, gain_ref[...], dot(grad, head_ref[...]))
        dgain_ref[...] = dgain_ref[...] + dgain
        dy_ref[rows, :] = back.astype(bf16)

    tiles(SEQ // size, tile)
    dhead_ref[...] = dot(h_scr[...], dp_scr[...], TN)


def head_step(y, gain, head_rows, target, cosines, valid):
    return call(
        head_body,
        (shape((SEQ, D), bf16), shape((D, VP)), shape((1, D)), shape((1, VP))),
        [pltpu.VMEM((SEQ, D), bf16), pltpu.VMEM((SEQ, VP), bf16)],
        flops=700_000_000,
        traffic=4_000_000,
    )(y, gain, head_rows, target, cosines, valid)


def dot3(left, right, dims=NN):
    return dot(left[0], right[0], dims) + dot(left[0], right[1], dims) + dot(left[1], right[0], dims)


def chosen_rows(count, width, start, offset):
    row = lax.broadcasted_iota(jnp.int32, (count, width), 0)
    col = lax.broadcasted_iota(jnp.int32, (count, width), 1)
    return jnp.where(col + offset == row + start, 1.0, 0.0).astype(bf16)


def pick(selector, pair, dims=NN):
    return [dot(selector, part, dims).astype(bf16) for part in pair]


def shampoo_body(along, index_ref, factor_ref, small_ref, qkv_ref, wide_ref, around_ref,
                 left_out_ref, left_fc2_ref, right_qkv_ref, right_fc1_ref,
                 wout_ref, wfc2_ref, eout_ref, efc2_ref, piece_ref,
                 nsmall_ref, nqkv_ref, nwide_ref, nout_ref, nfc2_ref, meout_ref, mefc2_ref,
                 step_ref, high_scr, low_scr):
    pieces = piece_ref.shape[1]
    me = index_ref[0]
    factor = factor_ref[0]
    wide_rows, tall_rows = 2 * FF // (pieces * along), 4 * D // (pieces * along)
    for k in range(pieces):
        block = jnp.bitwise_xor(index_ref[1], k) * along
        for j in range(along):
            place = block + jnp.bitwise_xor(index_ref[2], j)
            at = j * (wide_rows + tall_rows)
            high, low = halves(piece_ref[0, k, at : at + wide_rows, :])
            rows = pl.ds(pl.multiple_of(4 * D + place * wide_rows, 16), wide_rows)
            high_scr[rows, :] = high
            low_scr[rows, :] = low
            high, low = halves(piece_ref[0, k, at + wide_rows : at + wide_rows + tall_rows, :])
            rows = pl.ds(pl.multiple_of(place * tall_rows, 16), tall_rows)
            high_scr[rows, :] = high
            low_scr[rows, :] = low

    def grad(b):
        return square(high_scr, b), square(low_scr, b)

    def mixed(old, product):
        return stat_beta * old + (1.0 - stat_beta) * (factor * (factor * product))

    def root(k):
        return halves(around_ref[0, k])

    rows = small_ref.shape[2]
    own_row = chosen_rows(rows, D, me * rows, 0)

    def own_part(first, count):
        if count % 16:
            selector = chosen_rows(count, D, me * count, first)
            return lambda b: pick(selector, grad(b))
        return lambda b: [
            scr[pl.ds(pl.multiple_of(b * D + me * count, 16), count), :] for scr in (high_scr, low_scr)
        ]

    own_rows = own_part(0, rows)
    place = 0
    for first, count, left, right_ref, nright_ref, right_root_ref, left_root in (
        (0, 3, 0, qkv_ref, nqkv_ref, right_qkv_ref, 0),
        (4, FF // D, 3, wide_ref, nwide_ref, right_fc1_ref, 2),
    ):
        take = (0, 0) if first else (0,)
        cols = right_ref.shape[-2]
        total = jnp.zeros((rows, D), f32)
        own_cols = [jnp.zeros((cols, D), f32)] * 2
        share = right_root_ref.shape[-2]
        reach = jnp.zeros((D, share), f32)
        for b in range(count):
            block = grad(first + b)
            total = total + dot3(own_rows(first + b), block, NT)
            selector = chosen_rows(cols, D, me * cols, b * D)
            own_cols = [own + dot(selector, part, NT) for own, part in zip(own_cols, block)]
            reach = reach + dot3(block, halves(right_root_ref[take + (slice(None), slice(b * D, (b + 1) * D))]), NT)
        nsmall_ref[0, left] = mixed(small_ref[0, left], total)
        own_cols = [own.astype(bf16) for own in own_cols]
        for b in range(count):
            lanes = slice(b * D, (b + 1) * D)
            nright_ref[take + (slice(None), lanes)] = mixed(
                right_ref[take + (slice(None), lanes)], dot3(own_cols, grad(first + b))
            )
        step_ref[0, :, place : place + share] = dot3(root(left_root), halves(reach))
        place = place + share

    block = grad(3)
    nsmall_ref[0, 1] = mixed(small_ref[0, 1], dot3(own_rows(3), block, NT))
    nsmall_ref[0, 2] = mixed(small_ref[0, 2], dot3(pick(own_row, block, NT), block))
    moved = dot3(halves(dot3(halves(left_out_ref[0, 0]), block)), root(1))
    updated = wout_ref[0] - rate_matrix * factor * moved
    nout_ref[0] = updated
    meout_ref[0] = average(eout_ref[0], updated)

    tall = wide_ref.shape[2]
    total = jnp.zeros((rows, D), f32)
    own = [jnp.zeros((tall, D), f32)] * 2
    reach = jnp.zeros((tall, D), f32)
    whole = tall % 16 == 0
    for b in range(FF // D):
        block = grad(8 + b)
        total = total + dot3(pick(own_row, block, NT), block)
        if not whole:
            selector = chosen_rows(tall, D, me * tall, b * D)
            own = [o + dot(selector, part) for o, part in zip(own, block)]
        reach = reach + dot3(halves(left_fc2_ref[0, 0, :, b * D : (b + 1) * D]), block)
    nsmall_ref[0, 4] = mixed(small_ref[0, 4], total)
    own = own_part(0, tall)(8) if whole else [o.astype(bf16) for o in own]
    for b in range(FF // D):
        lanes = slice(b * D, (b + 1) * D)
        nwide_ref[0, 1, :, lanes] = mixed(wide_ref[0, 1, :, lanes], dot3(own, grad(8 + b), NT))
    updated = wfc2_ref[0] - rate_matrix * factor * dot3(halves(reach), root(3))
    nfc2_ref[0] = updated
    mefc2_ref[0] = average(efc2_ref[0], updated)


def layer_block(array, *second):
    lead = len(second)
    dims = (1,) * (1 + lead) + array.shape[1 + lead :]
    return pl.BlockSpec(dims, lambda i: (i,) + second + (0,) * (array.ndim - 1 - lead))


def shampoo(pieces, along, index, factor, stats, around, roots, weights, averages):
    small, qkv, wide = stats
    root_small, root_qkv, root_wide = roots
    scalar = pl.BlockSpec(memory_space=pltpu.SMEM)
    layered = [small, qkv, wide, around]
    tails = [*weights, *averages, pieces]
    results = [small, qkv, wide, *weights, *averages]
    specs = [scalar, scalar] + [layer_block(x) for x in layered]
    specs += [layer_block(root_small, 1), layer_block(root_wide, 1), layer_block(root_qkv), layer_block(root_wide, 0)]
    specs += [layer_block(x) for x in tails]
    step = shape((LAYERS, D, root_qkv.shape[1] + root_wide.shape[2]))
    return pl.pallas_call(
        functools.partial(shampoo_body, along),
        grid=(LAYERS,),
        in_specs=specs,
        out_specs=[layer_block(x) for x in [*results, step]],
        out_shape=[shape(x.shape) for x in results] + [step],
        scratch_shapes=[pltpu.VMEM((BLOCKS * D, D), bf16)] * 2,
        compiler_params=pltpu.CompilerParams(vmem_limit_bytes=62 << 20),
        cost_estimate=pl.CostEstimate(flops=10_000_000_000, bytes_accessed=60_000_000, transcendentals=0),
    )(index, factor, *layered, root_small, root_wide, root_qkv, root_wide, *tails)


def close_body(feed1_ref, mix1_ref, feed0_ref, mix0_ref, turned_ref, scalar_ref,
               out_ref, outd_ref, outs_ref,
               own1_scr, own0_scr, feed1_scr, mix1_scr, feed_scr, mix_scr, mixz_scr, dense_scr, core_scr, cross_scr, along_scr,
               mix_sum, dense_sum, own_dense, own_scalar,
               pass_feed, pass_feed1, pass_mix, pass_mix1, pass_dense, send_sem, recv_sem, local_sem):
    s = lax.axis_index("section")
    dp = lax.axis_index("dp")
    z, c = dp // 2, dp % 2
    mine = c * 4 + s
    rows = own0_scr.shape[0]
    out0_ref, out1_ref = out_ref.at[0], out_ref.at[1]
    feed_rows, mix_rows = feed0_ref.shape[0] // 4, mix0_ref.shape[0] // 16
    width = turned_ref.shape[2]
    span = SLOTS // 4
    peers = [{"section": s, "dp": jnp.bitwise_xor(dp, 1)}]
    peers += [{"section": jnp.bitwise_xor(s, k), "dp": dp} for k in (1, 2, 3)]
    peers += [{"section": s, "dp": jnp.bitwise_xor(dp, 2 * k)} for k in (1, 2, 3)]
    barrier = pltpu.get_barrier_semaphore()
    for peer in peers:
        pl.semaphore_signal(barrier, inc=1, device_id=peer, device_id_type=pl.DeviceIdType.MESH)
    pl.semaphore_wait(barrier, len(peers))
    count = [0, 0]
    sent = []

    def send(source, target, peer):
        n = count[0]
        count[0] = n + 1
        copy = pltpu.make_async_remote_copy(
            src_ref=source, dst_ref=target, send_sem=send_sem.at[n], recv_sem=recv_sem.at[n],
            device_id=peer, device_id_type=pl.DeviceIdType.MESH,
        )
        copy.start()
        sent.append(copy)
        return copy

    def keep(source, target):
        n = count[1]
        count[1] = n + 1
        copy = pltpu.make_async_copy(source, target, local_sem.at[n])
        copy.start()
        return copy

    def arrive(copies):
        for copy in copies:
            copy.wait_recv()

    def across(k):
        return jnp.bitwise_xor(s, k)

    def up(k):
        return jnp.bitwise_xor(z, k)

    def at(index, size, align):
        return pl.ds(pl.multiple_of(index * size, align), size)

    core, (x, y, diagonal), tower = peers[0], peers[1:4], peers[4:]
    flat = (x, y, diagonal)

    def gather_up(own_ref, out_ref):
        place = out_ref.at[mine, at(z, rows, 16), :]
        local = keep(own_ref, place)
        return local, [send(own_ref, place, peer) for peer in tower[:2]]

    def gather_flat(out_ref, started):
        local, copies = started
        local.wait()
        near, far = copies
        far.wait_recv()
        place = out_ref.at[mine, at(up(2), rows, 16), :]
        passed = send(place, place, tower[0])
        near.wait_recv()
        passed.wait_recv()
        block = out_ref.at[mine]
        found = [send(block, block, x), send(block, block, y)]
        send_core = [send(block, block, core)]
        return found, send_core

    def gather_turn(out_ref, started):
        (from_x, from_y), to_core = started
        half = 2 * rows
        from_x.wait_recv()
        block_x = c * 4 + across(1)
        upper = out_ref.at[block_x, pl.ds(0, half), :]
        turn_y = send(upper, upper, y)
        to_core.append(send(out_ref.at[block_x], out_ref.at[block_x], core))
        from_y.wait_recv()
        block_y = c * 4 + across(2)
        lower = out_ref.at[block_y, pl.ds(half, half), :]
        turn_x = send(lower, lower, x)
        to_core.append(send(out_ref.at[block_y], out_ref.at[block_y], core))
        return [turn_y, turn_x], to_core

    def gather_core(out_ref, started):
        turned, to_core = started
        arrive(turned)
        block = out_ref.at[c * 4 + across(3)]
        return to_core + [send(block, block, core)]


    def climb(view, slots):
        return [send(view(up(1)), slots.at[0], tower[0]), send(view(up(3)), slots.at[1], tower[0])]

    def climb_more(view, slots, pass_ref, started):
        arrive(started)
        pass_ref[...] = view(up(2))[...] + slots[1]
        return send(pass_ref, slots.at[2], tower[1])

    def climb_end(view, slots, started):
        started.wait_recv()
        return view(z)[...] + slots[0] + slots[2]

    def part_of(ref, size):
        return lambda k: ref.at[at(k, size, 16), :]

    feed1, mix1, feed0 = part_of(feed1_ref, feed_rows), part_of(mix1_ref, mix_rows), part_of(feed0_ref, feed_rows)
    mix0 = part_of(mix_sum, mix_rows)
    feed_up = climb(feed0, feed_scr)
    feed1_up = climb(feed1, feed1_scr)
    mix1_up = climb(mix1, mix1_scr)
    dense_core = send(turned_ref.at[:, 1 - c], core_scr, core)
    mix_flat = [
        send(mix0_ref.at[at(across(k), 4 * mix_rows, 16), :], mix_scr.at[k - 1], flat[k - 1]) for k in (1, 2, 3)
    ]
    dense_core.wait_recv()

    def add_core(k):
        dense_sum[k] = turned_ref[k, c] + core_scr[k]

    tiles(4, add_core)
    dense_flat = [
        send(dense_sum.at[:, :, at(across(k), span, LANES)], cross_scr.at[k - 1], flat[k - 1]) for k in (1, 2, 3)
    ]
    feed_up = climb_more(feed0, feed_scr, pass_feed, feed_up)
    feed1_up = climb_more(feed1, feed1_scr, pass_feed1, feed1_up)
    mix1_up = climb_more(mix1, mix1_scr, pass_mix1, mix1_up)
    arrive(mix_flat)
    mix_sum[...] = mix0_ref[at(s, 4 * mix_rows, 16), :] + mix_scr[0] + mix_scr[1] + mix_scr[2]
    mix_up = climb(mix0, mixz_scr)
    own1_scr[0:feed_rows, :] = climb_end(feed1, feed1_scr, feed1_up)
    own1_scr[feed_rows:rows, :] = climb_end(mix1, mix1_scr, mix1_up)
    up1 = gather_up(own1_scr, out1_ref)
    mix_up = climb_more(mix0, mixz_scr, pass_mix, mix_up)
    own0_scr[0:feed_rows, :] = climb_end(feed0, feed_scr, feed_up)
    own0_scr[feed_rows:rows, :] = climb_end(mix0, mixz_scr, mix_up)
    up0 = gather_up(own0_scr, out0_ref)
    flat1 = gather_flat(out1_ref, up1)
    arrive(dense_flat)

    def add_flat(k):
        mid = dense_sum[k, :, at(s, span, LANES)]
        dense_scr[k] = mid + cross_scr[0, k] + cross_scr[1, k] + cross_scr[2, k]

    tiles(4, add_flat)
    dense_view = lambda k: dense_scr.at[k]
    dense_up = climb(dense_view, along_scr)
    flat0 = gather_flat(out0_ref, up0)
    dense_up = climb_more(dense_view, along_scr, pass_dense, dense_up)
    turn1 = gather_turn(out1_ref, flat1)
    own_dense[...] = climb_end(dense_view, along_scr, dense_up)
    home = outd_ref.at[s]
    local_dense = keep(own_dense, home)
    spread_dense = [send(own_dense, home, peer) for peer in flat]
    total = jnp.zeros((1, 1), f32)
    for part in (own1_scr[...], own0_scr[...], own_dense[...]):
        total = total + jnp.sum(jnp.sum(part * part, 0, keepdims=True), 1, keepdims=True)
    lane = lax.broadcasted_iota(jnp.int32, (8, LANES), 1)
    own_scalar[...] = jnp.where(lane == 0, total, scalar_ref[...])
    home = outs_ref.at[c, s, z]
    local_scalar = keep(own_scalar, home)
    scalar_up = [send(own_scalar, home, peer) for peer in tower]
    local_scalar.wait()
    arrive(scalar_up)
    home = outs_ref.at[c, s]
    scalar_flat = [send(home, home, peer) for peer in flat]
    turn0 = gather_turn(out0_ref, flat0)
    core1 = gather_core(out1_ref, turn1)
    arrive(scalar_flat)
    home = outs_ref.at[c]
    scalar_core = send(home, home, core)
    core0 = gather_core(out0_ref, turn0)
    local_dense.wait()
    arrive(spread_dense)
    arrive(core1)
    arrive(core0)
    scalar_core.wait_recv()
    for copy in sent:
        copy.wait_send()


def close_exchange(feed1, mix1, feed0, mix0, turned, scalars):
    feed_rows, mix_rows = feed0.shape[0] // 4, mix0.shape[0] // 16
    rows = feed_rows + mix_rows
    width, span = turned.shape[2], SLOTS // 4
    anywhere = pl.BlockSpec(memory_space=pl.ANY)
    copies = 54
    return pl.pallas_call(
        close_body,
        in_specs=[pl.BlockSpec(memory_space=pltpu.VMEM)] * 6,
        out_specs=[anywhere] * 3,
        out_shape=[
            shape((2, 8, 4 * rows, D)), shape((4, width, span)), shape((2, 4, 4, 8, LANES)),
        ],
        scratch_shapes=[
            pltpu.VMEM((rows, D), f32),
            pltpu.VMEM((rows, D), f32),
            pltpu.VMEM((3, feed_rows, D), f32),
            pltpu.VMEM((3, mix_rows, D), f32),
            pltpu.VMEM((3, feed_rows, D), f32),
            pltpu.VMEM((3, 4 * mix_rows, D), f32),
            pltpu.VMEM((3, mix_rows, D), f32),
            pltpu.VMEM((4, width, span), f32),
            pltpu.VMEM((4, width, SLOTS), f32),
            pltpu.VMEM((3, 4, width, span), f32),
            pltpu.VMEM((3, width, span), f32),
            pltpu.VMEM((4 * mix_rows, D), f32),
            pltpu.VMEM((4, width, SLOTS), f32),
            pltpu.VMEM((width, span), f32),
            pltpu.VMEM((8, LANES), f32),
            pltpu.VMEM((feed_rows, D), f32),
            pltpu.VMEM((feed_rows, D), f32),
            pltpu.VMEM((mix_rows, D), f32),
            pltpu.VMEM((mix_rows, D), f32),
            pltpu.VMEM((width, span), f32),
            pltpu.SemaphoreType.DMA((copies,)),
            pltpu.SemaphoreType.DMA((copies,)),
            pltpu.SemaphoreType.DMA((4,)),
        ],
        compiler_params=pltpu.CompilerParams(
            vmem_limit_bytes=60 << 20, collective_id=0, has_side_effects=True
        ),
        cost_estimate=pl.CostEstimate(flops=10_000_000, bytes_accessed=300_000_000, transcendentals=0),
    )(feed1, mix1, feed0, mix0, turned, scalars)


def turn_body(step_ref, out_ref, send_sem, recv_sem, local_sem):
    s = lax.axis_index("section")
    dp = lax.axis_index("dp")
    half, parts = out_ref.shape[2], out_ref.shape[1]
    x, y = [{"section": jnp.bitwise_xor(s, k), "dp": dp} for k in (1, 2)]
    peers = [{"section": s, "dp": jnp.bitwise_xor(dp, k)} for k in range(8)]
    barrier = pltpu.get_barrier_semaphore()
    for peer in [x, y, *peers[1:]]:
        pl.semaphore_signal(barrier, inc=1, device_id=peer, device_id_type=pl.DeviceIdType.MESH)
    pl.semaphore_wait(barrier, len(peers) + 1)
    sent = []

    def send(source, target, peer):
        n = len(sent)
        copy = pltpu.make_async_remote_copy(
            src_ref=source, dst_ref=target, send_sem=send_sem.at[n], recv_sem=recv_sem.at[n],
            device_id=peer, device_id_type=pl.DeviceIdType.MESH,
        )
        copy.start()
        sent.append(copy)
        return copy

    def source(k):
        start = pl.multiple_of(jnp.bitwise_xor(dp, k) * 2 * half + (s % 2) * half, 8)
        return step_ref.at[s // 2, pl.ds(start, half), :]

    own = out_ref.at[s]
    local = pltpu.make_async_copy(source(0), own.at[dp], local_sem)
    local.start()
    around = [send(source(k), own.at[dp], peers[k]) for k in (4, 6, 5, 7, 2, 3, 1)]
    local.wait()
    for copy in around:
        copy.wait_recv()
    from_x, from_y = send(own, own, x), send(own, own, y)
    from_x.wait_recv()
    piece = out_ref.at[jnp.bitwise_xor(s, 1), pl.ds(0, parts // 2)]
    upper = send(piece, piece, y)
    from_y.wait_recv()
    piece = out_ref.at[jnp.bitwise_xor(s, 2), pl.ds(parts // 2, parts // 2)]
    lower = send(piece, piece, x)
    upper.wait_recv()
    lower.wait_recv()
    for copy in sent:
        copy.wait_send()


def turn_exchange(step):
    layers, rows, lanes = step.shape
    copies = 7 + 2 + 2
    return pl.pallas_call(
        turn_body,
        in_specs=[pl.BlockSpec(memory_space=pl.ANY)],
        out_specs=pl.BlockSpec(memory_space=pl.ANY),
        out_shape=shape((2 * layers, 8, rows // 16, lanes)),
        scratch_shapes=[
            pltpu.SemaphoreType.DMA((copies,)), pltpu.SemaphoreType.DMA((copies,)), pltpu.SemaphoreType.DMA,
        ],
        compiler_params=pltpu.CompilerParams(vmem_limit_bytes=60 << 20, collective_id=1, has_side_effects=True),
        cost_estimate=pl.CostEstimate(flops=1000, bytes_accessed=80_000_000, transcendentals=0),
    )(step)


def open_body(part_ref, out_ref, send_sem, recv_sem, local_sem):
    s = lax.axis_index("section")
    dp = lax.axis_index("dp")
    z, c = dp // 2, dp % 2
    rows = part_ref.shape[0] // 4
    core = {"section": s, "dp": jnp.bitwise_xor(dp, 1)}
    flat = [{"section": jnp.bitwise_xor(s, k), "dp": dp} for k in (1, 2)]
    tower = [{"section": s, "dp": jnp.bitwise_xor(dp, 2 * k)} for k in (1, 2, 3)]
    peers = [core, *flat, *tower]
    barrier = pltpu.get_barrier_semaphore()
    for peer in peers:
        pl.semaphore_signal(barrier, inc=1, device_id=peer, device_id_type=pl.DeviceIdType.MESH)
    pl.semaphore_wait(barrier, len(peers))
    sent = []

    def send(source, target, peer):
        n = len(sent)
        copy = pltpu.make_async_remote_copy(
            src_ref=source, dst_ref=target, send_sem=send_sem.at[n], recv_sem=recv_sem.at[n],
            device_id=peer, device_id_type=pl.DeviceIdType.MESH,
        )
        copy.start()
        sent.append(copy)
        return copy

    def place(k, across):
        return out_ref.at[jnp.bitwise_xor(z, k), c, jnp.bitwise_xor(s, across)]

    own = part_ref.at[pl.ds(pl.multiple_of(s * rows, 16), rows), :]
    upward = [send(own, place(0, 0), peer) for peer in tower]
    local = pltpu.make_async_copy(own, place(0, 0), local_sem)
    local.start()
    local.wait()
    half = rows // 32 * 16
    crossed, ended = [], []
    for k in range(4):
        if k:
            upward[k - 1].wait_recv()
        crossed.append([send(place(k, 0), place(k, 0), peer) for peer in flat])
        ended.append(send(place(k, 0), place(k, 0), core))
    for k in range(4):
        from_x, from_y = crossed[k]
        from_x.wait_recv()
        piece = place(k, 1).at[0:half]
        turned = [send(piece, piece, flat[1])]
        ended.append(send(place(k, 1), place(k, 1), core))
        from_y.wait_recv()
        piece = place(k, 2).at[half:rows]
        turned.append(send(piece, piece, flat[0]))
        ended.append(send(place(k, 2), place(k, 2), core))
        crossed[k] = turned
    for k in range(4):
        for copy in crossed[k]:
            copy.wait_recv()
        ended.append(send(place(k, 3), place(k, 3), core))
    for copy in ended:
        copy.wait_recv()
    for copy in sent:
        copy.wait_send()


def open_exchange(part):
    rows = part.shape[0]
    copies = 3 + 8 + 8 + 16
    return pl.pallas_call(
        open_body,
        in_specs=[pl.BlockSpec(memory_space=pl.ANY)],
        out_specs=pl.BlockSpec(memory_space=pl.ANY),
        out_shape=shape((4, 2, 4, rows // 4, D), bf16),
        scratch_shapes=[
            pltpu.SemaphoreType.DMA((copies,)), pltpu.SemaphoreType.DMA((copies,)), pltpu.SemaphoreType.DMA,
        ],
        compiler_params=pltpu.CompilerParams(vmem_limit_bytes=60 << 20, collective_id=2, has_side_effects=True),
        cost_estimate=pl.CostEstimate(flops=1000, bytes_accessed=80_000_000, transcendentals=0),
    )(part).reshape(8, rows, D)


def finish_body(parts, factor_ref, found_ref, *refs):
    (wqkv_ref, wfc1_ref, eqkv_ref, efc1_ref, nqkv_ref, nfc1_ref, mqkv_ref, mfc1_ref) = refs
    scale = rate_matrix * factor_ref[0]
    cuts, tall = found_ref.shape[0] // LAYERS, found_ref.shape[2]
    for layer in range(LAYERS):
        place = 0
        for w_ref, e_ref, n_ref, a_ref in (
            (wqkv_ref, eqkv_ref, nqkv_ref, mqkv_ref), (wfc1_ref, efc1_ref, nfc1_ref, mfc1_ref)
        ):
            share = w_ref.shape[2] // parts
            for j in range(parts):
                lanes = slice(j * share, (j + 1) * share)
                for cut in range(cuts):
                    rows = slice(cut * tall, (cut + 1) * tall)
                    step = found_ref[layer * cuts + cut, j, :, place : place + share]
                    updated = w_ref[layer, rows, lanes] - scale * step
                    n_ref[layer, rows, lanes] = updated
                    a_ref[layer, rows, lanes] = average(e_ref[layer, rows, lanes], updated)
            place = place + share


def finish(parts, factor, found, weights, averages):
    scalar = pl.BlockSpec(memory_space=pltpu.SMEM)
    operands = [found, *weights, *averages]
    return pl.pallas_call(
        functools.partial(finish_body, parts),
        in_specs=[scalar] + [pl.BlockSpec(memory_space=pltpu.VMEM)] * len(operands),
        out_shape=[shape(x.shape) for x in (*weights, *averages)],
        compiler_params=pltpu.CompilerParams(vmem_limit_bytes=60 << 20),
        cost_estimate=pl.CostEstimate(flops=10_000_000, bytes_accessed=6_000_000, transcendentals=0),
    )(factor, *operands)


def adam_body(index_ref, scalar_ref, pieces_ref, *refs):
    dense, vectors, new_dense, new_vectors, turned_scr, gradient_scr = (
        refs[:4], refs[4:8], refs[8:12], refs[12:16], refs[16], refs[17]
    )
    width, count = dense[0].shape
    span = pieces_ref.shape[2]
    for k in range(pieces_ref.shape[0]):
        place = jnp.bitwise_xor(index_ref[3], k)
        lanes = pl.ds(pl.multiple_of(place * span, LANES), span)
        turned_scr[:, lanes] = pieces_ref[k, 0:width, :]
    row = lax.broadcasted_iota(jnp.int32, (EXT, TABLE), 0)
    col = lax.broadcasted_iota(jnp.int32, (EXT, TABLE), 1)
    mixed = (row % LANES) * (PIX + 1) + row // LANES == col
    mixed = jnp.where(mixed & (row % LANES < VARS), 1.0, 0.0)
    gradient_scr[:, 0:TABLE] = lax.dot_general(
        turned_scr[:, AT_TABLE:AT_VECTOR], mixed, NN, precision=highest, preferred_element_type=f32
    )
    gradient_scr[:, TABLE : TABLE + AT_HEAD + VP] = turned_scr[:, 0 : AT_HEAD + VP]

    def update(refs, news, gradient, rate, decay):
        old = [ref[...] for ref in refs]
        gradient = gradient * scalar_ref[0]
        first = beta_first * old[1] + (1.0 - beta_first) * gradient
        second = beta_second * old[2] + (1.0 - beta_second) * gradient * gradient
        first_hat = first / scalar_ref[1]
        second_hat = second / scalar_ref[2]
        updated = old[0] - rate * (first_hat / (jnp.sqrt(second_hat) + adam_eps) + decay * old[0])
        for ref, value in zip(news, (updated, first, second, average(old[3], updated))):
            ref[...] = value

    update(dense, new_dense, gradient_scr[...], rate_dense, weight_decay)
    few = vectors[0].shape[1]
    update(vectors, new_vectors, turned_scr[:, AT_VECTOR : AT_VECTOR + few], rate_vector, 0.0)


def adam(index, scalars, pieces, dense, vectors):
    scalar = pl.BlockSpec(memory_space=pltpu.SMEM)
    states = [x.T for x in (*dense, *vectors)]
    width, count = states[0].shape
    return [
        new.T
        for new in pl.pallas_call(
            adam_body,
            in_specs=[scalar, scalar] + [pl.BlockSpec(memory_space=pltpu.VMEM)] * (1 + len(states)),
            out_shape=[shape(x.shape) for x in states],
            scratch_shapes=[pltpu.VMEM((width, SLOTS), f32), pltpu.VMEM((width, count), f32)],
            compiler_params=pltpu.CompilerParams(vmem_limit_bytes=60 << 20),
            cost_estimate=pl.CostEstimate(flops=10_000_000, bytes_accessed=8_000_000, transcendentals=0),
        )(index, scalars, pieces, *states)
    ]


def digits(count, start=1):
    found = []
    while start < count:
        radix = min(4, count // start)
        found.append((start, radix))
        start *= radix
    return found


def swap(values, axis, bits):
    return lax.ppermute(values, axis, [(k, k ^ bits) for k in range(lax.axis_size(axis))])


def digit(axis, bit, radix):
    return (lax.axis_index(axis) // bit) % radix


def share_out(values, dim, axis, bit, radix):
    size = values.shape[dim] // radix
    mine = digit(axis, bit, radix)

    def part(k):
        return lax.dynamic_slice_in_dim(values, jnp.bitwise_xor(mine, k) * size, size, dim)

    arrived = [swap(part(k), axis, k * bit) for k in range(1, radix)]
    total = part(0)
    for other in arrived:
        total = total + other
    return total


def collect(values, axis, bit, radix):
    return [values] + [swap(values, axis, k * bit) for k in range(1, radix)]


def in_order(found, place):
    low = 1
    while low < len(found):
        even = (place // low) % 2 == 0
        found = [jnp.where(even, found[k], found[k ^ low]) for k in range(len(found))]
        low *= 2
    return found


def gate(values, first):
    return lax.optimization_barrier((values, first))


def advance(values, sums, wanted=None):
    wanted = [k for k in range(len(sums)) if sums[k][1] and (wanted is None or k in wanted)]
    moved = [share_out(sums[k][0], 0, *sums[k][1][0]) for k in wanted]
    values, moved = gate(values, moved)
    sums = list(sums)
    for k, part in zip(wanted, moved):
        sums[k] = [part, sums[k][1][1:]]
    return values, sums


def total_of(values, stages):
    for axis, bit, radix in stages:
        values = sum(in_order(collect(values, axis, bit, radix), digit(axis, bit, radix)))
    return values


def valid_flags(counts):
    var_index = jnp.arange(VARS)
    level_index = (var_index - SURF) % LEVELS
    inside = (var_index[None, :] < SURF) | (level_index[None, :] < counts[:, None])
    return jnp.where(inside, 1.0, 0.0).astype(f32)


def cosine_table():
    pixel_rows = 2 * LAT_ROWS
    latitude = (np.arange(pixel_rows) + 0.5) * (np.pi / pixel_rows) - 0.5 * np.pi
    cosine = np.cos(latitude)
    cosine = cosine / np.mean(cosine)
    by_row = cosine.reshape(LAT_ROWS, 2).repeat(LON_COLS, 0)
    return by_row.astype(np.float32), float(by_row.sum() * (PIX // 2))


def average(old_state, new_state):
    return ema_beta * old_state + (1.0 - ema_beta) * new_state


def column_blocks(part):
    rows, cols = part.shape
    return part.reshape(rows, cols // D, D).transpose(1, 0, 2).reshape(-1, D)


def pack_layer(parts):
    qkv, out, fc1, fc2 = [part.astype(bf16) for part in parts]
    return jnp.concatenate([column_blocks(qkv), out, column_blocks(fc1), fc2], 0)


def unpack_layer(full, rows):
    above = full[:, : rows * 8].reshape(-1, 8, rows, D).transpose(1, 0, 2, 3).reshape(8 * D, D)
    return jnp.concatenate([above, full[:, rows * 8 :].reshape(FF, D)], 0)


def per_device(
    fields, targets, level_count, step_count,
    dense, dense_m, dense_v, dense_ema, vectors, vectors_m, vectors_v, vectors_ema,
    w_qkv, w_out, w_fc1, w_fc2, ema_qkv, ema_out, ema_fc1, ema_fc2,
    stat_small, stat_qkv, stat_wide, root_small, root_qkv, root_wide,
):
    section = lax.axis_index("section")
    sections = lax.axis_size("section")
    dp_index = lax.axis_index("dp")
    parts = lax.axis_size("dp")
    direct = sections == 4 and parts == 8
    rows_dense = dense.shape[0]
    width = D // parts
    both_rows = jnp.concatenate([dense, vectors], 0).astype(bf16)
    packed = [pack_layer([part[layer] for part in (w_qkv, w_out, w_fc1, w_fc2)]) for layer in range(LAYERS)]
    layer_weights = []
    if direct:
        slots = -(-both_rows.shape[0] // LANES) * LANES
        turned = jnp.pad(both_rows, ((0, slots - both_rows.shape[0]), (0, 0))).T
        first = turned.size // D
        before = open_exchange(jnp.concatenate([turned.reshape(first, D), packed[0]], 0))
        full_dense = before[:, :first].reshape(D, slots).T
        layer_weights.append(before)
        packed = packed[1:]
    else:
        full_dense = lax.all_gather(both_rows, "dp", axis=1, tiled=True)
        before = full_dense
    for part in packed:
        part, before = gate(part, before)
        if not layer_weights:
            full_dense = before
        elif not direct:
            layer_weights[-1] = before
        before = lax.all_gather(part, "dp", axis=0)
        layer_weights.append(before)
    near, layer_weights[-1] = gate(root_small, layer_weights[-1])
    around = lax.all_gather(near[:, np.array([0, 2, 3, 4])], "dp", axis=2, tiled=True)
    if direct:
        layer_weights = list(zip(layer_weights, [first] + [0] * (LAYERS - 1)))
    else:
        layer_weights = [unpack_layer(full, w_qkv.shape[1]) for full in layer_weights]
    gain_rows = full_dense[rows_dense : rows_dense + vectors.shape[0]].astype(f32)
    micro_count = fields.shape[0]
    table = full_dense[:TABLE].reshape(VARS, PIX + 1, D).transpose(1, 0, 2)
    table = jnp.pad(table, ((0, 0), (0, LANES - VARS), (0, 0))).reshape(EXT, D)
    position = full_dense[TABLE : TABLE + SEQ]
    proj = full_dense[TABLE + SEQ : TABLE + SEQ + D]
    head_rows = full_dense[TABLE + SEQ + D : rows_dense]
    flags = valid_flags(level_count)
    by_row, row_total = cosine_table()
    weight_local = jnp.sum(flags) * row_total
    cosines = jnp.asarray(by_row)

    core = [("dp", 1, 2)]
    cross = [("section", bit, radix) for bit, radix in digits(sections)]
    along = [("dp", bit, radix) for bit, radix in digits(parts, 2)]
    turns = -(-micro_count // sections)
    turned, error_sum, d_mats = 0.0, 0.0, [0.0] * (2 * LAYERS)
    pending, ready = [], []
    for turn in range(turns):
        index = turn * sections + section
        active = jnp.where(index < micro_count, 1.0, 0.0).astype(f32)
        index = jnp.minimum(index, micro_count - 1)
        field_rows = lax.dynamic_index_in_dim(fields, index, 0, False)
        target = lax.dynamic_index_in_dim(targets, index, 0, False)
        flag_row = lax.dynamic_index_in_dim(flags, index, 0, True)
        valid_vars = jnp.pad(flag_row, ((0, 0), (0, LANES - VARS)), constant_values=-1.0)
        valid_values = jnp.repeat(flag_row * active, PIX, axis=1)
        x, agg = embed_forward(field_rows, table, gain_rows[0:1], valid_vars, proj, position)
        kept = []
        for layer in range(LAYERS):
            gains = gain_rows[1 + 2 * layer : 3 + 2 * layer]
            if direct:
                layer_weights[layer], *saved, y = block_forward(x, gains, *layer_weights[layer])
            else:
                *saved, y = block_forward(x, gains, layer_weights[layer])
            kept.append((x, saved))
            x = y
        grad, d_head, d_final, errors = head_step(
            x, gain_rows[2 * LAYERS + 1 :], head_rows, target, cosines, valid_values
        )
        d_gains = [None] * (2 * LAYERS)
        for layer in reversed(range(LAYERS)):
            gains = gain_rows[1 + 2 * layer : 3 + 2 * layer]
            x, (h, qkv, o, lse, m, h2) = kept[layer]
            pending, ready = pending + ready, []
            grad, pending = advance(grad, pending)
            dm, do, d_gains[2 * layer + 1], found = feed_back(h2, m, grad, gains, layer_weights[layer])
            d_mats[2 * layer + 1] = d_mats[2 * layer + 1] + found if turn else found
            if turn == turns - 1:
                ready = [[d_mats[2 * layer + 1], core + cross]]
            do, pending = advance(do, pending, range(0, len(pending), 2))
            pending, ready = pending + ready, []
            grad, d_gains[2 * layer], found = mix_back(
                x, (h, qkv, o, lse), dm, do, gains, layer_weights[layer]
            )
            d_mats[2 * layer] = d_mats[2 * layer] + found if turn else found
            if turn == turns - 1:
                ready = [[d_mats[2 * layer], core + cross]]
        grad, pending = advance(grad, pending)
        pending, ready = pending + ready, []
        d_vectors = jnp.concatenate(
            [jnp.zeros((1, D), f32), *d_gains, d_final, jnp.zeros((6 - 2 * LAYERS, D), f32)], 0
        )
        found = embed_back(
            field_rows, table, gain_rows[0:1], valid_vars, proj, agg, grad, d_head, d_vectors
        )
        turned = turned + found if turn else found
        error_sum = error_sum + jnp.sum(errors)

    turned, pending = advance(turned, pending)
    width = D // parts
    scalars = jnp.stack([jnp.zeros((), f32), error_sum, jnp.where(section == 0, weight_local, 0.0)])
    scalars = jnp.broadcast_to(jnp.pad(scalars, (0, LANES - 3))[None], (8, LANES))
    if direct:
        feed1, mix1, feed0, mix0 = [part for part, unused in pending]
        pieces, dense_pieces, scalars = close_exchange(
            feed1, mix1, feed0, mix0, turned.reshape(parts // 2, 2, width, SLOTS), scalars
        )
        scalars = jnp.sum(scalars, (0, 1, 2))
        runs, places = parts // 2, [0, 0, 0]
    else:
        own_mats = []
        for part, stages in pending:
            for stage in stages + along:
                part = share_out(part, 0, *stage)
            own_mats.append(part)
        own_dense = turned
        for axis, bit, radix in core:
            own_dense = share_out(own_dense.reshape(-1, radix, width, SLOTS), 1, axis, bit, radix)
        for axis, bit, radix in cross:
            own_dense = share_out(own_dense, 3, axis, bit, radix)
        for axis, bit, radix in along:
            own_dense = share_out(own_dense.reshape(-1, radix, width, own_dense.shape[3]), 1, axis, bit, radix)
        own_dense = own_dense.reshape(width, -1)

        square_own = sum(jnp.sum(part * part) for part in [own_dense] + own_mats)
        scalars = jnp.where(jnp.arange(LANES) == 0, square_own, scalars)
        scalars = total_of(scalars, core + cross + along)

        pieces = []
        for tall_part, wide_part in zip(own_mats[1::2], own_mats[::2]):
            if len(along) == 1 and wide_part.shape[0] % 16 == 0 and tall_part.shape[0] % 16 == 0:
                runs = along[0][2]
                part = jnp.concatenate(collect(jnp.concatenate([wide_part, tall_part], 0), *along[0]), 0)
            else:
                runs = 1
                for stage in reversed(along):
                    turn_at = digit(*stage)
                    wide_part = jnp.concatenate(in_order(collect(wide_part, *stage), turn_at), 0)
                    tall_part = jnp.concatenate(in_order(collect(tall_part, *stage), turn_at), 0)
                part = jnp.concatenate([wide_part, tall_part], 0)
            found = [part]
            for stage in (cross + core if len(cross) == 1 else cross[::-1] + core):
                rounds = [collect(part, *stage) for part in found]
                found = [rounds[j][k] for k in range(stage[2]) for j in range(len(rounds))]
            pieces.insert(0, found)
        fill = -width % 8
        dense_pieces = [jnp.pad(own_dense, ((0, fill), (0, 0)))]
        for stage in cross[::-1]:
            rounds = [collect(part, *stage) for part in dense_pieces]
            dense_pieces = [rounds[j][k] for k in range(stage[2]) for j in range(len(rounds))]
        dense_pieces = jnp.stack(dense_pieces)
        pieces = jnp.stack([jnp.stack(found) for found in pieces])
        places = [(dp_index % 2) * sections + section, dp_index // 2 if runs > 1 else 0, section]

    square_total, error_total, weight_total = scalars[0, 0], scalars[0, 1], scalars[0, 2]
    grad_norm = jnp.sqrt(square_total) / weight_total
    factor = jnp.minimum(1.0, clip_level / grad_norm) / weight_total
    steps_done = step_count[0].astype(f32)
    corrections = [1.0 - jnp.power(beta, steps_done) for beta in (beta_first, beta_second)]
    index = jnp.stack([jnp.asarray(k, jnp.int32) for k in (dp_index, *places)])
    (
        dense_new, dense_m_new, dense_v_new, dense_ema_new,
        vectors_new, vectors_m_new, vectors_v_new, vectors_ema_new,
    ) = adam(
        index, jnp.stack([factor, *corrections]), dense_pieces,
        (dense, dense_m, dense_v, dense_ema), (vectors, vectors_m, vectors_v, vectors_ema),
    )

    (
        stat_small_new, stat_qkv_new, stat_wide_new, out_new, fc2_new, ema_out_new, ema_fc2_new, step,
    ) = shampoo(
        pieces, runs, index, factor.reshape(1), (stat_small, stat_qkv, stat_wide), around,
        (root_small, root_qkv, root_wide), (w_out, w_fc2), (ema_out, ema_fc2),
    )
    if direct:
        arrived = turn_exchange(step)
    else:
        step = step.reshape(LAYERS, parts, width, -1)
        sent = [
            lax.dynamic_index_in_dim(step, jnp.bitwise_xor(dp_index, k), 1, False) for k in range(parts)
        ]
        arrived = jnp.stack([swap(part, "dp", k) if k else part for k, part in enumerate(sent)], 1)
        arrived = jnp.take(arrived, jnp.bitwise_xor(jnp.arange(parts), dp_index), axis=1)
    qkv_new, fc1_new, ema_qkv_new, ema_fc1_new = finish(
        parts, factor.reshape(1), arrived, (w_qkv, w_fc1), (ema_qkv, ema_fc1)
    )
    return (
        error_total / weight_total,
        grad_norm,
        dense_new,
        dense_m_new,
        dense_v_new,
        dense_ema_new,
        vectors_new,
        vectors_m_new,
        vectors_v_new,
        vectors_ema_new,
        qkv_new,
        out_new,
        fc1_new,
        fc2_new,
        ema_qkv_new,
        ema_out_new,
        ema_fc1_new,
        ema_fc2_new,
        stat_small_new,
        stat_qkv_new,
        stat_wide_new,
    )


def solution(mesh):
    items = P("dp", None, None)
    columns = P(None, "dp")
    matrix = P(None, "dp", None)
    stacked = P(None, None, "dp", None)
    return jax.shard_map(
        per_device,
        mesh=mesh,
        in_specs=(
            (items, items, P("dp"), P())
            + (columns,) * 8
            + (matrix,) * 8
            + (stacked, matrix, stacked) * 2
        ),
        out_specs=(P(), P()) + (columns,) * 8 + (matrix,) * 8 + (stacked, matrix, stacked),
        check_vma=False,
    )
```

```python
import functools
import math

import jax
import jax.numpy as jnp
import numpy as np
from jax import lax
from jax.experimental import pallas as pl
from jax.experimental.pallas import tpu as pltpu
from jax.sharding import PartitionSpec as P

D = 384
HEADS = 6
HDIM = 64
SURF = 4
LEVELS = 13
VARS = 69
PIX = 4
VP = 276
LAT_ROWS = 64
LON_COLS = 16
SEQ = 1024
LAYERS = 2
FF = 1536
BLOCKS = 4 + 2 * (FF // D)

LANES = 128
PAIRS = HEADS // 2
EXT = (PIX + 1) * LANES
TABLE = VARS * (PIX + 1)

AT_PROJ = SEQ
AT_HEAD = AT_PROJ + D
AT_TABLE = AT_HEAD + 3 * LANES
AT_VECTOR = AT_TABLE + EXT
SLOTS = AT_VECTOR + LANES

highest = lax.Precision.HIGHEST
f32 = jnp.float32
bf16 = jnp.bfloat16
norm_eps = 1e-05
clip_level = 0.001
rate_dense = 0.05
rate_vector = 0.2
rate_matrix = 0.5
beta_first = 0.9
beta_second = 0.95
adam_eps = 1e-08
weight_decay = 0.1
stat_beta = 0.95
ema_beta = 0.9
LOG2E = math.log2(math.e)
SCALE2 = LOG2E * HDIM ** (-0.5)

NN = (((1,), (0,)), ((), ()))
NT = (((1,), (1,)), ((), ()))
TN = (((0,), (0,)), ((), ()))


def dot(left, right, dims=NN):
    return lax.dot_general(left, right, dims, preferred_element_type=f32)


def halves(value):
    high = value.astype(bf16)
    return high, (value - high.astype(f32)).astype(bf16)


def call(body, out_shape, scratch=(), vmem=60 << 20, flops=0, traffic=0):
    return pl.pallas_call(
        body,
        out_shape=out_shape,
        scratch_shapes=list(scratch),
        compiler_params=pltpu.CompilerParams(vmem_limit_bytes=vmem),
        cost_estimate=pl.CostEstimate(flops=flops, bytes_accessed=traffic, transcendentals=0),
    )


def shape(dims, kind=f32):
    return jax.ShapeDtypeStruct(dims, kind)


def norm_parts(values):
    center = values - jnp.mean(values, -1, keepdims=True)
    spread = jnp.mean(center * center, -1, keepdims=True)
    inverse = lax.rsqrt(spread + norm_eps)
    return center * inverse, inverse


def norm_back(values, gain, upstream):
    unit, inverse = norm_parts(values)
    scaled = upstream * gain
    back = inverse * (
        scaled
        - jnp.mean(scaled, -1, keepdims=True)
        - unit * jnp.mean(scaled * unit, -1, keepdims=True)
    )
    return back, jnp.sum(upstream * unit, 0, keepdims=True)


def tiles(count, body):
    def step(index, carry):
        body(index)
        return carry

    lax.fori_loop(0, count, step, 0)


def rows_of(index, size):
    return pl.ds(pl.multiple_of(index * size, size), size)


def head_mask(rows, which):
    lane = lax.broadcasted_iota(jnp.int32, (rows, LANES), 1)
    return (lane >= which * HDIM) & (lane < (which + 1) * HDIM)


def spread_fields(field_rows):
    row = lax.broadcasted_iota(jnp.int32, (VP, PIX * LANES), 0)
    col = lax.broadcasted_iota(jnp.int32, (VP, PIX * LANES), 1)
    var, pixel = col % LANES, col // LANES
    chosen = (row == PIX * var + pixel) & (var < VARS)
    return dot(field_rows, jnp.where(chosen, 1.0, 0.0).astype(bf16))


def query_mask(query_row):
    head = lax.broadcasted_iota(jnp.int32, (8, D), 0)
    lane = lax.broadcasted_iota(jnp.int32, (8, D), 1)
    return jnp.where(lane // HDIM == head, query_row * HDIM ** (-0.5), 0.0)


def query_scores(table_ref, mask, query_scr):
    for j in range(PIX + 1):
        part = table_ref[j * LANES : (j + 1) * LANES, :]
        query_scr[j * 8 : (j + 1) * 8, :] = dot(mask.astype(bf16), part, NT)


def mix_weights(extended, query_scr, head, valid):
    score = query_scr[pl.ds(PIX * 8 + head, 1), :]
    for j in range(PIX):
        score = score + extended[j] * query_scr[pl.ds(j * 8 + head, 1), :]
    score = jnp.where(valid > 0, score, jnp.where(valid < 0, -jnp.inf, -1e9))
    peak = jnp.max(score, -1, keepdims=True)
    weight = jnp.exp(score - peak)
    return weight / jnp.sum(weight, -1, keepdims=True)


def embed_body(field_ref, table_ref, query_ref, valid_ref, proj_ref, pos_ref, out_ref, agg_ref, query_scr):
    size = 256
    query_scores(table_ref, query_mask(query_ref[...]), query_scr)

    def tile(index):
        rows = rows_of(index, size)
        wide = spread_fields(field_ref[rows, :])
        extended = [wide[:, j * LANES : (j + 1) * LANES] for j in range(PIX)]
        valid = valid_ref[...]

        def pair(hp, carry):
            lanes = rows_of(hp, LANES)
            table = table_ref[:, lanes]
            total = jnp.zeros((size, LANES), f32)
            for which in range(2):
                weight = mix_weights(extended, query_scr, 2 * hp + which, valid)
                mixing = jnp.concatenate([weight * extended[j] for j in range(PIX)] + [weight], 1)
                own = jnp.where(head_mask(EXT, which), table, jnp.zeros_like(table))
                high, low = halves(mixing)
                total = total + dot(high, own) + dot(low, own)
            agg_ref[rows, lanes] = total.astype(bf16)
            return carry

        lax.fori_loop(0, PAIRS, pair, 0)
        out_ref[rows, :] = (dot(agg_ref[rows, :], proj_ref[...]) + pos_ref[rows, :].astype(f32)).astype(bf16)

    tiles(SEQ // size, tile)


def embed_forward(field_rows, table, query_row, valid, proj, position):
    return call(
        embed_body,
        (shape((SEQ, D), bf16), shape((SEQ, D), bf16)),
        [pltpu.VMEM((40, LANES), f32)],
        flops=4_000_000_000,
        traffic=4_000_000,
    )(field_rows, table, query_row, valid, proj, position)


def embed_back_body(
    field_ref, table_ref, query_ref, valid_ref, proj_ref, agg_ref, grad_ref, dhead_ref, dvector_ref,
    out_ref, vector_scr, query_scr, wide_scr, merged_scr, high_scr, low_scr, dscore_scr,
):
    size = 256
    mask = query_mask(query_ref[...])
    query_scores(table_ref, mask, query_scr)
    out_ref[:, AT_PROJ : AT_PROJ + D] = dot(grad_ref[...], agg_ref[...], TN)
    out_ref[:, AT_HEAD:AT_TABLE] = jnp.zeros((D, AT_TABLE - AT_HEAD), f32)
    out_ref[:, AT_HEAD : AT_HEAD + VP] = dhead_ref[...]
    dscore_scr[...] = jnp.zeros_like(dscore_scr)

    def prepare(index):
        rows = rows_of(index, size)
        wide_scr[rows, :] = spread_fields(field_ref[rows, :])
        merged_scr[rows, :] = dot(grad_ref[rows, :], proj_ref[...], NT)
        out_ref[:, rows] = grad_ref[rows, :].astype(f32).T

    tiles(SEQ // size, prepare)

    def pair(hp):
        lanes = rows_of(hp, LANES)
        table = table_ref[:, lanes]
        total = jnp.zeros((LANES, EXT), f32)
        for which in range(2):
            head = 2 * hp + which
            own = jnp.where(head_mask(EXT, which), table, jnp.zeros_like(table))
            twice = jnp.concatenate([own, own], 1)

            def tile(index):
                rows = rows_of(index, size)
                extended = [wide_scr[rows, j * LANES : (j + 1) * LANES] for j in range(PIX)]
                weight = mix_weights(extended, query_scr, head, valid_ref[...])
                mixing = jnp.concatenate([weight * extended[j] for j in range(PIX)] + [weight], 1)
                high, low = halves(mixing)
                high_scr[rows, :] = high
                low_scr[rows, :] = low
                grad_high, grad_low = halves(merged_scr[rows, lanes])
                dmix = dot(jnp.concatenate([grad_high, grad_low], 1), twice, NT)
                dweight = dmix[:, PIX * LANES :]
                for j in range(PIX):
                    dweight = dweight + dmix[:, j * LANES : (j + 1) * LANES] * extended[j]
                dscore = weight * (dweight - jnp.sum(weight * dweight, -1, keepdims=True))
                for j in range(PIX + 1):
                    piece = dscore * extended[j] if j < PIX else dscore
                    at = pl.ds(j * 8 + head, 1)
                    dscore_scr[at, :] = dscore_scr[at, :] + jnp.sum(piece, 0, keepdims=True)

            tiles(SEQ // size, tile)
            grad_high, grad_low = halves(merged_scr[:, lanes])
            keep = head_mask(SEQ, which)
            grad_high = jnp.where(keep, grad_high, jnp.zeros_like(grad_high))
            grad_low = jnp.where(keep, grad_low, jnp.zeros_like(grad_low))
            both = dot(jnp.concatenate([grad_high, grad_low], 1), high_scr[...], TN)
            total = total + both[:LANES, :] + both[LANES:, :] + dot(grad_high, low_scr[...], TN)
        out_ref[lanes, AT_TABLE:AT_VECTOR] = total

    tiles(PAIRS, pair)
    dquery = jnp.zeros((1, D), f32)
    head = lax.broadcasted_iota(jnp.int32, (8, D), 0)
    lane = lax.broadcasted_iota(jnp.int32, (8, D), 1)
    for j in range(PIX + 1):
        part = dscore_scr[j * 8 : (j + 1) * 8, :]
        block = slice(j * LANES, (j + 1) * LANES)
        lanes = slice(AT_TABLE + j * LANES, AT_TABLE + (j + 1) * LANES)
        out_ref[:, lanes] = out_ref[:, lanes] + lax.dot_general(
            mask, part, TN, precision=highest, preferred_element_type=f32
        )
        spread = lax.dot_general(
            part, table_ref[block, :].astype(f32), NN, precision=highest, preferred_element_type=f32
        )
        dquery = dquery + jnp.sum(jnp.where(lane // HDIM == head, spread, 0.0), 0, keepdims=True)
    vector_scr[...] = jnp.zeros_like(vector_scr)
    vector_scr[0:8, :] = dvector_ref[...]
    vector_scr[0:1, :] = dquery * HDIM ** (-0.5)
    out_ref[:, AT_VECTOR:SLOTS] = vector_scr[...].T


def embed_back(field_rows, table, query_row, valid, proj, agg, grad, dhead, dvector):
    return call(
        embed_back_body,
        shape((D, SLOTS)),
        [
            pltpu.VMEM((LANES, D), f32),
            pltpu.VMEM((40, LANES), f32),
            pltpu.VMEM((SEQ, PIX * LANES), f32),
            pltpu.VMEM((SEQ, D), f32),
            pltpu.VMEM((SEQ, EXT), bf16),
            pltpu.VMEM((SEQ, EXT), bf16),
            pltpu.VMEM((40, LANES), f32),
        ],
        flops=12_000_000_000,
        traffic=6_000_000,
    )(field_rows, table, query_row, valid, proj, agg, grad, dhead, dvector)


def square(ref, index):
    return ref[index * D : (index + 1) * D, :]


def block_body(start, x_ref, gain_ref, packed_ref, *refs):
    *refs, m_ref, h2_ref, y_ref = refs[: 7 if start is None else 8]
    if start is None:
        w_ref = packed_ref
        h_ref, qkv_ref, o_ref, lse_ref = refs
    else:
        w_ref, h_ref, qkv_ref, o_ref, lse_ref = refs
        shards = packed_ref.shape[0]
        rows, tall = D // shards, FF // shards
        above = BLOCKS - FF // D
        for k in range(shards):
            for b in range(above):
                at = start + b * rows
                w_ref[b * D + k * rows : b * D + (k + 1) * rows, :] = packed_ref[k, at : at + rows, :]
            at = start + above * rows
            to = above * D + k * tall
            w_ref[to : to + tall, :] = packed_ref[k, at : at + tall, :]
    size = 256

    def enter(index):
        rows = rows_of(index, size)
        unit, unused = norm_parts(x_ref[rows, :].astype(f32))
        hidden = (unit * gain_ref[0:1, :]).astype(bf16)
        h_ref[rows, :] = hidden
        for b in range(3):
            qkv_ref[rows, b * D : (b + 1) * D] = dot(hidden, square(w_ref, b)).astype(bf16)

    tiles(SEQ // size, enter)
    lse_ref[...] = jnp.zeros_like(lse_ref)

    def pair(hp):
        keys = qkv_ref[:, pl.ds(pl.multiple_of(D + hp * LANES, LANES), LANES)]
        values = qkv_ref[:, pl.ds(pl.multiple_of(2 * D + hp * LANES, LANES), LANES)]

        def tile(index):
            rows = rows_of(index, size)
            queries = qkv_ref[rows, rows_of(hp, LANES)]
            parts = []
            for which in range(2):
                own = jnp.where(head_mask(size, which), queries, jnp.zeros_like(queries))
                score = dot(keys, own, NT) * SCALE2
                peak = jnp.max(score, 0, keepdims=True)
                power = jnp.exp2(score - peak)
                total = jnp.sum(power, 0, keepdims=True)
                chance = (power * (1.0 / total)).astype(bf16)
                mixed = dot(values, chance, TN)
                parts.append(mixed[which * HDIM : (which + 1) * HDIM, :])
                lse_ref[pl.ds(2 * hp + which, 1), rows] = peak + jnp.log2(total)
            o_ref[rows, rows_of(hp, LANES)] = jnp.concatenate(parts, 0).T.astype(bf16)

        tiles(SEQ // size, tile)

    tiles(PAIRS, pair)

    def leave(index):
        rows = rows_of(index, size)
        middle = x_ref[rows, :].astype(f32) + dot(o_ref[rows, :], square(w_ref, 3))
        m_ref[rows, :] = middle
        unit, unused = norm_parts(middle)
        hidden = (unit * gain_ref[1:2, :]).astype(bf16)
        h2_ref[rows, :] = hidden
        total = jnp.zeros((size, D), f32)
        for b in range(FF // D):
            before = dot(hidden, square(w_ref, 4 + b))
            active = (0.5 * before * (1.0 + lax.erf(before * math.sqrt(0.5)))).astype(bf16)
            total = total + dot(active, square(w_ref, 8 + b))
        y_ref[rows, :] = (middle + total).astype(bf16)

    tiles(SEQ // size, leave)


def block_forward(x, gains, weights, start=None):
    return call(
        functools.partial(block_body, start),
        (() if start is None else (shape((BLOCKS * D, D), bf16),))
        + (
            shape((SEQ, D), bf16),
            shape((SEQ, 3 * D), bf16),
            shape((SEQ, D), bf16),
            shape((8, SEQ)),
            shape((SEQ, D)),
            shape((SEQ, D), bf16),
            shape((SEQ, D), bf16),
        ),
        flops=12_000_000_000,
        traffic=12_000_000,
    )(x, gains, weights)


def feed_back_body(h2_ref, m_ref, dy_ref, gain_ref, w_ref, dm_ref, do_ref, dgain_ref, dw_ref, r_scr, df_scr):
    size = 256
    dgain_ref[...] = jnp.zeros_like(dgain_ref)

    def first(index):
        rows = rows_of(index, size)
        grad_next = dy_ref[rows, :]
        hidden = h2_ref[rows, :]
        upstream = jnp.zeros((size, D), f32)
        for b in range(FF // D):
            cols = slice(b * D, (b + 1) * D)
            before = dot(hidden, square(w_ref, 4 + b))
            upper = 0.5 * (1.0 + lax.erf(before * math.sqrt(0.5)))
            r_scr[rows, cols] = (before * upper).astype(bf16)
            slope = upper + before * (jnp.exp2(before * before * (-0.5 * LOG2E)) * (1.0 / math.sqrt(2 * math.pi)))
            grad_before = (dot(grad_next, square(w_ref, 8 + b), NT) * slope).astype(bf16)
            df_scr[rows, cols] = grad_before
            upstream = upstream + dot(grad_before, square(w_ref, 4 + b), NT)
        back, dgain = norm_back(m_ref[rows, :], gain_ref[1:2, :], upstream)
        dgain_ref[...] = dgain_ref[...] + dgain
        middle = grad_next.astype(f32) + back
        dm_ref[rows, :] = middle
        do_ref[rows, :] = dot(middle.astype(bf16), square(w_ref, 3), NT).astype(bf16)

    tiles(SEQ // size, first)

    def wide(index):
        cols = rows_of(index, D)
        dw_ref[rows_of(index, D), :] = dot(h2_ref[...], df_scr[:, cols], TN)
        dw_ref[rows_of(FF // D + index, D), :] = dot(r_scr[:, cols], dy_ref[...], TN)

    tiles(FF // D, wide)


def feed_back(h2, m, dy, gains, weights):
    return call(
        feed_back_body,
        (shape((SEQ, D)), shape((SEQ, D), bf16), shape((1, D)), shape((2 * FF, D))),
        [pltpu.VMEM((SEQ, FF), bf16), pltpu.VMEM((SEQ, FF), bf16)],
        flops=17_000_000_000,
        traffic=14_000_000,
    )(h2, m, dy, gains, weights)


def mix_back_body(x_ref, h_ref, qkv_ref, o_ref, lse_ref, dm_ref, do_ref, gain_ref, w_ref,
                  dx_ref, dgain_ref, dw_ref, dqkv_scr, dkv_scr):
    size = 256
    dgain_ref[...] = jnp.zeros_like(dgain_ref)
    dw_ref[3 * D : 4 * D, :] = dot(o_ref[...], dm_ref[...].astype(bf16), TN)

    def pair(hp):
        lanes = rows_of(hp, LANES)
        klanes = pl.ds(pl.multiple_of(D + hp * LANES, LANES), LANES)
        vlanes = pl.ds(pl.multiple_of(2 * D + hp * LANES, LANES), LANES)
        keys = qkv_ref[:, klanes]
        values = qkv_ref[:, vlanes]
        dkv_scr[...] = jnp.zeros_like(dkv_scr)

        def tile(index):
            rows = rows_of(index, size)
            queries = qkv_ref[rows, lanes]
            upstream = do_ref[rows, lanes]
            parts = []
            for which in range(2):
                keep = head_mask(size, which)
                own = jnp.where(keep, queries, jnp.zeros_like(queries))
                own_up = jnp.where(keep, upstream, jnp.zeros_like(upstream))
                score = dot(keys, own, NT) * SCALE2
                chance = jnp.exp2(score - lse_ref[pl.ds(2 * hp + which, 1), rows])
                dchance = dot(values, own_up, NT)
                shift = jnp.sum(dchance * chance, 0, keepdims=True)
                dscore = (chance * (dchance - shift)).astype(bf16)
                dkv_scr[:, :LANES] = dkv_scr[:, :LANES] + dot(dscore, own)
                dkv_scr[:, LANES:] = dkv_scr[:, LANES:] + dot(chance.astype(bf16), own_up)
                dquery = dot(keys, dscore, TN)
                parts.append(dquery[which * HDIM : (which + 1) * HDIM, :])
            dqkv_scr[rows, lanes] = (jnp.concatenate(parts, 0).T * HDIM ** (-0.5)).astype(bf16)

        tiles(SEQ // size, tile)
        dqkv_scr[:, klanes] = (dkv_scr[:, :LANES] * HDIM ** (-0.5)).astype(bf16)
        dqkv_scr[:, vlanes] = dkv_scr[:, LANES:].astype(bf16)

    tiles(PAIRS, pair)

    def third(index):
        cols = rows_of(index, D)
        dw_ref[cols, :] = dot(h_ref[...], dqkv_scr[:, cols], TN)

    tiles(3, third)

    def last(index):
        rows = rows_of(index, size)
        upstream = jnp.zeros((size, D), f32)
        for b in range(3):
            upstream = upstream + dot(dqkv_scr[rows, b * D : (b + 1) * D], square(w_ref, b), NT)
        back, dgain = norm_back(x_ref[rows, :].astype(f32), gain_ref[0:1, :], upstream)
        dgain_ref[...] = dgain_ref[...] + dgain
        dx_ref[rows, :] = (dm_ref[rows, :] + back).astype(bf16)

    tiles(SEQ // size, last)


def mix_back(x, kept, dm, do, gains, weights):
    return call(
        mix_back_body,
        (shape((SEQ, D), bf16), shape((1, D)), shape((4 * D, D))),
        [pltpu.VMEM((SEQ, 3 * D), bf16), pltpu.VMEM((SEQ, 2 * LANES), f32)],
        flops=17_000_000_000,
        traffic=14_000_000,
    )(x, *kept, dm, do, gains, weights)


def head_body(y_ref, gain_ref, head_ref, target_ref, cos_ref, valid_ref,
              dy_ref, dhead_ref, dgain_ref, error_ref, h_scr, dp_scr):
    size = 256
    dgain_ref[...] = jnp.zeros_like(dgain_ref)
    error_ref[...] = jnp.zeros_like(error_ref)

    def tile(index):
        rows = rows_of(index, size)
        values = y_ref[rows, :].astype(f32)
        unit, unused = norm_parts(values)
        hidden = (unit * gain_ref[...]).astype(bf16)
        h_scr[rows, :] = hidden
        residual = dot(hidden, head_ref[...], NT) - target_ref[rows, :].astype(f32)
        lane = lax.broadcasted_iota(jnp.int32, (size, VP), 1)
        cosine = jnp.where(lane % PIX < 2, cos_ref[rows, 0:1], cos_ref[rows, 1:2])
        weight = cosine * valid_ref[...]
        error_ref[...] = error_ref[...] + jnp.sum(weight * residual * residual, 0, keepdims=True)
        grad = (2.0 * weight * residual).astype(bf16)
        dp_scr[rows, :] = grad
        back, dgain = norm_back(values, gain_ref[...], dot(grad, head_ref[...]))
        dgain_ref[...] = dgain_ref[...] + dgain
        dy_ref[rows, :] = back.astype(bf16)

    tiles(SEQ // size, tile)
    dhead_ref[...] = dot(h_scr[...], dp_scr[...], TN)


def head_step(y, gain, head_rows, target, cosines, valid):
    return call(
        head_body,
        (shape((SEQ, D), bf16), shape((D, VP)), shape((1, D)), shape((1, VP))),
        [pltpu.VMEM((SEQ, D), bf16), pltpu.VMEM((SEQ, VP), bf16)],
        flops=700_000_000,
        traffic=4_000_000,
    )(y, gain, head_rows, target, cosines, valid)


def dot3(left, right, dims=NN):
    return dot(left[0], right[0], dims) + dot(left[0], right[1], dims) + dot(left[1], right[0], dims)


def chosen_rows(count, width, start, offset):
    row = lax.broadcasted_iota(jnp.int32, (count, width), 0)
    col = lax.broadcasted_iota(jnp.int32, (count, width), 1)
    return jnp.where(col + offset == row + start, 1.0, 0.0).astype(bf16)


def pick(selector, pair, dims=NN):
    return [dot(selector, part, dims).astype(bf16) for part in pair]


def shampoo_body(along, index_ref, factor_ref, small_ref, qkv_ref, wide_ref, around_ref,
                 left_out_ref, left_fc2_ref, right_qkv_ref, right_fc1_ref,
                 wout_ref, wfc2_ref, eout_ref, efc2_ref, piece_ref,
                 nsmall_ref, nqkv_ref, nwide_ref, nout_ref, nfc2_ref, meout_ref, mefc2_ref,
                 step_ref, high_scr, low_scr):
    pieces = piece_ref.shape[1]
    me = index_ref[0]
    factor = factor_ref[0]
    wide_rows, tall_rows = 2 * FF // (pieces * along), 4 * D // (pieces * along)
    for k in range(pieces):
        block = jnp.bitwise_xor(index_ref[1], k) * along
        for j in range(along):
            place = block + jnp.bitwise_xor(index_ref[2], j)
            at = j * (wide_rows + tall_rows)
            high, low = halves(piece_ref[0, k, at : at + wide_rows, :])
            rows = pl.ds(pl.multiple_of(4 * D + place * wide_rows, 16), wide_rows)
            high_scr[rows, :] = high
            low_scr[rows, :] = low
            high, low = halves(piece_ref[0, k, at + wide_rows : at + wide_rows + tall_rows, :])
            rows = pl.ds(pl.multiple_of(place * tall_rows, 16), tall_rows)
            high_scr[rows, :] = high
            low_scr[rows, :] = low

    def grad(b):
        return square(high_scr, b), square(low_scr, b)

    def mixed(old, product):
        return stat_beta * old + (1.0 - stat_beta) * (factor * (factor * product))

    def root(k):
        return halves(around_ref[0, k])

    rows = small_ref.shape[2]
    own_row = chosen_rows(rows, D, me * rows, 0)

    def own_part(first, count):
        if count % 16:
            selector = chosen_rows(count, D, me * count, first)
            return lambda b: pick(selector, grad(b))
        return lambda b: [
            scr[pl.ds(pl.multiple_of(b * D + me * count, 16), count), :] for scr in (high_scr, low_scr)
        ]

    own_rows = own_part(0, rows)
    place = 0
    for first, count, left, right_ref, nright_ref, right_root_ref, left_root in (
        (0, 3, 0, qkv_ref, nqkv_ref, right_qkv_ref, 0),
        (4, FF // D, 3, wide_ref, nwide_ref, right_fc1_ref, 3),
    ):
        take = (0, 0) if first else (0,)
        cols = right_ref.shape[-2]
        total = jnp.zeros((rows, D), f32)
        own_cols = [jnp.zeros((cols, D), f32)] * 2
        share = right_root_ref.shape[-2]
        reach = jnp.zeros((D, share), f32)
        for b in range(count):
            block = grad(first + b)
            total = total + dot3(own_rows(first + b), block, NT)
            selector = chosen_rows(cols, D, me * cols, b * D)
            own_cols = [own + dot(selector, part, NT) for own, part in zip(own_cols, block)]
            reach = reach + dot3(block, halves(right_root_ref[take + (slice(None), slice(b * D, (b + 1) * D))]), NT)
        nsmall_ref[0, left] = mixed(small_ref[0, left], total)
        own_cols = [own.astype(bf16) for own in own_cols]
        for b in range(count):
            lanes = slice(b * D, (b + 1) * D)
            nright_ref[take + (slice(None), lanes)] = mixed(
                right_ref[take + (slice(None), lanes)], dot3(own_cols, grad(first + b))
            )
        step_ref[0, :, place : place + share] = dot3(root(left_root), halves(reach))
        place = place + share

    block = grad(3)
    nsmall_ref[0, 1] = mixed(small_ref[0, 1], dot3(own_rows(3), block, NT))
    nsmall_ref[0, 2] = mixed(small_ref[0, 2], dot3(pick(own_row, block, NT), block))
    moved = dot3(halves(dot3(halves(left_out_ref[0, 0]), block)), root(2))
    updated = wout_ref[0] - rate_matrix * factor * moved
    nout_ref[0] = updated
    meout_ref[0] = average(eout_ref[0], updated)

    tall = wide_ref.shape[2]
    total = jnp.zeros((rows, D), f32)
    own = [jnp.zeros((tall, D), f32)] * 2
    reach = jnp.zeros((tall, D), f32)
    whole = tall % 16 == 0
    for b in range(FF // D):
        block = grad(8 + b)
        total = total + dot3(pick(own_row, block, NT), block)
        if not whole:
            selector = chosen_rows(tall, D, me * tall, b * D)
            own = [o + dot(selector, part) for o, part in zip(own, block)]
        reach = reach + dot3(halves(left_fc2_ref[0, 0, :, b * D : (b + 1) * D]), block)
    nsmall_ref[0, 4] = mixed(small_ref[0, 4], total)
    own = own_part(0, tall)(8) if whole else [o.astype(bf16) for o in own]
    for b in range(FF // D):
        lanes = slice(b * D, (b + 1) * D)
        nwide_ref[0, 1, :, lanes] = mixed(wide_ref[0, 1, :, lanes], dot3(own, grad(8 + b), NT))
    updated = wfc2_ref[0] - rate_matrix * factor * dot3(halves(reach), root(4))
    nfc2_ref[0] = updated
    mefc2_ref[0] = average(efc2_ref[0], updated)


def layer_block(array, *second):
    lead = len(second)
    dims = (1,) * (1 + lead) + array.shape[1 + lead :]
    return pl.BlockSpec(dims, lambda i: (i,) + second + (0,) * (array.ndim - 1 - lead))


def shampoo(pieces, along, index, factor, stats, around, roots, weights, averages):
    small, qkv, wide = stats
    root_small, root_qkv, root_wide = roots
    scalar = pl.BlockSpec(memory_space=pltpu.SMEM)
    layered = [small, qkv, wide, around]
    tails = [*weights, *averages, pieces]
    results = [small, qkv, wide, *weights, *averages]
    specs = [scalar, scalar] + [layer_block(x) for x in layered]
    specs += [layer_block(root_small, 1), layer_block(root_wide, 1), layer_block(root_qkv), layer_block(root_wide, 0)]
    specs += [layer_block(x) for x in tails]
    step = shape((LAYERS, D, root_qkv.shape[1] + root_wide.shape[2]))
    return pl.pallas_call(
        functools.partial(shampoo_body, along),
        grid=(LAYERS,),
        in_specs=specs,
        out_specs=[layer_block(x) for x in [*results, step]],
        out_shape=[shape(x.shape) for x in results] + [step],
        scratch_shapes=[pltpu.VMEM((BLOCKS * D, D), bf16)] * 2,
        compiler_params=pltpu.CompilerParams(vmem_limit_bytes=62 << 20),
        cost_estimate=pl.CostEstimate(flops=10_000_000_000, bytes_accessed=60_000_000, transcendentals=0),
    )(index, factor, *layered, root_small, root_wide, root_qkv, root_wide, *tails)


def close_body(feed1_ref, mix1_ref, feed0_ref, mix0_ref, turned_ref, scalar_ref,
               out_ref, outd_ref, outs_ref,
               own1_scr, own0_scr, feed1_scr, mix1_scr, feed_scr, mix_scr, mixz_scr, dense_scr, core_scr, cross_scr, along_scr,
               mix_sum, dense_sum, own_dense, own_scalar,
               pass_feed, pass_feed1, pass_mix, pass_mix1, pass_dense, send_sem, recv_sem, local_sem):
    s = lax.axis_index("section")
    dp = lax.axis_index("dp")
    z, c = dp // 2, dp % 2
    mine = c * 4 + s
    rows = own0_scr.shape[0]
    out0_ref, out1_ref = out_ref.at[0], out_ref.at[1]
    feed_rows, mix_rows = feed0_ref.shape[0] // 4, mix0_ref.shape[0] // 16
    width = turned_ref.shape[2]
    span = SLOTS // 4
    peers = [{"section": s, "dp": jnp.bitwise_xor(dp, 1)}]
    peers += [{"section": jnp.bitwise_xor(s, k), "dp": dp} for k in (1, 2, 3)]
    peers += [{"section": s, "dp": jnp.bitwise_xor(dp, 2 * k)} for k in (1, 2, 3)]
    barrier = pltpu.get_barrier_semaphore()
    for peer in peers:
        pl.semaphore_signal(barrier, inc=1, device_id=peer, device_id_type=pl.DeviceIdType.MESH)
    pl.semaphore_wait(barrier, len(peers))
    count = [0, 0]
    sent = []

    def send(source, target, peer):
        n = count[0]
        count[0] = n + 1
        copy = pltpu.make_async_remote_copy(
            src_ref=source, dst_ref=target, send_sem=send_sem.at[n], recv_sem=recv_sem.at[n],
            device_id=peer, device_id_type=pl.DeviceIdType.MESH,
        )
        copy.start()
        sent.append(copy)
        return copy

    def keep(source, target):
        n = count[1]
        count[1] = n + 1
        copy = pltpu.make_async_copy(source, target, local_sem.at[n])
        copy.start()
        return copy

    def arrive(copies):
        for copy in copies:
            copy.wait_recv()

    def across(k):
        return jnp.bitwise_xor(s, k)

    def up(k):
        return jnp.bitwise_xor(z, k)

    def at(index, size, align):
        return pl.ds(pl.multiple_of(index * size, align), size)

    core, (x, y, diagonal), tower = peers[0], peers[1:4], peers[4:]
    flat = (x, y, diagonal)

    def gather_up(own_ref, out_ref):
        place = out_ref.at[mine, at(z, rows, 16), :]
        local = keep(own_ref, place)
        return local, [send(own_ref, place, peer) for peer in tower[:2]]

    def gather_flat(out_ref, started):
        local, copies = started
        local.wait()
        near, far = copies
        far.wait_recv()
        place = out_ref.at[mine, at(up(2), rows, 16), :]
        passed = send(place, place, tower[0])
        near.wait_recv()
        passed.wait_recv()
        block = out_ref.at[mine]
        found = [send(block, block, x), send(block, block, y)]
        send_core = [send(block, block, core)]
        return found, send_core

    def gather_turn(out_ref, started):
        (from_x, from_y), to_core = started
        half = 2 * rows
        from_x.wait_recv()
        block_x = c * 4 + across(1)
        upper = out_ref.at[block_x, pl.ds(0, half), :]
        turn_y = send(upper, upper, y)
        to_core.append(send(out_ref.at[block_x], out_ref.at[block_x], core))
        from_y.wait_recv()
        block_y = c * 4 + across(2)
        lower = out_ref.at[block_y, pl.ds(half, half), :]
        turn_x = send(lower, lower, x)
        to_core.append(send(out_ref.at[block_y], out_ref.at[block_y], core))
        return [turn_y, turn_x], to_core

    def gather_core(out_ref, started):
        turned, to_core = started
        arrive(turned)
        block = out_ref.at[c * 4 + across(3)]
        return to_core + [send(block, block, core)]


    def climb(view, slots):
        return [send(view(up(1)), slots.at[0], tower[0]), send(view(up(3)), slots.at[1], tower[0])]

    def climb_more(view, slots, pass_ref, started):
        arrive(started)
        pass_ref[...] = view(up(2))[...] + slots[1]
        return send(pass_ref, slots.at[2], tower[1])

    def climb_end(view, slots, started):
        started.wait_recv()
        return view(z)[...] + slots[0] + slots[2]

    def part_of(ref, size):
        return lambda k: ref.at[at(k, size, 16), :]

    feed1, mix1, feed0 = part_of(feed1_ref, feed_rows), part_of(mix1_ref, mix_rows), part_of(feed0_ref, feed_rows)
    mix0 = part_of(mix_sum, mix_rows)
    feed_up = climb(feed0, feed_scr)
    feed1_up = climb(feed1, feed1_scr)
    mix1_up = climb(mix1, mix1_scr)
    dense_core = send(turned_ref.at[:, 1 - c], core_scr, core)
    mix_flat = [
        send(mix0_ref.at[at(across(k), 4 * mix_rows, 16), :], mix_scr.at[k - 1], flat[k - 1]) for k in (1, 2, 3)
    ]
    dense_core.wait_recv()

    def add_core(k):
        dense_sum[k] = turned_ref[k, c] + core_scr[k]

    tiles(4, add_core)
    dense_flat = [
        send(dense_sum.at[:, :, at(across(k), span, LANES)], cross_scr.at[k - 1], flat[k - 1]) for k in (1, 2, 3)
    ]
    feed_up = climb_more(feed0, feed_scr, pass_feed, feed_up)
    feed1_up = climb_more(feed1, feed1_scr, pass_feed1, feed1_up)
    mix1_up = climb_more(mix1, mix1_scr, pass_mix1, mix1_up)
    arrive(mix_flat)
    mix_sum[...] = mix0_ref[at(s, 4 * mix_rows, 16), :] + mix_scr[0] + mix_scr[1] + mix_scr[2]
    mix_up = climb(mix0, mixz_scr)
    own1_scr[0:feed_rows, :] = climb_end(feed1, feed1_scr, feed1_up)
    own1_scr[feed_rows:rows, :] = climb_end(mix1, mix1_scr, mix1_up)
    up1 = gather_up(own1_scr, out1_ref)
    mix_up = climb_more(mix0, mixz_scr, pass_mix, mix_up)
    own0_scr[0:feed_rows, :] = climb_end(feed0, feed_scr, feed_up)
    own0_scr[feed_rows:rows, :] = climb_end(mix0, mixz_scr, mix_up)
    up0 = gather_up(own0_scr, out0_ref)
    flat1 = gather_flat(out1_ref, up1)
    arrive(dense_flat)

    def add_flat(k):
        mid = dense_sum[k, :, at(s, span, LANES)]
        dense_scr[k] = mid + cross_scr[0, k] + cross_scr[1, k] + cross_scr[2, k]

    tiles(4, add_flat)
    dense_view = lambda k: dense_scr.at[k]
    dense_up = climb(dense_view, along_scr)
    flat0 = gather_flat(out0_ref, up0)
    dense_up = climb_more(dense_view, along_scr, pass_dense, dense_up)
    turn1 = gather_turn(out1_ref, flat1)
    own_dense[...] = climb_end(dense_view, along_scr, dense_up)
    home = outd_ref.at[s]
    local_dense = keep(own_dense, home)
    spread_dense = [send(own_dense, home, peer) for peer in flat]
    total = jnp.zeros((1, 1), f32)
    for part in (own1_scr[...], own0_scr[...], own_dense[...]):
        total = total + jnp.sum(jnp.sum(part * part, 0, keepdims=True), 1, keepdims=True)
    lane = lax.broadcasted_iota(jnp.int32, (8, LANES), 1)
    own_scalar[...] = jnp.where(lane == 0, total, scalar_ref[...])
    home = outs_ref.at[c, s, z]
    local_scalar = keep(own_scalar, home)
    scalar_up = [send(own_scalar, home, peer) for peer in tower]
    local_scalar.wait()
    arrive(scalar_up)
    home = outs_ref.at[c, s]
    scalar_flat = [send(home, home, peer) for peer in flat]
    turn0 = gather_turn(out0_ref, flat0)
    core1 = gather_core(out1_ref, turn1)
    arrive(scalar_flat)
    home = outs_ref.at[c]
    scalar_core = send(home, home, core)
    core0 = gather_core(out0_ref, turn0)
    local_dense.wait()
    arrive(spread_dense)
    arrive(core1)
    arrive(core0)
    scalar_core.wait_recv()
    for copy in sent:
        copy.wait_send()


def close_exchange(feed1, mix1, feed0, mix0, turned, scalars):
    feed_rows, mix_rows = feed0.shape[0] // 4, mix0.shape[0] // 16
    rows = feed_rows + mix_rows
    width, span = turned.shape[2], SLOTS // 4
    anywhere = pl.BlockSpec(memory_space=pl.ANY)
    copies = 54
    return pl.pallas_call(
        close_body,
        in_specs=[pl.BlockSpec(memory_space=pltpu.VMEM)] * 6,
        out_specs=[anywhere] * 3,
        out_shape=[
            shape((2, 8, 4 * rows, D)), shape((4, width, span)), shape((2, 4, 4, 8, LANES)),
        ],
        scratch_shapes=[
            pltpu.VMEM((rows, D), f32),
            pltpu.VMEM((rows, D), f32),
            pltpu.VMEM((3, feed_rows, D), f32),
            pltpu.VMEM((3, mix_rows, D), f32),
            pltpu.VMEM((3, feed_rows, D), f32),
            pltpu.VMEM((3, 4 * mix_rows, D), f32),
            pltpu.VMEM((3, mix_rows, D), f32),
            pltpu.VMEM((4, width, span), f32),
            pltpu.VMEM((4, width, SLOTS), f32),
            pltpu.VMEM((3, 4, width, span), f32),
            pltpu.VMEM((3, width, span), f32),
            pltpu.VMEM((4 * mix_rows, D), f32),
            pltpu.VMEM((4, width, SLOTS), f32),
            pltpu.VMEM((width, span), f32),
            pltpu.VMEM((8, LANES), f32),
            pltpu.VMEM((feed_rows, D), f32),
            pltpu.VMEM((feed_rows, D), f32),
            pltpu.VMEM((mix_rows, D), f32),
            pltpu.VMEM((mix_rows, D), f32),
            pltpu.VMEM((width, span), f32),
            pltpu.SemaphoreType.DMA((copies,)),
            pltpu.SemaphoreType.DMA((copies,)),
            pltpu.SemaphoreType.DMA((4,)),
        ],
        compiler_params=pltpu.CompilerParams(
            vmem_limit_bytes=60 << 20, collective_id=0, has_side_effects=True
        ),
        cost_estimate=pl.CostEstimate(flops=10_000_000, bytes_accessed=300_000_000, transcendentals=0),
    )(feed1, mix1, feed0, mix0, turned, scalars)


def turn_body(step_ref, out_ref, send_sem, recv_sem, local_sem):
    s = lax.axis_index("section")
    dp = lax.axis_index("dp")
    half, parts = out_ref.shape[2], out_ref.shape[1]
    x, y = [{"section": jnp.bitwise_xor(s, k), "dp": dp} for k in (1, 2)]
    peers = [{"section": s, "dp": jnp.bitwise_xor(dp, k)} for k in range(8)]
    barrier = pltpu.get_barrier_semaphore()
    for peer in [x, y, *peers[1:]]:
        pl.semaphore_signal(barrier, inc=1, device_id=peer, device_id_type=pl.DeviceIdType.MESH)
    pl.semaphore_wait(barrier, len(peers) + 1)
    sent = []

    def send(source, target, peer):
        n = len(sent)
        copy = pltpu.make_async_remote_copy(
            src_ref=source, dst_ref=target, send_sem=send_sem.at[n], recv_sem=recv_sem.at[n],
            device_id=peer, device_id_type=pl.DeviceIdType.MESH,
        )
        copy.start()
        sent.append(copy)
        return copy

    def source(k):
        start = pl.multiple_of(jnp.bitwise_xor(dp, k) * 2 * half + (s % 2) * half, 8)
        return step_ref.at[s // 2, pl.ds(start, half), :]

    own = out_ref.at[s]
    local = pltpu.make_async_copy(source(0), own.at[dp], local_sem)
    local.start()
    around = [send(source(k), own.at[dp], peers[k]) for k in (4, 6, 5, 7, 2, 3, 1)]
    local.wait()
    for copy in around:
        copy.wait_recv()
    from_x, from_y = send(own, own, x), send(own, own, y)
    from_x.wait_recv()
    piece = out_ref.at[jnp.bitwise_xor(s, 1), pl.ds(0, parts // 2)]
    upper = send(piece, piece, y)
    from_y.wait_recv()
    piece = out_ref.at[jnp.bitwise_xor(s, 2), pl.ds(parts // 2, parts // 2)]
    lower = send(piece, piece, x)
    upper.wait_recv()
    lower.wait_recv()
    for copy in sent:
        copy.wait_send()


def turn_exchange(step):
    layers, rows, lanes = step.shape
    copies = 7 + 2 + 2
    return pl.pallas_call(
        turn_body,
        in_specs=[pl.BlockSpec(memory_space=pl.ANY)],
        out_specs=pl.BlockSpec(memory_space=pl.ANY),
        out_shape=shape((2 * layers, 8, rows // 16, lanes)),
        scratch_shapes=[
            pltpu.SemaphoreType.DMA((copies,)), pltpu.SemaphoreType.DMA((copies,)), pltpu.SemaphoreType.DMA,
        ],
        compiler_params=pltpu.CompilerParams(vmem_limit_bytes=60 << 20, collective_id=1, has_side_effects=True),
        cost_estimate=pl.CostEstimate(flops=1000, bytes_accessed=80_000_000, transcendentals=0),
    )(step)


def open_body(part_ref, out_ref, send_sem, recv_sem, local_sem):
    s = lax.axis_index("section")
    dp = lax.axis_index("dp")
    z, c = dp // 2, dp % 2
    rows = part_ref.shape[0] // 4
    core = {"section": s, "dp": jnp.bitwise_xor(dp, 1)}
    flat = [{"section": jnp.bitwise_xor(s, k), "dp": dp} for k in (1, 2)]
    tower = [{"section": s, "dp": jnp.bitwise_xor(dp, 2 * k)} for k in (1, 2, 3)]
    peers = [core, *flat, *tower]
    barrier = pltpu.get_barrier_semaphore()
    for peer in peers:
        pl.semaphore_signal(barrier, inc=1, device_id=peer, device_id_type=pl.DeviceIdType.MESH)
    pl.semaphore_wait(barrier, len(peers))
    sent = []

    def send(source, target, peer):
        n = len(sent)
        copy = pltpu.make_async_remote_copy(
            src_ref=source, dst_ref=target, send_sem=send_sem.at[n], recv_sem=recv_sem.at[n],
            device_id=peer, device_id_type=pl.DeviceIdType.MESH,
        )
        copy.start()
        sent.append(copy)
        return copy

    def place(k, across):
        return out_ref.at[jnp.bitwise_xor(z, k), c, jnp.bitwise_xor(s, across)]

    own = part_ref.at[pl.ds(pl.multiple_of(s * rows, 16), rows), :]
    upward = [send(own, place(0, 0), peer) for peer in tower]
    local = pltpu.make_async_copy(own, place(0, 0), local_sem)
    local.start()
    local.wait()
    half = rows // 32 * 16
    crossed, ended = [], []
    for k in range(4):
        if k:
            upward[k - 1].wait_recv()
        crossed.append([send(place(k, 0), place(k, 0), peer) for peer in flat])
        ended.append(send(place(k, 0), place(k, 0), core))
    for k in range(4):
        from_x, from_y = crossed[k]
        from_x.wait_recv()
        piece = place(k, 1).at[0:half]
        turned = [send(piece, piece, flat[1])]
        ended.append(send(place(k, 1), place(k, 1), core))
        from_y.wait_recv()
        piece = place(k, 2).at[half:rows]
        turned.append(send(piece, piece, flat[0]))
        ended.append(send(place(k, 2), place(k, 2), core))
        crossed[k] = turned
    for k in range(4):
        for copy in crossed[k]:
            copy.wait_recv()
        ended.append(send(place(k, 3), place(k, 3), core))
    for copy in ended:
        copy.wait_recv()
    for copy in sent:
        copy.wait_send()


def open_exchange(part):
    rows = part.shape[0]
    copies = 3 + 8 + 8 + 16
    return pl.pallas_call(
        open_body,
        in_specs=[pl.BlockSpec(memory_space=pl.ANY)],
        out_specs=pl.BlockSpec(memory_space=pl.ANY),
        out_shape=shape((4, 2, 4, rows // 4, D), bf16),
        scratch_shapes=[
            pltpu.SemaphoreType.DMA((copies,)), pltpu.SemaphoreType.DMA((copies,)), pltpu.SemaphoreType.DMA,
        ],
        compiler_params=pltpu.CompilerParams(vmem_limit_bytes=60 << 20, collective_id=2, has_side_effects=True),
        cost_estimate=pl.CostEstimate(flops=1000, bytes_accessed=80_000_000, transcendentals=0),
    )(part).reshape(8, rows, D)


def finish_body(parts, factor_ref, found_ref, *refs):
    (wqkv_ref, wfc1_ref, eqkv_ref, efc1_ref, nqkv_ref, nfc1_ref, mqkv_ref, mfc1_ref) = refs
    scale = rate_matrix * factor_ref[0]
    cuts, tall = found_ref.shape[0] // LAYERS, found_ref.shape[2]
    for layer in range(LAYERS):
        place = 0
        for w_ref, e_ref, n_ref, a_ref in (
            (wqkv_ref, eqkv_ref, nqkv_ref, mqkv_ref), (wfc1_ref, efc1_ref, nfc1_ref, mfc1_ref)
        ):
            share = w_ref.shape[2] // parts
            for j in range(parts):
                lanes = slice(j * share, (j + 1) * share)
                for cut in range(cuts):
                    rows = slice(cut * tall, (cut + 1) * tall)
                    step = found_ref[layer * cuts + cut, j, :, place : place + share]
                    updated = w_ref[layer, rows, lanes] - scale * step
                    n_ref[layer, rows, lanes] = updated
                    a_ref[layer, rows, lanes] = average(e_ref[layer, rows, lanes], updated)
            place = place + share


def finish(parts, factor, found, weights, averages):
    scalar = pl.BlockSpec(memory_space=pltpu.SMEM)
    operands = [found, *weights, *averages]
    return pl.pallas_call(
        functools.partial(finish_body, parts),
        in_specs=[scalar] + [pl.BlockSpec(memory_space=pltpu.VMEM)] * len(operands),
        out_shape=[shape(x.shape) for x in (*weights, *averages)],
        compiler_params=pltpu.CompilerParams(vmem_limit_bytes=60 << 20),
        cost_estimate=pl.CostEstimate(flops=10_000_000, bytes_accessed=6_000_000, transcendentals=0),
    )(factor, *operands)


def adam_body(index_ref, scalar_ref, pieces_ref, *refs):
    dense, vectors, new_dense, new_vectors, turned_scr, gradient_scr = (
        refs[:4], refs[4:8], refs[8:12], refs[12:16], refs[16], refs[17]
    )
    width, count = dense[0].shape
    span = pieces_ref.shape[2]
    for k in range(pieces_ref.shape[0]):
        place = jnp.bitwise_xor(index_ref[3], k)
        lanes = pl.ds(pl.multiple_of(place * span, LANES), span)
        turned_scr[:, lanes] = pieces_ref[k, 0:width, :]
    row = lax.broadcasted_iota(jnp.int32, (EXT, TABLE), 0)
    col = lax.broadcasted_iota(jnp.int32, (EXT, TABLE), 1)
    mixed = (row % LANES) * (PIX + 1) + row // LANES == col
    mixed = jnp.where(mixed & (row % LANES < VARS), 1.0, 0.0)
    gradient_scr[:, 0:TABLE] = lax.dot_general(
        turned_scr[:, AT_TABLE:AT_VECTOR], mixed, NN, precision=highest, preferred_element_type=f32
    )
    gradient_scr[:, TABLE : TABLE + AT_HEAD + VP] = turned_scr[:, 0 : AT_HEAD + VP]

    def update(refs, news, gradient, rate, decay):
        old = [ref[...] for ref in refs]
        gradient = gradient * scalar_ref[0]
        first = beta_first * old[1] + (1.0 - beta_first) * gradient
        second = beta_second * old[2] + (1.0 - beta_second) * gradient * gradient
        first_hat = first / scalar_ref[1]
        second_hat = second / scalar_ref[2]
        updated = old[0] - rate * (first_hat / (jnp.sqrt(second_hat) + adam_eps) + decay * old[0])
        for ref, value in zip(news, (updated, first, second, average(old[3], updated))):
            ref[...] = value

    update(dense, new_dense, gradient_scr[...], rate_dense, weight_decay)
    few = vectors[0].shape[0]
    row = lax.broadcasted_iota(jnp.int32, (width, width), 0)
    col = lax.broadcasted_iota(jnp.int32, (width, width), 1)
    back = lax.dot_general(
        turned_scr[:, AT_VECTOR:SLOTS], jnp.where(row == col, 1.0, 0.0), TN,
        precision=highest, preferred_element_type=f32,
    )
    update(vectors, new_vectors, back[0:few, :], rate_vector, 0.0)


def adam(index, scalars, pieces, dense, vectors):
    scalar = pl.BlockSpec(memory_space=pltpu.SMEM)
    states = [x.T for x in dense] + list(vectors)
    width, count = states[0].shape
    *new_dense, v0, v1, v2, v3 = pl.pallas_call(
        adam_body,
        in_specs=[scalar, scalar] + [pl.BlockSpec(memory_space=pltpu.VMEM)] * (1 + len(states)),
        out_shape=[shape(x.shape) for x in states],
        scratch_shapes=[pltpu.VMEM((width, SLOTS), f32), pltpu.VMEM((width, count), f32)],
        compiler_params=pltpu.CompilerParams(vmem_limit_bytes=60 << 20),
        cost_estimate=pl.CostEstimate(flops=10_000_000, bytes_accessed=8_000_000, transcendentals=0),
    )(index, scalars, pieces, *states)
    return [new.T for new in new_dense] + [v0, v1, v2, v3]


def digits(count, start=1):
    found = []
    while start < count:
        radix = min(4, count // start)
        found.append((start, radix))
        start *= radix
    return found


def swap(values, axis, bits):
    return lax.ppermute(values, axis, [(k, k ^ bits) for k in range(lax.axis_size(axis))])


def digit(axis, bit, radix):
    return (lax.axis_index(axis) // bit) % radix


def share_out(values, dim, axis, bit, radix):
    size = values.shape[dim] // radix
    mine = digit(axis, bit, radix)

    def part(k):
        return lax.dynamic_slice_in_dim(values, jnp.bitwise_xor(mine, k) * size, size, dim)

    arrived = [swap(part(k), axis, k * bit) for k in range(1, radix)]
    total = part(0)
    for other in arrived:
        total = total + other
    return total


def collect(values, axis, bit, radix):
    return [values] + [swap(values, axis, k * bit) for k in range(1, radix)]


def in_order(found, place):
    low = 1
    while low < len(found):
        even = (place // low) % 2 == 0
        found = [jnp.where(even, found[k], found[k ^ low]) for k in range(len(found))]
        low *= 2
    return found


def gate(values, first):
    return lax.optimization_barrier((values, first))


def advance(values, sums, wanted=None):
    wanted = [k for k in range(len(sums)) if sums[k][1] and (wanted is None or k in wanted)]
    moved = [share_out(sums[k][0], 0, *sums[k][1][0]) for k in wanted]
    values, moved = gate(values, moved)
    sums = list(sums)
    for k, part in zip(wanted, moved):
        sums[k] = [part, sums[k][1][1:]]
    return values, sums


def total_of(values, stages):
    for axis, bit, radix in stages:
        values = sum(in_order(collect(values, axis, bit, radix), digit(axis, bit, radix)))
    return values


def valid_flags(counts):
    var_index = jnp.arange(VARS)
    level_index = (var_index - SURF) % LEVELS
    inside = (var_index[None, :] < SURF) | (level_index[None, :] < counts[:, None])
    return jnp.where(inside, 1.0, 0.0).astype(f32)


def cosine_table():
    pixel_rows = 2 * LAT_ROWS
    latitude = (np.arange(pixel_rows) + 0.5) * (np.pi / pixel_rows) - 0.5 * np.pi
    cosine = np.cos(latitude)
    cosine = cosine / np.mean(cosine)
    by_row = cosine.reshape(LAT_ROWS, 2).repeat(LON_COLS, 0)
    return by_row.astype(np.float32), float(by_row.sum() * (PIX // 2))


def average(old_state, new_state):
    return ema_beta * old_state + (1.0 - ema_beta) * new_state


def column_blocks(part):
    rows, cols = part.shape
    return part.reshape(rows, cols // D, D).transpose(1, 0, 2).reshape(-1, D)


def pack_layer(parts):
    qkv, out, fc1, fc2 = [part.astype(bf16) for part in parts]
    return jnp.concatenate([column_blocks(qkv), out, column_blocks(fc1), fc2], 0)


def unpack_layer(full, rows):
    above = full[:, : rows * 8].reshape(-1, 8, rows, D).transpose(1, 0, 2, 3).reshape(8 * D, D)
    return jnp.concatenate([above, full[:, rows * 8 :].reshape(FF, D)], 0)


def per_device(
    fields, targets, level_count, step_count,
    dense, dense_m, dense_v, dense_ema, vectors, vectors_m, vectors_v, vectors_ema,
    w_qkv, w_out, w_fc1, w_fc2, ema_qkv, ema_out, ema_fc1, ema_fc2,
    stat_small, stat_qkv, stat_wide, root_small, root_qkv, root_wide,
):
    section = lax.axis_index("section")
    sections = lax.axis_size("section")
    dp_index = lax.axis_index("dp")
    parts = lax.axis_size("dp")
    direct = sections == 4 and parts == 8
    rows_dense = dense.shape[0]
    width = D // parts
    both_rows = jnp.concatenate([dense, vectors], 0).astype(bf16)
    packed = [pack_layer([part[layer] for part in (w_qkv, w_out, w_fc1, w_fc2)]) for layer in range(LAYERS)]
    layer_weights = []
    if direct:
        slots = -(-both_rows.shape[0] // LANES) * LANES
        turned = jnp.pad(both_rows, ((0, slots - both_rows.shape[0]), (0, 0))).T
        first = turned.size // D
        before = open_exchange(jnp.concatenate([turned.reshape(first, D), packed[0]], 0))
        full_dense = before[:, :first].reshape(D, slots).T
        layer_weights.append(before)
        packed = packed[1:]
    else:
        full_dense = lax.all_gather(both_rows, "dp", axis=1, tiled=True)
        before = full_dense
    for part in packed:
        part, before = gate(part, before)
        if not layer_weights:
            full_dense = before
        elif not direct:
            layer_weights[-1] = before
        before = lax.all_gather(part, "dp", axis=0)
        layer_weights.append(before)
    near, layer_weights[-1] = gate(root_small, layer_weights[-1])
    around = lax.all_gather(near, "dp", axis=2, tiled=True)
    if direct:
        layer_weights = list(zip(layer_weights, [first] + [0] * (LAYERS - 1)))
    else:
        layer_weights = [unpack_layer(full, w_qkv.shape[1]) for full in layer_weights]
    gain_rows = full_dense[rows_dense : rows_dense + vectors.shape[0]].astype(f32)
    micro_count = fields.shape[0]
    table = full_dense[:TABLE].reshape(VARS, PIX + 1, D).transpose(1, 0, 2)
    table = jnp.pad(table, ((0, 0), (0, LANES - VARS), (0, 0))).reshape(EXT, D)
    position = full_dense[TABLE : TABLE + SEQ]
    proj = full_dense[TABLE + SEQ : TABLE + SEQ + D]
    head_rows = full_dense[TABLE + SEQ + D : rows_dense]
    flags = valid_flags(level_count)
    by_row, row_total = cosine_table()
    weight_local = jnp.sum(flags) * row_total
    cosines = jnp.asarray(by_row)

    core = [("dp", 1, 2)]
    cross = [("section", bit, radix) for bit, radix in digits(sections)]
    along = [("dp", bit, radix) for bit, radix in digits(parts, 2)]
    turns = -(-micro_count // sections)
    turned, error_sum, d_mats = 0.0, 0.0, [0.0] * (2 * LAYERS)
    pending, ready = [], []
    for turn in range(turns):
        index = turn * sections + section
        active = jnp.where(index < micro_count, 1.0, 0.0).astype(f32)
        index = jnp.minimum(index, micro_count - 1)
        field_rows = lax.dynamic_index_in_dim(fields, index, 0, False)
        target = lax.dynamic_index_in_dim(targets, index, 0, False)
        flag_row = lax.dynamic_index_in_dim(flags, index, 0, True)
        valid_vars = jnp.pad(flag_row, ((0, 0), (0, LANES - VARS)), constant_values=-1.0)
        valid_values = jnp.repeat(flag_row * active, PIX, axis=1)
        x, agg = embed_forward(field_rows, table, gain_rows[0:1], valid_vars, proj, position)
        kept = []
        for layer in range(LAYERS):
            gains = gain_rows[1 + 2 * layer : 3 + 2 * layer]
            if direct:
                layer_weights[layer], *saved, y = block_forward(x, gains, *layer_weights[layer])
            else:
                *saved, y = block_forward(x, gains, layer_weights[layer])
            kept.append((x, saved))
            x = y
        grad, d_head, d_final, errors = head_step(
            x, gain_rows[2 * LAYERS + 1 :], head_rows, target, cosines, valid_values
        )
        d_gains = [None] * (2 * LAYERS)
        for layer in reversed(range(LAYERS)):
            gains = gain_rows[1 + 2 * layer : 3 + 2 * layer]
            x, (h, qkv, o, lse, m, h2) = kept[layer]
            pending, ready = pending + ready, []
            grad, pending = advance(grad, pending)
            dm, do, d_gains[2 * layer + 1], found = feed_back(h2, m, grad, gains, layer_weights[layer])
            d_mats[2 * layer + 1] = d_mats[2 * layer + 1] + found if turn else found
            if turn == turns - 1:
                ready = [[d_mats[2 * layer + 1], core + cross]]
            do, pending = advance(do, pending, range(0, len(pending), 2))
            pending, ready = pending + ready, []
            grad, d_gains[2 * layer], found = mix_back(
                x, (h, qkv, o, lse), dm, do, gains, layer_weights[layer]
            )
            d_mats[2 * layer] = d_mats[2 * layer] + found if turn else found
            if turn == turns - 1:
                ready = [[d_mats[2 * layer], core + cross]]
        grad, pending = advance(grad, pending)
        pending, ready = pending + ready, []
        d_vectors = jnp.concatenate(
            [jnp.zeros((1, D), f32), *d_gains, d_final, jnp.zeros((6 - 2 * LAYERS, D), f32)], 0
        )
        found = embed_back(
            field_rows, table, gain_rows[0:1], valid_vars, proj, agg, grad, d_head, d_vectors
        )
        turned = turned + found if turn else found
        error_sum = error_sum + jnp.sum(errors)

    turned, pending = advance(turned, pending)
    width = D // parts
    scalars = jnp.stack([jnp.zeros((), f32), error_sum, jnp.where(section == 0, weight_local, 0.0)])
    scalars = jnp.broadcast_to(jnp.pad(scalars, (0, LANES - 3))[None], (8, LANES))
    if direct:
        feed1, mix1, feed0, mix0 = [part for part, unused in pending]
        pieces, dense_pieces, scalars = close_exchange(
            feed1, mix1, feed0, mix0, turned.reshape(parts // 2, 2, width, SLOTS), scalars
        )
        scalars = jnp.sum(scalars, (0, 1, 2))
        runs, places = parts // 2, [0, 0, 0]
    else:
        own_mats = []
        for part, stages in pending:
            for stage in stages + along:
                part = share_out(part, 0, *stage)
            own_mats.append(part)
        own_dense = turned
        for axis, bit, radix in core:
            own_dense = share_out(own_dense.reshape(-1, radix, width, SLOTS), 1, axis, bit, radix)
        for axis, bit, radix in cross:
            own_dense = share_out(own_dense, 3, axis, bit, radix)
        for axis, bit, radix in along:
            own_dense = share_out(own_dense.reshape(-1, radix, width, own_dense.shape[3]), 1, axis, bit, radix)
        own_dense = own_dense.reshape(width, -1)

        square_own = sum(jnp.sum(part * part) for part in [own_dense] + own_mats)
        scalars = jnp.where(jnp.arange(LANES) == 0, square_own, scalars)
        scalars = total_of(scalars, core + cross + along)

        pieces = []
        for tall_part, wide_part in zip(own_mats[1::2], own_mats[::2]):
            if len(along) == 1 and wide_part.shape[0] % 16 == 0 and tall_part.shape[0] % 16 == 0:
                runs = along[0][2]
                part = jnp.concatenate(collect(jnp.concatenate([wide_part, tall_part], 0), *along[0]), 0)
            else:
                runs = 1
                for stage in reversed(along):
                    turn_at = digit(*stage)
                    wide_part = jnp.concatenate(in_order(collect(wide_part, *stage), turn_at), 0)
                    tall_part = jnp.concatenate(in_order(collect(tall_part, *stage), turn_at), 0)
                part = jnp.concatenate([wide_part, tall_part], 0)
            found = [part]
            for stage in (cross + core if len(cross) == 1 else cross[::-1] + core):
                rounds = [collect(part, *stage) for part in found]
                found = [rounds[j][k] for k in range(stage[2]) for j in range(len(rounds))]
            pieces.insert(0, found)
        fill = -width % 8
        dense_pieces = [jnp.pad(own_dense, ((0, fill), (0, 0)))]
        for stage in cross[::-1]:
            rounds = [collect(part, *stage) for part in dense_pieces]
            dense_pieces = [rounds[j][k] for k in range(stage[2]) for j in range(len(rounds))]
        dense_pieces = jnp.stack(dense_pieces)
        pieces = jnp.stack([jnp.stack(found) for found in pieces])
        places = [(dp_index % 2) * sections + section, dp_index // 2 if runs > 1 else 0, section]

    square_total, error_total, weight_total = scalars[0, 0], scalars[0, 1], scalars[0, 2]
    grad_norm = jnp.sqrt(square_total) / weight_total
    factor = jnp.minimum(1.0, clip_level / grad_norm) / weight_total
    steps_done = step_count[0].astype(f32)
    corrections = [1.0 - jnp.power(beta, steps_done) for beta in (beta_first, beta_second)]
    index = jnp.stack([jnp.asarray(k, jnp.int32) for k in (dp_index, *places)])
    (
        dense_new, dense_m_new, dense_v_new, dense_ema_new,
        vectors_new, vectors_m_new, vectors_v_new, vectors_ema_new,
    ) = adam(
        index, jnp.stack([factor, *corrections]), dense_pieces,
        (dense, dense_m, dense_v, dense_ema), (vectors, vectors_m, vectors_v, vectors_ema),
    )

    (
        stat_small_new, stat_qkv_new, stat_wide_new, out_new, fc2_new, ema_out_new, ema_fc2_new, step,
    ) = shampoo(
        pieces, runs, index, factor.reshape(1), (stat_small, stat_qkv, stat_wide), around,
        (root_small, root_qkv, root_wide), (w_out, w_fc2), (ema_out, ema_fc2),
    )
    if direct:
        arrived = turn_exchange(step)
    else:
        step = step.reshape(LAYERS, parts, width, -1)
        sent = [
            lax.dynamic_index_in_dim(step, jnp.bitwise_xor(dp_index, k), 1, False) for k in range(parts)
        ]
        arrived = jnp.stack([swap(part, "dp", k) if k else part for k, part in enumerate(sent)], 1)
        arrived = jnp.take(arrived, jnp.bitwise_xor(jnp.arange(parts), dp_index), axis=1)
    qkv_new, fc1_new, ema_qkv_new, ema_fc1_new = finish(
        parts, factor.reshape(1), arrived, (w_qkv, w_fc1), (ema_qkv, ema_fc1)
    )
    return (
        error_total / weight_total,
        grad_norm,
        dense_new,
        dense_m_new,
        dense_v_new,
        dense_ema_new,
        vectors_new,
        vectors_m_new,
        vectors_v_new,
        vectors_ema_new,
        qkv_new,
        out_new,
        fc1_new,
        fc2_new,
        ema_qkv_new,
        ema_out_new,
        ema_fc1_new,
        ema_fc2_new,
        stat_small_new,
        stat_qkv_new,
        stat_wide_new,
    )


def solution(mesh):
    items = P("dp", None, None)
    columns = P(None, "dp")
    matrix = P(None, "dp", None)
    stacked = P(None, None, "dp", None)
    return jax.shard_map(
        per_device,
        mesh=mesh,
        in_specs=(
            (items, items, P("dp"), P())
            + (columns,) * 8
            + (matrix,) * 8
            + (stacked, matrix, stacked) * 2
        ),
        out_specs=(P(), P()) + (columns,) * 8 + (matrix,) * 8 + (stacked, matrix, stacked),
        check_vma=False,
    )
```
